256 devices in a mesh: shot: 128 (over x, y, z), freq: 2 (over core).
Axes of the slice: x: 4, y: 4, z: 8, core: 2. Of those that a mesh axis runs over, the one named last changes fastest.
Arguments:
- traces: bfloat16 [256, 1024, 1024], P('shot', None, 'freq'), may hold values from -6 to 6
- frequency_bins: int32 [8], replicated, may hold values from 1 to 511
- aperture: int32 [256, 1024, 32], P(None, 'shot'), may hold values from 0 to 255, as said below
- lengths: int32 [256, 1024], P(None, 'shot'), may hold values from 1 to 32, as said below
- filters: bfloat16 [256, 31], P('shot'), may hold values from -1 to 1
Outputs:
- multiples: bfloat16 [256, 1024, 1024], P('shot', None, 'freq')
The draws below stay inside these ranges and needn't reach their ends.
Inputs may be any that keep to these rules, and one draw needn't show every extreme that they name: aperture[s, r, k] names a shot whose source lies at receiver station 4 times that number; only entries with k below lengths[s, r] are used. The lengths of the shots held by one device along `shot` (one index of the `shot` axis) and the receivers of one index of shot sum to at most 264; in every draw the shots of some index reach 264 with the receivers of every index.
All inputs are finite; a program needn't handle non-finite values.
Results may differ from the reference program's by a relative error of at most 0.015.
Values may be sent and summed in bfloat16 or wider, within the bound.
A program may use at most 192 MiB of HBM per device.

```python
import math
import jax
import jax.numpy as jnp
from jax import lax

R = 1024
NT = 1024
NF = 8
KMAX = 32
TAPS = 31
SHOT_DEV = 2
SHOTS = 256
STRIDE = 4
HALF = 15
N_SHOT = 128


def draw_aperture(key, part):
    shot_ids = jnp.arange(SHOTS, dtype=jnp.int32)[:, None, None]
    receiver_ids = jnp.arange(R, dtype=jnp.int32)[None, :, None]
    middle = (shot_ids + receiver_ids // STRIDE) // 2
    offsets = jax.random.randint(key, (SHOTS, R, KMAX), -KMAX, KMAX + 1)
    return ((middle + offsets) % SHOTS).astype(jnp.int32)


def draw_lengths(key, part):
    groups = N_SHOT
    receiver_dev = R // N_SHOT
    block_size = SHOT_DEV * receiver_dev
    half_block = block_size // 2
    key_total, key_split, key_row, key_column = jax.random.split(key, 4)
    totals = jax.random.randint(key_total, (groups, groups), KMAX // 4 + 2, KMAX + 2)
    full_row = jax.random.randint(key_row, (), 0, groups)
    full_column = jax.random.randint(key_column, (), 0, groups)
    rows_index = jnp.arange(groups, dtype=jnp.int32)[:, None]
    totals = jnp.where(rows_index == full_row, KMAX + 1, totals)
    raw_bits = jax.random.randint(key_split, (groups, groups, half_block), 0, 1 << 20)
    first_part = raw_bits % (totals[:, :, None] - 1) + 1
    corner = (rows_index[:, :, None] == full_row) & (jnp.arange(groups, dtype=jnp.int32)[None, :, None] == full_column) & (jnp.arange(half_block, dtype=jnp.int32)[None, None, :] == 0)
    first_part = jnp.where(corner, 1, first_part)
    second_part = totals[:, :, None] - first_part
    blocks = jnp.concatenate([first_part, second_part], axis=2)
    blocks = blocks.reshape(groups, groups, SHOT_DEV, receiver_dev).transpose(0, 2, 1, 3)
    return blocks.reshape(SHOT_DEV * groups, R).astype(jnp.int32)


def touch_ends(drawn, own_key, least, high):
    longest = drawn.shape.index(max(drawn.shape))
    spots = []
    for shift in (0, 1):
        where = [jax.random.randint(jax.random.fold_in(own_key, axis), (), 0, length) for axis, length in enumerate(drawn.shape)]
        where[longest] = (where[longest] + shift) % drawn.shape[longest]
        spots.append(tuple(where))
    return drawn.at[spots[0]].set(least).at[spots[1]].set(high)


def shard_levels(rng, shape, cuts, least, high):
    level, own = 1.0, jax.random.fold_in(rng, 6)
    for position, blocks in cuts:
        steps = jnp.exp(jax.random.uniform(jax.random.fold_in(own, position), (blocks,), jnp.float32, least / len(cuts), high / len(cuts)))
        level = level * jnp.repeat(steps, shape[position] // blocks).reshape([-1 if axis == position else 1 for axis in range(len(shape))])
    return level


def centred(stream_key, extent, deviation, limit, pieces=(), kind=jnp.bfloat16):
    gain = shard_levels(stream_key, extent, pieces, -0.22, 0.18) if pieces else 1.0
    drawn = jax.random.normal(stream_key, extent, jnp.float32) * deviation * gain
    return jnp.minimum(jnp.maximum(drawn, -limit), limit).astype(kind)


def setup_inputs(seed: int = 0) -> dict:
    arg_keys = jax.random.split(jax.random.key(seed), 6)
    traces = centred(arg_keys[0], (SHOTS, R, NT), 1.0, 6.0, ((0, 128), (2, 2)))
    frequency_bins = touch_ends(jax.random.randint(arg_keys[1], (NF,), 1, NT // 2), jax.random.fold_in(arg_keys[1], 1), 1, (NT // 2) - 1).astype(jnp.int32)
    aperture = draw_aperture(jax.random.fold_in(arg_keys[5], 71), 0)
    lengths = draw_lengths(jax.random.fold_in(arg_keys[5], 71), 0)
    filters = centred(arg_keys[4], (SHOTS, TAPS), TAPS ** -0.5, 1.0, ((0, 128),))
    return dict(traces=traces, frequency_bins=frequency_bins, aperture=aperture, lengths=lengths, filters=filters)


def fourier_rows(bin_rows, first_time, sample_count, period):
    sample_times = first_time + jnp.arange(sample_count, dtype=jnp.int32)
    phases = (bin_rows[:, None] * sample_times[None, :]) % period
    angles = phases.astype(jnp.float32) * (2.0 * math.pi / period)
    return jnp.cos(angles), jnp.sin(angles)


def pair_product(first_leg, second):
    first_leg = first_leg.astype(jnp.float32)
    second = second.astype(jnp.float32)
    real_part = first_leg[:, 0] * second[:, 0] - first_leg[:, 1] * second[:, 1]
    imag_part = first_leg[:, 0] * second[:, 1] + first_leg[:, 1] * second[:, 0]
    return jnp.stack([real_part, imag_part], axis=1)


def reference(traces, frequency_bins, aperture, lengths, filters):
    cosines, sines = fourier_rows(frequency_bins, 0, NT, NT)
    basis_rows = (jnp.stack([cosines, -sines], axis=1) * (NT ** -0.5)).astype(jnp.bfloat16).reshape(NF * 2, NT)
    spectra = lax.dot_general(basis_rows, traces.reshape(SHOTS * R, NT), (((1,), (1,)), ((), ())), preferred_element_type=jnp.float32)
    spectra = spectra.astype(jnp.bfloat16).reshape(NF, 2, SHOTS, R)
    synthesis_rows = jnp.stack([cosines, -sines], axis=1).astype(jnp.bfloat16).reshape(NF * 2, NT)
    every_receiver = jnp.arange(R, dtype=jnp.int32)[:, None]
    list_slots = jnp.arange(KMAX, dtype=jnp.int32)[None, :]

    def one_shot(inputs):
        shot_index, shot_list, shot_lengths, shot_filter = inputs
        shot_spectra = spectra[:, :, shot_index, :]
        first_leg = shot_spectra[:, :, shot_list * STRIDE]
        second = spectra[:, :, shot_list, every_receiver]
        product_terms = pair_product(first_leg, second)
        keep_mask = (list_slots < shot_lengths[:, None])[None, None]
        summed = jnp.where(keep_mask, product_terms, 0.0).sum(axis=-1)
        spectra_out = (summed * (KMAX ** -0.5)).astype(jnp.bfloat16).reshape(NF * 2, R)
        predicted = lax.dot_general(spectra_out, synthesis_rows, (((0,), (0,)), ((), ())), preferred_element_type=jnp.float32).astype(jnp.bfloat16)
        padded = jnp.pad(predicted.astype(jnp.float32), ((0, 0), (HALF, HALF)))
        running = jnp.zeros((R, NT), jnp.float32)
        for tap in range(TAPS):
            running = running + shot_filter[tap].astype(jnp.float32) * padded[:, 2 * HALF - tap: 2 * HALF - tap + NT]
        return running.astype(jnp.bfloat16)

    return lax.map(one_shot, (jnp.arange(SHOTS, dtype=jnp.int32), aperture, lengths, filters))
```

```python
import math

import jax
import jax.numpy as jnp
from jax import lax
from jax.sharding import PartitionSpec as P

NT = 1024
NF = 8
KMAX = 32
TAPS = 31


def extended(shard, sides, width):
    for axis, dim in sides:
        devices, length = (lax.axis_size(axis), shard.shape[dim])
        up = [(i, (i + 1) % devices) for i in range(devices - 1)]
        down = [(j, i) for i, j in up]
        last = lax.slice_in_dim(shard, length - width, length, axis=dim)
        leading = lax.slice_in_dim(shard, 0, width, axis=dim)
        before = lax.ppermute(last, axis, up)
        after = lax.ppermute(leading, axis, down)
        shard = jnp.concatenate([before, shard, after], axis=dim)
    return shard


def fourier_rows(bin_rows, first_time, sample_count, period):
    sample_times = first_time + jnp.arange(sample_count, dtype=jnp.int32)
    phases = bin_rows[:, None] * sample_times[None, :] % period
    angles = phases.astype(jnp.float32) * (2.0 * math.pi / period)
    return (jnp.cos(angles), jnp.sin(angles))


def shards(traces, frequency_bins, aperture, lengths, filters):
    shot_dev, receivers, time_dev = traces.shape
    groups = lax.axis_size("shot")
    shots = shot_dev * groups
    receiver_dev = receivers // groups
    stride = receivers // shots
    freq_dev = lax.axis_size("freq")
    local_bins = NF // freq_dev
    start_time = lax.axis_index("freq") * time_dev
    half_taps = (TAPS - 1) // 2
    flat_traces = traces.reshape(shot_dev * receivers, time_dev)
    cosines, sines = fourier_rows(frequency_bins, start_time, time_dev, NT)
    basis_rows = (jnp.stack([cosines, -sines], axis=1) * NT ** (-0.5)).astype(jnp.bfloat16)
    basis_rows = basis_rows.reshape(NF * 2, time_dev)
    term = lax.dot_general(
        basis_rows, flat_traces, (((1,), (1,)), ((), ())), preferred_element_type=jnp.float32
    )
    spectra = lax.psum_scatter(
        term.reshape(NF, 2, shot_dev, receivers), "freq", scatter_dimension=0, tiled=True
    ).astype(jnp.bfloat16)
    rows = local_bins * 2 * shot_dev
    near = spectra.reshape(rows, groups, receiver_dev).transpose(1, 0, 2).reshape(groups, rows * receiver_dev)
    stations = spectra[:, :, :, ::stride].reshape(1, rows * shots)
    outgoing = jnp.concatenate([near, jnp.broadcast_to(stations, (groups, rows * shots))], axis=1)
    incoming = lax.all_to_all(outgoing, "shot", 0, 0, tiled=True)
    q_part = incoming[:, : rows * receiver_dev].reshape(groups, local_bins, 2, shot_dev, receiver_dev)
    q_part = q_part.transpose(1, 2, 0, 3, 4).reshape(local_bins, 2, shots, receiver_dev).astype(jnp.float32)
    p_part = incoming[:, rows * receiver_dev :].reshape(groups, local_bins, 2, shot_dev, shots)
    p_part = p_part.transpose(1, 2, 0, 3, 4).reshape(local_bins, 2, shots, shots).astype(jnp.float32)
    used = jnp.arange(KMAX, dtype=jnp.int32)[None, None, :] < lengths[:, :, None]
    codes = jnp.where(used, aperture, -1)
    counts = jnp.sum(
        (codes[:, :, :, None] == jnp.arange(shots, dtype=jnp.int32)[None, None, None, :]).astype(jnp.float32),
        axis=2,
    )
    pr, pi = p_part[:, 0][:, :, None, :], p_part[:, 1][:, :, None, :]
    qr = q_part[:, 0].transpose(0, 2, 1)[:, None, :, :]
    qi = q_part[:, 1].transpose(0, 2, 1)[:, None, :, :]
    weight = counts[None]
    real_part = jnp.sum(weight * (pr * qr - pi * qi), axis=-1)
    imag_part = jnp.sum(weight * (pr * qi + pi * qr), axis=-1)
    summed = jnp.stack([real_part, imag_part], axis=1)
    multiples_spectra = (summed * KMAX ** (-0.5)).astype(jnp.bfloat16)
    back = multiples_spectra.reshape(local_bins, 2, groups, shot_dev, receiver_dev).transpose(2, 0, 1, 3, 4)
    back = lax.all_to_all(back.reshape(groups, rows * receiver_dev), "shot", 0, 0, tiled=True)
    piece = back.reshape(groups, local_bins, 2, shot_dev, receiver_dev).transpose(1, 2, 3, 0, 4)
    piece = piece.reshape(local_bins, 2, shot_dev, receivers)
    piece = lax.all_gather(piece, "freq", axis=0, tiled=True)
    synthesis_rows = jnp.stack([cosines, -sines], axis=1).astype(jnp.bfloat16).reshape(NF * 2, time_dev)
    flat_piece = piece.reshape(NF * 2, shot_dev * receivers)
    synthesized = lax.dot_general(
        flat_piece, synthesis_rows, (((0,), (0,)), ((), ())), preferred_element_type=jnp.float32
    )
    predicted = synthesized.astype(jnp.bfloat16).reshape(shot_dev, receivers, time_dev)
    padded = extended(predicted, (("freq", 2),), half_taps)
    padded_width = time_dev + 2 * half_taps
    lag_table = (
        jnp.arange(time_dev, dtype=jnp.int32)[None, :]
        + 2 * half_taps
        - jnp.arange(padded_width, dtype=jnp.int32)[:, None]
    )
    tap_onehot = (lag_table[None] == jnp.arange(TAPS, dtype=jnp.int32)[:, None, None]).astype(
        jnp.bfloat16
    )
    toeplitz = jnp.einsum(
        "sj,jut->sut", filters, tap_onehot, preferred_element_type=jnp.float32
    ).astype(jnp.bfloat16)
    filtered = jnp.einsum("sru,sut->srt", padded, toeplitz, preferred_element_type=jnp.float32)
    return filtered.astype(jnp.bfloat16)


def solution(mesh):
    in_specs = (
        P("shot", None, "freq"),
        P(),
        P(None, "shot", None),
        P(None, "shot"),
        P("shot", None),
    )
    out_specs = P("shot", None, "freq")
    return jax.shard_map(shards, mesh=mesh, in_specs=in_specs, out_specs=out_specs, check_vma=False)
```

```python
import math

import jax
import jax.numpy as jnp
from jax import lax
from jax.sharding import PartitionSpec as P

NT = 1024
NF = 8
KMAX = 32
TAPS = 31


def extended(shard, sides, width):
    for axis, dim in sides:
        devices, length = (lax.axis_size(axis), shard.shape[dim])
        up = [(i, (i + 1) % devices) for i in range(devices - 1)]
        down = [(j, i) for i, j in up]
        last = lax.slice_in_dim(shard, length - width, length, axis=dim)
        leading = lax.slice_in_dim(shard, 0, width, axis=dim)
        before = lax.ppermute(last, axis, up)
        after = lax.ppermute(leading, axis, down)
        shard = jnp.concatenate([before, shard, after], axis=dim)
    return shard


def fourier_rows(bin_rows, first_time, sample_count, period):
    sample_times = first_time + jnp.arange(sample_count, dtype=jnp.int32)
    phases = bin_rows[:, None] * sample_times[None, :] % period
    angles = phases.astype(jnp.float32) * (2.0 * math.pi / period)
    return (jnp.cos(angles), jnp.sin(angles))


def shards(traces, frequency_bins, aperture, lengths, filters):
    shot_dev, receivers, time_dev = traces.shape
    groups = lax.axis_size("shot")
    shots = shot_dev * groups
    receiver_dev = receivers // groups
    stride = receivers // shots
    freq_dev = lax.axis_size("freq")
    local_bins = NF // freq_dev
    start_time = lax.axis_index("freq") * time_dev
    half_taps = (TAPS - 1) // 2
    flat_traces = traces.reshape(shot_dev * receivers, time_dev)
    cosines, sines = fourier_rows(frequency_bins, start_time, time_dev, NT)
    basis_rows = (jnp.stack([cosines, -sines], axis=1) * NT ** (-0.5)).astype(jnp.bfloat16)
    basis_rows = basis_rows.reshape(NF * 2, time_dev)
    term = lax.dot_general(
        basis_rows, flat_traces, (((1,), (1,)), ((), ())), preferred_element_type=jnp.float32
    )
    spectra = lax.psum_scatter(
        term.reshape(NF, 2, shot_dev, receivers), "freq", scatter_dimension=0, tiled=True
    ).astype(jnp.bfloat16)
    rows = local_bins * 2 * shot_dev
    near = spectra.reshape(rows, groups, receiver_dev).transpose(1, 0, 2).reshape(groups, rows * receiver_dev)
    stations = spectra[:, :, :, ::stride].reshape(1, rows * shots)
    outgoing = jnp.concatenate([near, jnp.broadcast_to(stations, (groups, rows * shots))], axis=1)
    incoming = lax.all_to_all(outgoing, "shot", 0, 0, tiled=True)
    q_part = incoming[:, : rows * receiver_dev].reshape(groups, local_bins, 2, shot_dev, receiver_dev)
    q_t = q_part.transpose(1, 2, 4, 0, 3).reshape(local_bins, 2, receiver_dev, shots).astype(jnp.float32)
    p_in = incoming[:, rows * receiver_dev :].reshape(groups, local_bins, 2, shot_dev, shots)
    used = jnp.arange(KMAX, dtype=jnp.int32)[None, None, :] < lengths[:, :, None]
    codes = jnp.where(used, aperture, -1)
    counts = jnp.sum(
        (codes[:, :, :, None] == jnp.arange(shots, dtype=jnp.int32)[None, None, None, :]).astype(jnp.float32),
        axis=2,
    )
    weight = counts.reshape(groups, 1, shot_dev, receiver_dev, shots)
    pr = p_in[:, :, 0, :, None, :].astype(jnp.float32)
    pi = p_in[:, :, 1, :, None, :].astype(jnp.float32)
    qr = q_t[None, :, 0, None, :, :]
    qi = q_t[None, :, 1, None, :, :]
    real_part = jnp.sum(weight * (pr * qr - pi * qi), axis=-1)
    imag_part = jnp.sum(weight * (pr * qi + pi * qr), axis=-1)
    summed = jnp.stack([real_part, imag_part], axis=2)
    multiples_spectra = (summed * KMAX ** (-0.5)).astype(jnp.bfloat16)
    back = lax.all_to_all(multiples_spectra.reshape(groups, rows * receiver_dev), "shot", 0, 0, tiled=True)
    piece = lax.all_gather(back, "freq", axis=0, tiled=False)
    piece = piece.reshape(freq_dev, groups, local_bins, 2, shot_dev, receiver_dev)
    piece = piece.transpose(4, 1, 5, 0, 2, 3).reshape(shot_dev, receivers, NF * 2)
    wide = time_dev + 2 * half_taps
    wide_times = start_time - half_taps + jnp.arange(wide, dtype=jnp.int32)
    inside = (wide_times >= 0) & (wide_times < NT)
    phases = frequency_bins[:, None] * jnp.clip(wide_times, 0, NT - 1)[None, :] % NT
    angles = phases.astype(jnp.float32) * (2.0 * math.pi / NT)
    wide_rows = jnp.stack([jnp.cos(angles), -jnp.sin(angles)], axis=1).astype(jnp.bfloat16)
    wide_rows = jnp.where(inside[None, None, :], wide_rows.astype(jnp.float32), 0.0).reshape(NF * 2, wide)
    taps = filters.astype(jnp.float32)
    shaped = sum(
        taps[:, tap, None, None] * wide_rows[None, :, 2 * half_taps - tap : 2 * half_taps - tap + time_dev]
        for tap in range(TAPS)
    )
    filtered = lax.dot_general(
        piece.astype(jnp.float32),
        shaped,
        (((2,), (1,)), ((0,), (0,))),
        precision=lax.Precision.HIGHEST,
        preferred_element_type=jnp.float32,
    )
    return filtered.astype(jnp.bfloat16)


def solution(mesh):
    in_specs = (
        P("shot", None, "freq"),
        P(),
        P(None, "shot", None),
        P(None, "shot"),
        P("shot", None),
    )
    out_specs = P("shot", None, "freq")
    return jax.shard_map(shards, mesh=mesh, in_specs=in_specs, out_specs=out_specs, check_vma=False)
```

```python
import functools
import math

import jax
import jax.numpy as jnp
from jax import lax
from jax.experimental import pallas as pl
from jax.experimental.pallas import tpu as pltpu
from jax.sharding import PartitionSpec as P

NT = 1024
NF = 8
KMAX = 32
TAPS = 31


def extended(shard, sides, width):
    for axis, dim in sides:
        devices, length = (lax.axis_size(axis), shard.shape[dim])
        up = [(i, (i + 1) % devices) for i in range(devices - 1)]
        down = [(j, i) for i, j in up]
        last = lax.slice_in_dim(shard, length - width, length, axis=dim)
        leading = lax.slice_in_dim(shard, 0, width, axis=dim)
        before = lax.ppermute(last, axis, up)
        after = lax.ppermute(leading, axis, down)
        shard = jnp.concatenate([before, shard, after], axis=dim)
    return shard


def fourier_rows(bin_rows, first_time, sample_count, period):
    sample_times = first_time + jnp.arange(sample_count, dtype=jnp.int32)
    phases = bin_rows[:, None] * sample_times[None, :] % period
    angles = phases.astype(jnp.float32) * (2.0 * math.pi / period)
    return (jnp.cos(angles), jnp.sin(angles))


def multiply_kernel(incoming_ref, counts_ref, out_ref, acc_ref, *, local_bins, shot_dev, receiver_dev, groups):
    near = local_bins * 2 * shot_dev * receiver_dev
    q_t = incoming_ref[:, 0:near].astype(jnp.float32).T
    width = shot_dev * groups

    def q_row(f, c, i, r):
        row = ((f * 2 + c) * shot_dev + i) * receiver_dev + r
        return q_t[row : row + 1, :]

    for i in range(shot_dev):
        for r in range(receiver_dev):
            weights = [counts_ref[i, r, :, h * groups : (h + 1) * groups] for h in range(shot_dev)]
            for f in range(local_bins):
                real_sum = None
                imag_sum = None
                for h in range(shot_dev):
                    base_r = near + ((f * 2 + 0) * shot_dev + i) * width + h * groups
                    base_i = near + ((f * 2 + 1) * shot_dev + i) * width + h * groups
                    pr = incoming_ref[:, base_r : base_r + groups].astype(jnp.float32)
                    pi = incoming_ref[:, base_i : base_i + groups].astype(jnp.float32)
                    qr = q_row(f, 0, h, r)
                    qi = q_row(f, 1, h, r)
                    w = weights[h]
                    real_term = w * (pr * qr - pi * qi)
                    imag_term = w * (pr * qi + pi * qr)
                    real_sum = real_term if real_sum is None else real_sum + real_term
                    imag_sum = imag_term if imag_sum is None else imag_sum + imag_term
                col_r = ((f * 2 + 0) * shot_dev + i) * receiver_dev + r
                col_i = ((f * 2 + 1) * shot_dev + i) * receiver_dev + r
                acc_ref[:, col_r : col_r + 1] = jnp.sum(real_sum, axis=1, keepdims=True)
                acc_ref[:, col_i : col_i + 1] = jnp.sum(imag_sum, axis=1, keepdims=True)
    out_ref[...] = (acc_ref[...] * KMAX ** (-0.5)).astype(out_ref.dtype)


def shards(traces, frequency_bins, aperture, lengths, filters):
    shot_dev, receivers, time_dev = traces.shape
    groups = lax.axis_size("shot")
    shots = shot_dev * groups
    receiver_dev = receivers // groups
    stride = receivers // shots
    freq_dev = lax.axis_size("freq")
    local_bins = NF // freq_dev
    start_time = lax.axis_index("freq") * time_dev
    half_taps = (TAPS - 1) // 2
    flat_traces = traces.reshape(shot_dev * receivers, time_dev)
    cosines, sines = fourier_rows(frequency_bins, start_time, time_dev, NT)
    basis_rows = (jnp.stack([cosines, -sines], axis=1) * NT ** (-0.5)).astype(jnp.bfloat16)
    basis_rows = basis_rows.reshape(NF * 2, time_dev)
    term = lax.dot_general(
        basis_rows, flat_traces, (((1,), (1,)), ((), ())), preferred_element_type=jnp.float32
    )
    spectra = lax.psum_scatter(
        term.reshape(NF, 2, shot_dev, receivers), "freq", scatter_dimension=0, tiled=True
    ).astype(jnp.bfloat16)
    rows = local_bins * 2 * shot_dev
    near = spectra.reshape(rows, groups, receiver_dev).transpose(1, 0, 2).reshape(groups, rows * receiver_dev)
    stations = jnp.concatenate(
        [spectra[:, :, :, 0 :: 2 * stride], spectra[:, :, :, stride :: 2 * stride]], axis=-1
    ).reshape(1, rows * shots)
    outgoing = jnp.concatenate([near, jnp.broadcast_to(stations, (groups, rows * shots))], axis=1)
    incoming = lax.all_to_all(outgoing, "shot", 0, 0, tiled=True)
    used = jnp.arange(KMAX, dtype=jnp.int32)[None, None, :] < lengths[:, :, None]
    codes = jnp.where(used, (aperture % shot_dev) * groups + aperture // shot_dev, -1)
    codes = codes.reshape(groups, shot_dev, receiver_dev, KMAX).transpose(1, 2, 0, 3)
    counts = jnp.sum(
        (codes[..., None] == jnp.arange(shots, dtype=jnp.int32)).astype(jnp.float32), axis=3
    )
    kernel = functools.partial(
        multiply_kernel, local_bins=local_bins, shot_dev=shot_dev, receiver_dev=receiver_dev, groups=groups
    )
    multiples_spectra = pl.pallas_call(
        kernel,
        out_shape=jax.ShapeDtypeStruct((groups, rows * receiver_dev), jnp.bfloat16),
        in_specs=[pl.BlockSpec(memory_space=pltpu.VMEM)] * 2,
        out_specs=pl.BlockSpec(memory_space=pltpu.VMEM),
        scratch_shapes=[pltpu.VMEM((groups, rows * receiver_dev), jnp.float32)],
        cost_estimate=pl.CostEstimate(
            flops=16 * groups * shots * rows * receiver_dev // 2, transcendentals=0, bytes_accessed=4 * 1024 * 1024
        ),
    )(incoming, counts)
    back = lax.all_to_all(multiples_spectra.reshape(groups, rows * receiver_dev), "shot", 0, 0, tiled=True)
    piece = lax.all_gather(back, "freq", axis=0, tiled=False)
    piece = piece.reshape(freq_dev, groups, local_bins, 2, shot_dev, receiver_dev)
    piece = piece.transpose(4, 1, 5, 0, 2, 3).reshape(shot_dev, receivers, NF * 2)
    wide = time_dev + 2 * half_taps
    wide_times = start_time - half_taps + jnp.arange(wide, dtype=jnp.int32)
    inside = (wide_times >= 0) & (wide_times < NT)
    phases = frequency_bins[:, None] * jnp.clip(wide_times, 0, NT - 1)[None, :] % NT
    angles = phases.astype(jnp.float32) * (2.0 * math.pi / NT)
    wide_rows = jnp.stack([jnp.cos(angles), -jnp.sin(angles)], axis=1).astype(jnp.bfloat16)
    wide_rows = jnp.where(inside[None, None, :], wide_rows.astype(jnp.float32), 0.0).reshape(NF * 2, wide)
    taps = filters.astype(jnp.float32)
    shaped = sum(
        taps[:, tap, None, None] * wide_rows[None, :, 2 * half_taps - tap : 2 * half_taps - tap + time_dev]
        for tap in range(TAPS)
    )
    filtered = lax.dot_general(
        piece.astype(jnp.float32),
        shaped,
        (((2,), (1,)), ((0,), (0,))),
        precision=lax.Precision.HIGHEST,
        preferred_element_type=jnp.float32,
    )
    return filtered.astype(jnp.bfloat16)


def solution(mesh):
    in_specs = (
        P("shot", None, "freq"),
        P(),
        P(None, "shot", None),
        P(None, "shot"),
        P("shot", None),
    )
    out_specs = P("shot", None, "freq")
    return jax.shard_map(shards, mesh=mesh, in_specs=in_specs, out_specs=out_specs, check_vma=False)
```

```python
import functools
import math

import jax
import jax.numpy as jnp
from jax import lax
from jax.experimental import pallas as pl
from jax.experimental.pallas import tpu as pltpu
from jax.sharding import PartitionSpec as P

NT = 1024
NF = 8
KMAX = 32
TAPS = 31


def extended(shard, sides, width):
    for axis, dim in sides:
        devices, length = (lax.axis_size(axis), shard.shape[dim])
        up = [(i, (i + 1) % devices) for i in range(devices - 1)]
        down = [(j, i) for i, j in up]
        last = lax.slice_in_dim(shard, length - width, length, axis=dim)
        leading = lax.slice_in_dim(shard, 0, width, axis=dim)
        before = lax.ppermute(last, axis, up)
        after = lax.ppermute(leading, axis, down)
        shard = jnp.concatenate([before, shard, after], axis=dim)
    return shard


def fourier_rows(bin_rows, first_time, sample_count, period):
    sample_times = first_time + jnp.arange(sample_count, dtype=jnp.int32)
    phases = bin_rows[:, None] * sample_times[None, :] % period
    angles = phases.astype(jnp.float32) * (2.0 * math.pi / period)
    return (jnp.cos(angles), jnp.sin(angles))


def multiply_kernel(incoming_ref, counts_ref, out_ref, acc_ref, recv_ref, sems, *, local_bins, shot_dev, receiver_dev, groups):
    near = local_bins * 2 * shot_dev * receiver_dev
    q_t = incoming_ref[:, 0:near].astype(jnp.float32).T
    width = shot_dev * groups

    def q_row(f, c, i, r):
        row = ((f * 2 + c) * shot_dev + i) * receiver_dev + r
        return q_t[row : row + 1, :]

    for i in range(shot_dev):
        for r in range(receiver_dev):
            weights = [counts_ref[i, r, :, h * groups : (h + 1) * groups] for h in range(shot_dev)]
            for f in range(local_bins):
                real_sum = None
                imag_sum = None
                for h in range(shot_dev):
                    base_r = near + ((f * 2 + 0) * shot_dev + i) * width + h * groups
                    base_i = near + ((f * 2 + 1) * shot_dev + i) * width + h * groups
                    pr = incoming_ref[:, base_r : base_r + groups].astype(jnp.float32)
                    pi = incoming_ref[:, base_i : base_i + groups].astype(jnp.float32)
                    qr = q_row(f, 0, h, r)
                    qi = q_row(f, 1, h, r)
                    w = weights[h]
                    real_term = w * (pr * qr - pi * qi)
                    imag_term = w * (pr * qi + pi * qr)
                    real_sum = real_term if real_sum is None else real_sum + real_term
                    imag_sum = imag_term if imag_sum is None else imag_sum + imag_term
                col_r = ((f * 2 + 0) * shot_dev + i) * receiver_dev + r
                col_i = ((f * 2 + 1) * shot_dev + i) * receiver_dev + r
                acc_ref[:, col_r : col_r + 1] = jnp.sum(real_sum, axis=1, keepdims=True)
                acc_ref[:, col_i : col_i + 1] = jnp.sum(imag_sum, axis=1, keepdims=True)
    acc_ref[...] = (acc_ref[...] * KMAX ** (-0.5)).astype(jnp.bfloat16).astype(jnp.float32)
    me = lax.axis_index("shot")
    half = lax.axis_index("freq")
    recv_ref[pl.ds(me, 1), :] = acc_ref[pl.ds(me, 1), :]

    def send(step, carry):
        target = lax.rem(me + step, groups)
        pltpu.make_async_remote_copy(
            src_ref=acc_ref.at[pl.ds(target, 1)],
            dst_ref=recv_ref.at[pl.ds(me, 1)],
            send_sem=sems.at[0],
            recv_sem=sems.at[1],
            device_id=(target, half),
            device_id_type=pl.DeviceIdType.MESH,
        ).start()
        return carry

    lax.fori_loop(1, groups, send, 0)
    every = pltpu.make_async_remote_copy(
        src_ref=acc_ref.at[pl.ds(0, groups - 1)],
        dst_ref=recv_ref.at[pl.ds(0, groups - 1)],
        send_sem=sems.at[0],
        recv_sem=sems.at[1],
        device_id=(me, half),
        device_id_type=pl.DeviceIdType.MESH,
    )
    every.wait_send()
    every.wait_recv()
    out_ref[...] = recv_ref[...]


def shards(traces, frequency_bins, aperture, lengths, filters):
    shot_dev, receivers, time_dev = traces.shape
    groups = lax.axis_size("shot")
    shots = shot_dev * groups
    receiver_dev = receivers // groups
    stride = receivers // shots
    freq_dev = lax.axis_size("freq")
    local_bins = NF // freq_dev
    start_time = lax.axis_index("freq") * time_dev
    half_taps = (TAPS - 1) // 2
    flat_traces = traces.reshape(shot_dev * receivers, time_dev)
    cosines, sines = fourier_rows(frequency_bins, start_time, time_dev, NT)
    basis_rows = (jnp.stack([cosines, -sines], axis=1) * NT ** (-0.5)).astype(jnp.bfloat16)
    basis_rows = basis_rows.reshape(NF * 2, time_dev)
    term = lax.dot_general(
        basis_rows, flat_traces, (((1,), (1,)), ((), ())), preferred_element_type=jnp.float32
    )
    spectra = lax.psum_scatter(
        term.reshape(NF, 2, shot_dev, receivers), "freq", scatter_dimension=0, tiled=True
    ).astype(jnp.bfloat16)
    rows = local_bins * 2 * shot_dev
    near = spectra.reshape(rows, groups, receiver_dev).transpose(1, 0, 2).reshape(groups, rows * receiver_dev)
    stations = jnp.concatenate(
        [spectra[:, :, :, 0 :: 2 * stride], spectra[:, :, :, stride :: 2 * stride]], axis=-1
    ).reshape(1, rows * shots)
    outgoing = jnp.concatenate([near, jnp.broadcast_to(stations, (groups, rows * shots))], axis=1)
    incoming = lax.all_to_all(outgoing, "shot", 0, 0, tiled=True)
    used = jnp.arange(KMAX, dtype=jnp.int32)[None, None, :] < lengths[:, :, None]
    codes = jnp.where(used, (aperture % shot_dev) * groups + aperture // shot_dev, -1)
    codes = codes.reshape(groups, shot_dev, receiver_dev, KMAX).transpose(1, 2, 0, 3)
    counts = jnp.sum(
        (codes[..., None] == jnp.arange(shots, dtype=jnp.int32)).astype(jnp.float32), axis=3
    )
    kernel = functools.partial(
        multiply_kernel, local_bins=local_bins, shot_dev=shot_dev, receiver_dev=receiver_dev, groups=groups
    )
    back = pl.pallas_call(
        kernel,
        out_shape=jax.ShapeDtypeStruct((groups, rows * receiver_dev), jnp.float32),
        in_specs=[pl.BlockSpec(memory_space=pltpu.VMEM)] * 2,
        out_specs=pl.BlockSpec(memory_space=pltpu.VMEM),
        scratch_shapes=[
            pltpu.VMEM((groups, rows * receiver_dev), jnp.float32),
            pltpu.VMEM((groups, rows * receiver_dev), jnp.float32),
            pltpu.SemaphoreType.DMA((2,)),
        ],
        compiler_params=pltpu.CompilerParams(has_side_effects=True),
        cost_estimate=pl.CostEstimate(
            flops=16 * groups * shots * rows * receiver_dev // 2, transcendentals=0, bytes_accessed=4 * 1024 * 1024
        ),
    )(incoming, counts)
    piece = lax.all_gather(back.astype(jnp.bfloat16), "freq", axis=0, tiled=False)
    piece = piece.reshape(freq_dev, groups, local_bins, 2, shot_dev, receiver_dev)
    piece = piece.transpose(4, 1, 5, 0, 2, 3).reshape(shot_dev, receivers, NF * 2)
    wide = time_dev + 2 * half_taps
    wide_times = start_time - half_taps + jnp.arange(wide, dtype=jnp.int32)
    inside = (wide_times >= 0) & (wide_times < NT)
    phases = frequency_bins[:, None] * jnp.clip(wide_times, 0, NT - 1)[None, :] % NT
    angles = phases.astype(jnp.float32) * (2.0 * math.pi / NT)
    wide_rows = jnp.stack([jnp.cos(angles), -jnp.sin(angles)], axis=1).astype(jnp.bfloat16)
    wide_rows = jnp.where(inside[None, None, :], wide_rows.astype(jnp.float32), 0.0).reshape(NF * 2, wide)
    taps = filters.astype(jnp.float32)
    shaped = sum(
        taps[:, tap, None, None] * wide_rows[None, :, 2 * half_taps - tap : 2 * half_taps - tap + time_dev]
        for tap in range(TAPS)
    )
    filtered = lax.dot_general(
        piece.astype(jnp.float32),
        shaped,
        (((2,), (1,)), ((0,), (0,))),
        precision=lax.Precision.HIGHEST,
        preferred_element_type=jnp.float32,
    )
    return filtered.astype(jnp.bfloat16)


def solution(mesh):
    in_specs = (
        P("shot", None, "freq"),
        P(),
        P(None, "shot", None),
        P(None, "shot"),
        P("shot", None),
    )
    out_specs = P("shot", None, "freq")
    return jax.shard_map(shards, mesh=mesh, in_specs=in_specs, out_specs=out_specs, check_vma=False)
```

```python
import functools
import math

import jax
import jax.numpy as jnp
from jax import lax
from jax.experimental import pallas as pl
from jax.experimental.pallas import tpu as pltpu
from jax.sharding import PartitionSpec as P

NT = 1024
NF = 8
KMAX = 32
TAPS = 31


def extended(shard, sides, width):
    for axis, dim in sides:
        devices, length = (lax.axis_size(axis), shard.shape[dim])
        up = [(i, (i + 1) % devices) for i in range(devices - 1)]
        down = [(j, i) for i, j in up]
        last = lax.slice_in_dim(shard, length - width, length, axis=dim)
        leading = lax.slice_in_dim(shard, 0, width, axis=dim)
        before = lax.ppermute(last, axis, up)
        after = lax.ppermute(leading, axis, down)
        shard = jnp.concatenate([before, shard, after], axis=dim)
    return shard


def fourier_rows(bin_rows, first_time, sample_count, period):
    sample_times = first_time + jnp.arange(sample_count, dtype=jnp.int32)
    phases = bin_rows[:, None] * sample_times[None, :] % period
    angles = phases.astype(jnp.float32) * (2.0 * math.pi / period)
    return (jnp.cos(angles), jnp.sin(angles))


def multiply_kernel(
    incoming_ref, counts_ref, out_ref, qt_ref, acc_ref, recv_ref, sems, *, local_bins, shot_dev, receiver_dev, groups
):
    near = local_bins * 2 * shot_dev * receiver_dev
    width = shot_dev * groups
    qt_ref[...] = incoming_ref[:, 0:near].astype(jnp.float32).T
    me = lax.axis_index("shot")
    half = lax.axis_index("freq")
    block = 16

    def chunk(step, carry):
        top = pl.multiple_of(step * block, block)
        rows = pl.ds(top, block)
        for i in range(shot_dev):
            for r in range(receiver_dev):
                weights = [counts_ref[i, r, rows, h * groups : (h + 1) * groups] for h in range(shot_dev)]
                for f in range(local_bins):
                    real_sum = None
                    imag_sum = None
                    for h in range(shot_dev):
                        base_r = near + ((f * 2 + 0) * shot_dev + i) * width + h * groups
                        base_i = near + ((f * 2 + 1) * shot_dev + i) * width + h * groups
                        pr = incoming_ref[rows, base_r : base_r + groups].astype(jnp.float32)
                        pi = incoming_ref[rows, base_i : base_i + groups].astype(jnp.float32)
                        row_r = ((f * 2 + 0) * shot_dev + h) * receiver_dev + r
                        row_i = ((f * 2 + 1) * shot_dev + h) * receiver_dev + r
                        qr = qt_ref[row_r : row_r + 1, :]
                        qi = qt_ref[row_i : row_i + 1, :]
                        w = weights[h]
                        real_term = w * (pr * qr - pi * qi)
                        imag_term = w * (pr * qi + pi * qr)
                        real_sum = real_term if real_sum is None else real_sum + real_term
                        imag_sum = imag_term if imag_sum is None else imag_sum + imag_term
                    col_r = ((f * 2 + 0) * shot_dev + i) * receiver_dev + r
                    col_i = ((f * 2 + 1) * shot_dev + i) * receiver_dev + r
                    acc_ref[rows, col_r : col_r + 1] = jnp.sum(real_sum, axis=1, keepdims=True)
                    acc_ref[rows, col_i : col_i + 1] = jnp.sum(imag_sum, axis=1, keepdims=True)
        acc_ref[rows, :] = (acc_ref[rows, :] * KMAX ** (-0.5)).astype(jnp.bfloat16).astype(jnp.float32)
        for t in range(block):
            target = top + t

            @pl.when(target != me)
            def _():
                pltpu.make_async_remote_copy(
                    src_ref=acc_ref.at[pl.ds(target, 1)],
                    dst_ref=recv_ref.at[pl.ds(me, 1)],
                    send_sem=sems.at[0],
                    recv_sem=sems.at[1],
                    device_id=(target, half),
                    device_id_type=pl.DeviceIdType.MESH,
                ).start()

            @pl.when(target == me)
            def _():
                recv_ref[pl.ds(me, 1), :] = acc_ref[pl.ds(me, 1), :]

        return carry

    lax.fori_loop(0, groups // block, chunk, 0)
    every = pltpu.make_async_remote_copy(
        src_ref=acc_ref.at[pl.ds(0, groups - 1)],
        dst_ref=recv_ref.at[pl.ds(0, groups - 1)],
        send_sem=sems.at[0],
        recv_sem=sems.at[1],
        device_id=(me, half),
        device_id_type=pl.DeviceIdType.MESH,
    )
    every.wait_send()
    every.wait_recv()
    out_ref[...] = recv_ref[...]


def shards(traces, frequency_bins, aperture, lengths, filters):
    shot_dev, receivers, time_dev = traces.shape
    groups = lax.axis_size("shot")
    shots = shot_dev * groups
    receiver_dev = receivers // groups
    stride = receivers // shots
    freq_dev = lax.axis_size("freq")
    local_bins = NF // freq_dev
    start_time = lax.axis_index("freq") * time_dev
    half_taps = (TAPS - 1) // 2
    flat_traces = traces.reshape(shot_dev * receivers, time_dev)
    cosines, sines = fourier_rows(frequency_bins, start_time, time_dev, NT)
    basis_rows = (jnp.stack([cosines, -sines], axis=1) * NT ** (-0.5)).astype(jnp.bfloat16)
    basis_rows = basis_rows.reshape(NF * 2, time_dev)
    term = lax.dot_general(
        basis_rows, flat_traces, (((1,), (1,)), ((), ())), preferred_element_type=jnp.float32
    )
    spectra = lax.psum_scatter(
        term.reshape(NF, 2, shot_dev, receivers), "freq", scatter_dimension=0, tiled=True
    ).astype(jnp.bfloat16)
    rows = local_bins * 2 * shot_dev
    near = spectra.reshape(rows, groups, receiver_dev).transpose(1, 0, 2).reshape(groups, rows * receiver_dev)
    stations = jnp.concatenate(
        [spectra[:, :, :, 0 :: 2 * stride], spectra[:, :, :, stride :: 2 * stride]], axis=-1
    ).reshape(1, rows * shots)
    outgoing = jnp.concatenate([near, jnp.broadcast_to(stations, (groups, rows * shots))], axis=1)
    incoming = lax.all_to_all(outgoing, "shot", 0, 0, tiled=True)
    used = jnp.arange(KMAX, dtype=jnp.int32)[None, None, :] < lengths[:, :, None]
    codes = jnp.where(used, (aperture % shot_dev) * groups + aperture // shot_dev, -1)
    codes = codes.reshape(groups, shot_dev, receiver_dev, KMAX).transpose(1, 2, 0, 3)
    counts = jnp.sum(
        (codes[..., None] == jnp.arange(shots, dtype=jnp.int32)).astype(jnp.float32), axis=3
    )
    kernel = functools.partial(
        multiply_kernel, local_bins=local_bins, shot_dev=shot_dev, receiver_dev=receiver_dev, groups=groups
    )
    back = pl.pallas_call(
        kernel,
        out_shape=jax.ShapeDtypeStruct((groups, rows * receiver_dev), jnp.float32),
        in_specs=[pl.BlockSpec(memory_space=pltpu.VMEM)] * 2,
        out_specs=pl.BlockSpec(memory_space=pltpu.VMEM),
        scratch_shapes=[
            pltpu.VMEM((rows * receiver_dev, groups), jnp.float32),
            pltpu.VMEM((groups, rows * receiver_dev), jnp.float32),
            pltpu.VMEM((groups, rows * receiver_dev), jnp.float32),
            pltpu.SemaphoreType.DMA((2,)),
        ],
        compiler_params=pltpu.CompilerParams(has_side_effects=True),
        cost_estimate=pl.CostEstimate(
            flops=16 * groups * shots * rows * receiver_dev // 2, transcendentals=0, bytes_accessed=4 * 1024 * 1024
        ),
    )(incoming, counts)
    piece = lax.all_gather(back.astype(jnp.bfloat16), "freq", axis=0, tiled=False)
    piece = piece.reshape(freq_dev, groups, local_bins, 2, shot_dev, receiver_dev)
    piece = piece.transpose(4, 1, 5, 0, 2, 3).reshape(shot_dev, receivers, NF * 2)
    wide = time_dev + 2 * half_taps
    wide_times = start_time - half_taps + jnp.arange(wide, dtype=jnp.int32)
    inside = (wide_times >= 0) & (wide_times < NT)
    phases = frequency_bins[:, None] * jnp.clip(wide_times, 0, NT - 1)[None, :] % NT
    angles = phases.astype(jnp.float32) * (2.0 * math.pi / NT)
    wide_rows = jnp.stack([jnp.cos(angles), -jnp.sin(angles)], axis=1).astype(jnp.bfloat16)
    wide_rows = jnp.where(inside[None, None, :], wide_rows.astype(jnp.float32), 0.0).reshape(NF * 2, wide)
    taps = filters.astype(jnp.float32)
    shaped = sum(
        taps[:, tap, None, None] * wide_rows[None, :, 2 * half_taps - tap : 2 * half_taps - tap + time_dev]
        for tap in range(TAPS)
    )
    filtered = lax.dot_general(
        piece.astype(jnp.float32),
        shaped,
        (((2,), (1,)), ((0,), (0,))),
        precision=lax.Precision.HIGHEST,
        preferred_element_type=jnp.float32,
    )
    return filtered.astype(jnp.bfloat16)


def solution(mesh):
    in_specs = (
        P("shot", None, "freq"),
        P(),
        P(None, "shot", None),
        P(None, "shot"),
        P("shot", None),
    )
    out_specs = P("shot", None, "freq")
    return jax.shard_map(shards, mesh=mesh, in_specs=in_specs, out_specs=out_specs, check_vma=False)
```

```python
import functools
import math

import jax
import jax.numpy as jnp
from jax import lax
from jax.experimental import pallas as pl
from jax.experimental.pallas import tpu as pltpu
from jax.sharding import PartitionSpec as P

NT = 1024
NF = 8
KMAX = 32
TAPS = 31


def extended(shard, sides, width):
    for axis, dim in sides:
        devices, length = (lax.axis_size(axis), shard.shape[dim])
        up = [(i, (i + 1) % devices) for i in range(devices - 1)]
        down = [(j, i) for i, j in up]
        last = lax.slice_in_dim(shard, length - width, length, axis=dim)
        leading = lax.slice_in_dim(shard, 0, width, axis=dim)
        before = lax.ppermute(last, axis, up)
        after = lax.ppermute(leading, axis, down)
        shard = jnp.concatenate([before, shard, after], axis=dim)
    return shard


def fourier_rows(bin_rows, first_time, sample_count, period):
    sample_times = first_time + jnp.arange(sample_count, dtype=jnp.int32)
    phases = bin_rows[:, None] * sample_times[None, :] % period
    angles = phases.astype(jnp.float32) * (2.0 * math.pi / period)
    return (jnp.cos(angles), jnp.sin(angles))


def multiply_kernel(
    incoming_ref, counts_ref, out_ref, qt_ref, acc_ref, recv_ref, sems, *, local_bins, shot_dev, receiver_dev, groups
):
    near = local_bins * 2 * shot_dev * receiver_dev
    width = shot_dev * groups
    qt_ref[...] = incoming_ref[:, 0:near].astype(jnp.float32).T
    me = lax.axis_index("shot")
    half = lax.axis_index("freq")
    block = 16

    def chunk(step, carry):
        top = pl.multiple_of(step * block, block)
        rows = pl.ds(top, block)
        for i in range(shot_dev):
            for r in range(receiver_dev):
                weights = [counts_ref[i, r, rows, h * groups : (h + 1) * groups] for h in range(shot_dev)]
                for f in range(local_bins):
                    real_sum = None
                    imag_sum = None
                    for h in range(shot_dev):
                        base_r = near + ((f * 2 + 0) * shot_dev + i) * width + h * groups
                        base_i = near + ((f * 2 + 1) * shot_dev + i) * width + h * groups
                        pr = incoming_ref[rows, base_r : base_r + groups].astype(jnp.float32)
                        pi = incoming_ref[rows, base_i : base_i + groups].astype(jnp.float32)
                        row_r = ((f * 2 + 0) * shot_dev + h) * receiver_dev + r
                        row_i = ((f * 2 + 1) * shot_dev + h) * receiver_dev + r
                        qr = qt_ref[row_r : row_r + 1, :]
                        qi = qt_ref[row_i : row_i + 1, :]
                        w = weights[h]
                        real_term = w * (pr * qr - pi * qi)
                        imag_term = w * (pr * qi + pi * qr)
                        real_sum = real_term if real_sum is None else real_sum + real_term
                        imag_sum = imag_term if imag_sum is None else imag_sum + imag_term
                    col_r = ((f * 2 + 0) * shot_dev + i) * receiver_dev + r
                    col_i = ((f * 2 + 1) * shot_dev + i) * receiver_dev + r
                    acc_ref[rows, col_r : col_r + 1] = jnp.sum(real_sum, axis=1, keepdims=True)
                    acc_ref[rows, col_i : col_i + 1] = jnp.sum(imag_sum, axis=1, keepdims=True)
        acc_ref[rows, :] = (acc_ref[rows, :] * KMAX ** (-0.5)).astype(jnp.bfloat16).astype(jnp.float32)
        for t in range(block):
            target = top + t

            @pl.when(target != me)
            def _():
                pltpu.make_async_remote_copy(
                    src_ref=acc_ref.at[pl.ds(target, 1)],
                    dst_ref=recv_ref.at[pl.ds(me, 1)],
                    send_sem=sems.at[0],
                    recv_sem=sems.at[1],
                    device_id=(target, half),
                    device_id_type=pl.DeviceIdType.MESH,
                ).start()

            @pl.when(target == me)
            def _():
                recv_ref[pl.ds(me, 1), :] = acc_ref[pl.ds(me, 1), :]

        return carry

    lax.fori_loop(0, groups // block, chunk, 0)
    every = pltpu.make_async_remote_copy(
        src_ref=acc_ref.at[pl.ds(0, groups - 1)],
        dst_ref=recv_ref.at[pl.ds(0, groups - 1)],
        send_sem=sems.at[0],
        recv_sem=sems.at[1],
        device_id=(me, half),
        device_id_type=pl.DeviceIdType.MESH,
    )
    every.wait_send()
    every.wait_recv()
    out_ref[...] = recv_ref[...]


def shards(traces, frequency_bins, aperture, lengths, filters):
    shot_dev, receivers, time_dev = traces.shape
    groups = lax.axis_size("shot")
    shots = shot_dev * groups
    receiver_dev = receivers // groups
    stride = receivers // shots
    freq_dev = lax.axis_size("freq")
    local_bins = NF // freq_dev
    start_time = lax.axis_index("freq") * time_dev
    half_taps = (TAPS - 1) // 2
    flat_traces = traces.reshape(shot_dev * receivers, time_dev)
    cosines, sines = fourier_rows(frequency_bins, start_time, time_dev, NT)
    basis_rows = (jnp.stack([cosines, -sines], axis=1) * NT ** (-0.5)).astype(jnp.bfloat16)
    basis_rows = basis_rows.reshape(NF * 2, time_dev)
    term = lax.dot_general(
        basis_rows, flat_traces, (((1,), (1,)), ((), ())), preferred_element_type=jnp.float32
    )
    spectra = lax.psum_scatter(
        term.reshape(NF, 2, shot_dev, receivers), "freq", scatter_dimension=0, tiled=True
    ).astype(jnp.bfloat16)
    rows = local_bins * 2 * shot_dev
    near = spectra.reshape(rows, groups, receiver_dev).transpose(1, 0, 2).reshape(groups, rows * receiver_dev)
    stations = jnp.concatenate(
        [spectra[:, :, :, 0 :: 2 * stride], spectra[:, :, :, stride :: 2 * stride]], axis=-1
    ).reshape(1, rows * shots)
    outgoing = jnp.concatenate([near, jnp.broadcast_to(stations, (groups, rows * shots))], axis=1)
    incoming = lax.all_to_all(outgoing, "shot", 0, 0, tiled=True)
    used = jnp.arange(KMAX, dtype=jnp.int32)[None, None, :] < lengths[:, :, None]
    codes = jnp.where(used, (aperture % shot_dev) * groups + aperture // shot_dev, -1)
    codes = codes.reshape(groups, shot_dev, receiver_dev, KMAX).transpose(1, 2, 0, 3)
    counts = jnp.sum(
        (codes[..., None] == jnp.arange(shots, dtype=jnp.int32)).astype(jnp.float32), axis=3
    )
    kernel = functools.partial(
        multiply_kernel, local_bins=local_bins, shot_dev=shot_dev, receiver_dev=receiver_dev, groups=groups
    )
    back = pl.pallas_call(
        kernel,
        out_shape=jax.ShapeDtypeStruct((groups, rows * receiver_dev), jnp.float32),
        in_specs=[pl.BlockSpec(memory_space=pltpu.VMEM)] * 2,
        out_specs=pl.BlockSpec(memory_space=pltpu.VMEM),
        scratch_shapes=[
            pltpu.VMEM((rows * receiver_dev, groups), jnp.float32),
            pltpu.VMEM((groups, rows * receiver_dev), jnp.float32),
            pltpu.VMEM((groups, rows * receiver_dev), jnp.float32),
            pltpu.SemaphoreType.DMA((2,)),
        ],
        compiler_params=pltpu.CompilerParams(has_side_effects=True),
        cost_estimate=pl.CostEstimate(
            flops=16 * groups * shots * rows * receiver_dev // 2, transcendentals=0, bytes_accessed=4 * 1024 * 1024
        ),
    )(incoming, counts)
    piece = lax.all_gather(back.astype(jnp.bfloat16), "freq", axis=0, tiled=False)
    piece = piece.reshape(freq_dev, groups, local_bins, 2, shot_dev, receiver_dev)
    piece = piece.transpose(4, 1, 5, 0, 2, 3).reshape(shot_dev, receivers, NF * 2)
    wide = time_dev + 2 * half_taps
    wide_times = start_time - half_taps + jnp.arange(wide, dtype=jnp.int32)
    inside = (wide_times >= 0) & (wide_times < NT)
    phases = frequency_bins[:, None] * jnp.clip(wide_times, 0, NT - 1)[None, :] % NT
    angles = phases.astype(jnp.float32) * (2.0 * math.pi / NT)
    wide_rows = jnp.stack([jnp.cos(angles), -jnp.sin(angles)], axis=1).astype(jnp.bfloat16)
    wide_rows = jnp.where(inside[None, None, :], wide_rows.astype(jnp.float32), 0.0).reshape(NF * 2, wide)
    taps = filters.astype(jnp.float32)
    shaped = sum(
        taps[:, tap, None, None] * wide_rows[None, :, 2 * half_taps - tap : 2 * half_taps - tap + time_dev]
        for tap in range(TAPS)
    )
    leading = shaped.astype(jnp.bfloat16)
    trailing = (shaped - leading.astype(jnp.float32)).astype(jnp.bfloat16)
    filtered = lax.dot_general(
        jnp.concatenate([piece, piece], axis=2),
        jnp.concatenate([leading, trailing], axis=1),
        (((2,), (1,)), ((0,), (0,))),
        preferred_element_type=jnp.float32,
    )
    return filtered.astype(jnp.bfloat16)


def solution(mesh):
    in_specs = (
        P("shot", None, "freq"),
        P(),
        P(None, "shot", None),
        P(None, "shot"),
        P("shot", None),
    )
    out_specs = P("shot", None, "freq")
    return jax.shard_map(shards, mesh=mesh, in_specs=in_specs, out_specs=out_specs, check_vma=False)
```

```python
import functools
import math

import jax
import jax.numpy as jnp
from jax import lax
from jax.experimental import pallas as pl
from jax.experimental.pallas import tpu as pltpu
from jax.sharding import PartitionSpec as P

NT = 1024
NF = 8
KMAX = 32
TAPS = 31


def extended(shard, sides, width):
    for axis, dim in sides:
        devices, length = (lax.axis_size(axis), shard.shape[dim])
        up = [(i, (i + 1) % devices) for i in range(devices - 1)]
        down = [(j, i) for i, j in up]
        last = lax.slice_in_dim(shard, length - width, length, axis=dim)
        leading = lax.slice_in_dim(shard, 0, width, axis=dim)
        before = lax.ppermute(last, axis, up)
        after = lax.ppermute(leading, axis, down)
        shard = jnp.concatenate([before, shard, after], axis=dim)
    return shard


def fourier_rows(bin_rows, first_time, sample_count, period):
    sample_times = first_time + jnp.arange(sample_count, dtype=jnp.int32)
    phases = bin_rows[:, None] * sample_times[None, :] % period
    angles = phases.astype(jnp.float32) * (2.0 * math.pi / period)
    return (jnp.cos(angles), jnp.sin(angles))


def multiply_kernel(
    incoming_ref, counts_ref, out_ref, qt_ref, acc_ref, recv_ref, sems, *, local_bins, shot_dev, receiver_dev, groups
):
    qt_ref[...] = incoming_ref[0].astype(jnp.float32).T
    me = lax.axis_index("shot")
    half = lax.axis_index("freq")
    block = 16

    def chunk(step, carry):
        top = pl.multiple_of(step * block, block)
        rows = pl.ds(top, block)
        for i in range(shot_dev):
            for r in range(receiver_dev):
                weights = [counts_ref[i, r, rows, h * groups : (h + 1) * groups] for h in range(shot_dev)]
                for f in range(local_bins):
                    real_sum = None
                    imag_sum = None
                    for h in range(shot_dev):
                        slab_r = 1 + ((f * 2 + 0) * shot_dev + i) * shot_dev + h
                        slab_i = 1 + ((f * 2 + 1) * shot_dev + i) * shot_dev + h
                        pr = incoming_ref[slab_r, rows, :].astype(jnp.float32)
                        pi = incoming_ref[slab_i, rows, :].astype(jnp.float32)
                        row_r = ((f * 2 + 0) * shot_dev + h) * receiver_dev + r
                        row_i = ((f * 2 + 1) * shot_dev + h) * receiver_dev + r
                        qr = qt_ref[row_r : row_r + 1, :]
                        qi = qt_ref[row_i : row_i + 1, :]
                        w = weights[h]
                        real_term = w * (pr * qr - pi * qi)
                        imag_term = w * (pr * qi + pi * qr)
                        real_sum = real_term if real_sum is None else real_sum + real_term
                        imag_sum = imag_term if imag_sum is None else imag_sum + imag_term
                    col_r = ((f * 2 + 0) * shot_dev + i) * receiver_dev + r
                    col_i = ((f * 2 + 1) * shot_dev + i) * receiver_dev + r
                    acc_ref[rows, col_r : col_r + 1] = jnp.sum(real_sum, axis=1, keepdims=True)
                    acc_ref[rows, col_i : col_i + 1] = jnp.sum(imag_sum, axis=1, keepdims=True)
        acc_ref[rows, :] = (acc_ref[rows, :] * KMAX ** (-0.5)).astype(jnp.bfloat16).astype(jnp.float32)
        for t in range(block):
            target = top + t

            @pl.when(target != me)
            def _():
                pltpu.make_async_remote_copy(
                    src_ref=acc_ref.at[pl.ds(target, 1)],
                    dst_ref=recv_ref.at[pl.ds(me, 1)],
                    send_sem=sems.at[0],
                    recv_sem=sems.at[1],
                    device_id=(target, half),
                    device_id_type=pl.DeviceIdType.MESH,
                ).start()

            @pl.when(target == me)
            def _():
                recv_ref[pl.ds(me, 1), :] = acc_ref[pl.ds(me, 1), :]

        return carry

    lax.fori_loop(0, groups // block, chunk, 0)
    every = pltpu.make_async_remote_copy(
        src_ref=acc_ref.at[pl.ds(0, groups - 1)],
        dst_ref=recv_ref.at[pl.ds(0, groups - 1)],
        send_sem=sems.at[0],
        recv_sem=sems.at[1],
        device_id=(me, half),
        device_id_type=pl.DeviceIdType.MESH,
    )
    every.wait_send()
    every.wait_recv()
    out_ref[...] = recv_ref[...]


def shards(traces, frequency_bins, aperture, lengths, filters):
    shot_dev, receivers, time_dev = traces.shape
    groups = lax.axis_size("shot")
    shots = shot_dev * groups
    receiver_dev = receivers // groups
    stride = receivers // shots
    freq_dev = lax.axis_size("freq")
    local_bins = NF // freq_dev
    start_time = lax.axis_index("freq") * time_dev
    half_taps = (TAPS - 1) // 2
    flat_traces = traces.reshape(shot_dev * receivers, time_dev)
    cosines, sines = fourier_rows(frequency_bins, start_time, time_dev, NT)
    basis_rows = (jnp.stack([cosines, -sines], axis=1) * NT ** (-0.5)).astype(jnp.bfloat16)
    basis_rows = basis_rows.reshape(NF * 2, time_dev)
    term = lax.dot_general(
        basis_rows, flat_traces, (((1,), (1,)), ((), ())), preferred_element_type=jnp.float32
    )
    spectra = lax.psum_scatter(
        term.reshape(NF, 2, shot_dev, receivers), "freq", scatter_dimension=0, tiled=True
    ).astype(jnp.bfloat16)
    rows = local_bins * 2 * shot_dev
    near = spectra.reshape(rows, groups, receiver_dev).transpose(1, 0, 2).reshape(groups, rows * receiver_dev)
    stations = jnp.concatenate(
        [spectra[:, :, :, 0 :: 2 * stride], spectra[:, :, :, stride :: 2 * stride]], axis=-1
    ).reshape(1, rows * shots)
    lanes = 128
    outgoing = jnp.concatenate(
        [
            near.reshape(groups, rows * receiver_dev // lanes, lanes).transpose(1, 0, 2),
            jnp.broadcast_to(stations.reshape(rows * shots // lanes, 1, lanes), (rows * shots // lanes, groups, lanes)),
        ],
        axis=0,
    )
    incoming = lax.all_to_all(outgoing, "shot", 1, 1, tiled=True)
    used = jnp.arange(KMAX, dtype=jnp.int32)[None, None, :] < lengths[:, :, None]
    codes = jnp.where(used, (aperture % shot_dev) * groups + aperture // shot_dev, -1)
    codes = codes.reshape(groups, shot_dev, receiver_dev, KMAX).transpose(1, 2, 0, 3)
    counts = jnp.sum(
        (codes[..., None] == jnp.arange(shots, dtype=jnp.int32)).astype(jnp.float32), axis=3
    )
    kernel = functools.partial(
        multiply_kernel, local_bins=local_bins, shot_dev=shot_dev, receiver_dev=receiver_dev, groups=groups
    )
    back = pl.pallas_call(
        kernel,
        out_shape=jax.ShapeDtypeStruct((groups, rows * receiver_dev), jnp.float32),
        in_specs=[pl.BlockSpec(memory_space=pltpu.VMEM)] * 2,
        out_specs=pl.BlockSpec(memory_space=pltpu.VMEM),
        scratch_shapes=[
            pltpu.VMEM((rows * receiver_dev, groups), jnp.float32),
            pltpu.VMEM((groups, rows * receiver_dev), jnp.float32),
            pltpu.VMEM((groups, rows * receiver_dev), jnp.float32),
            pltpu.SemaphoreType.DMA((2,)),
        ],
        compiler_params=pltpu.CompilerParams(has_side_effects=True),
        cost_estimate=pl.CostEstimate(
            flops=16 * groups * shots * rows * receiver_dev // 2, transcendentals=0, bytes_accessed=4 * 1024 * 1024
        ),
    )(incoming, counts)
    piece = lax.all_gather(back.astype(jnp.bfloat16), "freq", axis=0, tiled=False)
    piece = piece.reshape(freq_dev, groups, local_bins, 2, shot_dev, receiver_dev)
    piece = piece.transpose(4, 1, 5, 0, 2, 3).reshape(shot_dev, receivers, NF * 2)
    wide = time_dev + 2 * half_taps
    wide_times = start_time - half_taps + jnp.arange(wide, dtype=jnp.int32)
    inside = (wide_times >= 0) & (wide_times < NT)
    phases = frequency_bins[:, None] * jnp.clip(wide_times, 0, NT - 1)[None, :] % NT
    angles = phases.astype(jnp.float32) * (2.0 * math.pi / NT)
    wide_rows = jnp.stack([jnp.cos(angles), -jnp.sin(angles)], axis=1).astype(jnp.bfloat16)
    wide_rows = jnp.where(inside[None, None, :], wide_rows.astype(jnp.float32), 0.0).reshape(NF * 2, wide)
    taps = filters.astype(jnp.float32)
    shaped = sum(
        taps[:, tap, None, None] * wide_rows[None, :, 2 * half_taps - tap : 2 * half_taps - tap + time_dev]
        for tap in range(TAPS)
    )
    leading = shaped.astype(jnp.bfloat16)
    trailing = (shaped - leading.astype(jnp.float32)).astype(jnp.bfloat16)
    filtered = lax.dot_general(
        jnp.concatenate([piece, piece], axis=2),
        jnp.concatenate([leading, trailing], axis=1),
        (((2,), (1,)), ((0,), (0,))),
        preferred_element_type=jnp.float32,
    )
    return filtered.astype(jnp.bfloat16)


def solution(mesh):
    in_specs = (
        P("shot", None, "freq"),
        P(),
        P(None, "shot", None),
        P(None, "shot"),
        P("shot", None),
    )
    out_specs = P("shot", None, "freq")
    return jax.shard_map(shards, mesh=mesh, in_specs=in_specs, out_specs=out_specs, check_vma=False)
```

```python
import functools
import math

import jax
import jax.numpy as jnp
from jax import lax
from jax.experimental import pallas as pl
from jax.experimental.pallas import tpu as pltpu
from jax.sharding import PartitionSpec as P

NT = 1024
NF = 8
KMAX = 32
TAPS = 31


def extended(shard, sides, width):
    for axis, dim in sides:
        devices, length = (lax.axis_size(axis), shard.shape[dim])
        up = [(i, (i + 1) % devices) for i in range(devices - 1)]
        down = [(j, i) for i, j in up]
        last = lax.slice_in_dim(shard, length - width, length, axis=dim)
        leading = lax.slice_in_dim(shard, 0, width, axis=dim)
        before = lax.ppermute(last, axis, up)
        after = lax.ppermute(leading, axis, down)
        shard = jnp.concatenate([before, shard, after], axis=dim)
    return shard


def fourier_rows(bin_rows, first_time, sample_count, period):
    sample_times = first_time + jnp.arange(sample_count, dtype=jnp.int32)
    phases = bin_rows[:, None] * sample_times[None, :] % period
    angles = phases.astype(jnp.float32) * (2.0 * math.pi / period)
    return (jnp.cos(angles), jnp.sin(angles))


def multiply_kernel(
    incoming_ref, counts_ref, out_ref, qt_ref, acc_ref, recv_ref, sems, *, local_bins, shot_dev, receiver_dev, groups
):
    qt_ref[...] = incoming_ref[0].astype(jnp.float32).T
    me = lax.axis_index("shot")
    half = lax.axis_index("freq")
    block = 16

    steps = groups // block

    def chunk(step, carry):
        top = pl.multiple_of(lax.rem(step + me, steps) * block, block)
        rows = pl.ds(top, block)
        for i in range(shot_dev):
            for r in range(receiver_dev):
                weights = [counts_ref[i, r, rows, h * groups : (h + 1) * groups] for h in range(shot_dev)]
                for f in range(local_bins):
                    real_sum = None
                    imag_sum = None
                    for h in range(shot_dev):
                        slab_r = 1 + ((f * 2 + 0) * shot_dev + i) * shot_dev + h
                        slab_i = 1 + ((f * 2 + 1) * shot_dev + i) * shot_dev + h
                        pr = incoming_ref[slab_r, rows, :].astype(jnp.float32)
                        pi = incoming_ref[slab_i, rows, :].astype(jnp.float32)
                        row_r = ((f * 2 + 0) * shot_dev + h) * receiver_dev + r
                        row_i = ((f * 2 + 1) * shot_dev + h) * receiver_dev + r
                        qr = qt_ref[row_r : row_r + 1, :]
                        qi = qt_ref[row_i : row_i + 1, :]
                        w = weights[h]
                        real_term = w * (pr * qr - pi * qi)
                        imag_term = w * (pr * qi + pi * qr)
                        real_sum = real_term if real_sum is None else real_sum + real_term
                        imag_sum = imag_term if imag_sum is None else imag_sum + imag_term
                    col_r = ((f * 2 + 0) * shot_dev + i) * receiver_dev + r
                    col_i = ((f * 2 + 1) * shot_dev + i) * receiver_dev + r
                    acc_ref[rows, col_r : col_r + 1] = jnp.sum(real_sum, axis=1, keepdims=True)
                    acc_ref[rows, col_i : col_i + 1] = jnp.sum(imag_sum, axis=1, keepdims=True)
        acc_ref[rows, :] = (acc_ref[rows, :] * KMAX ** (-0.5)).astype(jnp.bfloat16).astype(jnp.float32)
        for t in range(block):
            target = top + t

            @pl.when(target != me)
            def _():
                pltpu.make_async_remote_copy(
                    src_ref=acc_ref.at[pl.ds(target, 1)],
                    dst_ref=recv_ref.at[pl.ds(me, 1)],
                    send_sem=sems.at[0],
                    recv_sem=sems.at[1],
                    device_id=(target, half),
                    device_id_type=pl.DeviceIdType.MESH,
                ).start()

            @pl.when(target == me)
            def _():
                recv_ref[pl.ds(me, 1), :] = acc_ref[pl.ds(me, 1), :]

        return carry

    lax.fori_loop(0, steps, chunk, 0)
    every = pltpu.make_async_remote_copy(
        src_ref=acc_ref.at[pl.ds(0, groups - 1)],
        dst_ref=recv_ref.at[pl.ds(0, groups - 1)],
        send_sem=sems.at[0],
        recv_sem=sems.at[1],
        device_id=(me, half),
        device_id_type=pl.DeviceIdType.MESH,
    )
    every.wait_send()
    every.wait_recv()
    out_ref[...] = recv_ref[...]


def shards(traces, frequency_bins, aperture, lengths, filters):
    shot_dev, receivers, time_dev = traces.shape
    groups = lax.axis_size("shot")
    shots = shot_dev * groups
    receiver_dev = receivers // groups
    stride = receivers // shots
    freq_dev = lax.axis_size("freq")
    local_bins = NF // freq_dev
    start_time = lax.axis_index("freq") * time_dev
    half_taps = (TAPS - 1) // 2
    flat_traces = traces.reshape(shot_dev * receivers, time_dev)
    cosines, sines = fourier_rows(frequency_bins, start_time, time_dev, NT)
    basis_rows = (jnp.stack([cosines, -sines], axis=1) * NT ** (-0.5)).astype(jnp.bfloat16)
    basis_rows = basis_rows.reshape(NF * 2, time_dev)
    term = lax.dot_general(
        basis_rows, flat_traces, (((1,), (1,)), ((), ())), preferred_element_type=jnp.float32
    )
    term = term.reshape(NF, 2, shot_dev, receivers)
    core = lax.axis_index("freq")
    mine = lax.dynamic_slice_in_dim(term, core * local_bins, local_bins, axis=0)
    theirs = lax.dynamic_slice_in_dim(term, (1 - core) * local_bins, local_bins, axis=0)
    theirs = lax.ppermute(theirs, "freq", [(0, 1), (1, 0)])
    spectra = (mine + theirs).astype(jnp.bfloat16)
    rows = local_bins * 2 * shot_dev
    near = spectra.reshape(rows, groups, receiver_dev).transpose(1, 0, 2).reshape(groups, rows * receiver_dev)
    stations = jnp.concatenate(
        [spectra[:, :, :, 0 :: 2 * stride], spectra[:, :, :, stride :: 2 * stride]], axis=-1
    ).reshape(1, rows * shots)
    lanes = 128
    outgoing = jnp.concatenate(
        [
            near.reshape(groups, rows * receiver_dev // lanes, lanes).transpose(1, 0, 2),
            jnp.broadcast_to(stations.reshape(rows * shots // lanes, 1, lanes), (rows * shots // lanes, groups, lanes)),
        ],
        axis=0,
    )
    incoming = lax.all_to_all(outgoing, "shot", 1, 1, tiled=True)
    used = jnp.arange(KMAX, dtype=jnp.int32)[None, None, :] < lengths[:, :, None]
    codes = jnp.where(used, (aperture % shot_dev) * groups + aperture // shot_dev, -1)
    codes = codes.reshape(groups, shot_dev, receiver_dev, KMAX).transpose(1, 2, 0, 3)
    counts = jnp.sum(
        (codes[..., None] == jnp.arange(shots, dtype=jnp.int32)).astype(jnp.float32), axis=3
    )
    kernel = functools.partial(
        multiply_kernel, local_bins=local_bins, shot_dev=shot_dev, receiver_dev=receiver_dev, groups=groups
    )
    back = pl.pallas_call(
        kernel,
        out_shape=jax.ShapeDtypeStruct((groups, rows * receiver_dev), jnp.float32),
        in_specs=[pl.BlockSpec(memory_space=pltpu.VMEM)] * 2,
        out_specs=pl.BlockSpec(memory_space=pltpu.VMEM),
        scratch_shapes=[
            pltpu.VMEM((rows * receiver_dev, groups), jnp.float32),
            pltpu.VMEM((groups, rows * receiver_dev), jnp.float32),
            pltpu.VMEM((groups, rows * receiver_dev), jnp.float32),
            pltpu.SemaphoreType.DMA((2,)),
        ],
        compiler_params=pltpu.CompilerParams(has_side_effects=True),
        cost_estimate=pl.CostEstimate(
            flops=16 * groups * shots * rows * receiver_dev // 2, transcendentals=0, bytes_accessed=4 * 1024 * 1024
        ),
    )(incoming, counts)
    piece = lax.all_gather(back.astype(jnp.bfloat16), "freq", axis=0, tiled=False)
    piece = piece.reshape(freq_dev, groups, local_bins, 2, shot_dev, receiver_dev)
    piece = piece.transpose(4, 1, 5, 0, 2, 3).reshape(shot_dev, receivers, NF * 2)
    wide = time_dev + 2 * half_taps
    wide_times = start_time - half_taps + jnp.arange(wide, dtype=jnp.int32)
    inside = (wide_times >= 0) & (wide_times < NT)
    phases = frequency_bins[:, None] * jnp.clip(wide_times, 0, NT - 1)[None, :] % NT
    angles = phases.astype(jnp.float32) * (2.0 * math.pi / NT)
    wide_rows = jnp.stack([jnp.cos(angles), -jnp.sin(angles)], axis=1).astype(jnp.bfloat16)
    wide_rows = jnp.where(inside[None, None, :], wide_rows.astype(jnp.float32), 0.0).reshape(NF * 2, wide)
    taps = filters.astype(jnp.float32)
    shaped = sum(
        taps[:, tap, None, None] * wide_rows[None, :, 2 * half_taps - tap : 2 * half_taps - tap + time_dev]
        for tap in range(TAPS)
    )
    leading = shaped.astype(jnp.bfloat16)
    trailing = (shaped - leading.astype(jnp.float32)).astype(jnp.bfloat16)
    filtered = lax.dot_general(
        jnp.concatenate([piece, piece], axis=2),
        jnp.concatenate([leading, trailing], axis=1),
        (((2,), (1,)), ((0,), (0,))),
        preferred_element_type=jnp.float32,
    )
    return filtered.astype(jnp.bfloat16)


def solution(mesh):
    in_specs = (
        P("shot", None, "freq"),
        P(),
        P(None, "shot", None),
        P(None, "shot"),
        P("shot", None),
    )
    out_specs = P("shot", None, "freq")
    return jax.shard_map(shards, mesh=mesh, in_specs=in_specs, out_specs=out_specs, check_vma=False)
```

```python
import functools
import math

import jax
import jax.numpy as jnp
from jax import lax
from jax.experimental import pallas as pl
from jax.experimental.pallas import tpu as pltpu
from jax.sharding import PartitionSpec as P

NT = 1024
NF = 8
KMAX = 32
TAPS = 31


def extended(shard, sides, width):
    for axis, dim in sides:
        devices, length = (lax.axis_size(axis), shard.shape[dim])
        up = [(i, (i + 1) % devices) for i in range(devices - 1)]
        down = [(j, i) for i, j in up]
        last = lax.slice_in_dim(shard, length - width, length, axis=dim)
        leading = lax.slice_in_dim(shard, 0, width, axis=dim)
        before = lax.ppermute(last, axis, up)
        after = lax.ppermute(leading, axis, down)
        shard = jnp.concatenate([before, shard, after], axis=dim)
    return shard


def fourier_rows(bin_rows, first_time, sample_count, period):
    sample_times = first_time + jnp.arange(sample_count, dtype=jnp.int32)
    phases = bin_rows[:, None] * sample_times[None, :] % period
    angles = phases.astype(jnp.float32) * (2.0 * math.pi / period)
    return (jnp.cos(angles), jnp.sin(angles))


def multiply_kernel(
    incoming_ref, counts_ref, out_ref, qt_ref, acc_ref, recv_ref, sems, *, local_bins, shot_dev, receiver_dev, groups
):
    qt_ref[...] = incoming_ref[0].astype(jnp.float32).T
    me = lax.axis_index("shot")
    half = lax.axis_index("freq")
    block = 16

    steps = groups // block

    def chunk(step, carry):
        top = pl.multiple_of(lax.rem(step + me, steps) * block, block)
        rows = pl.ds(top, block)
        for i in range(shot_dev):
            for r in range(receiver_dev):
                weights = [counts_ref[i, r, rows, h * groups : (h + 1) * groups] for h in range(shot_dev)]
                for f in range(local_bins):
                    real_sum = None
                    imag_sum = None
                    for h in range(shot_dev):
                        slab_r = 1 + ((f * 2 + 0) * shot_dev + i) * shot_dev + h
                        slab_i = 1 + ((f * 2 + 1) * shot_dev + i) * shot_dev + h
                        pr = incoming_ref[slab_r, rows, :].astype(jnp.float32)
                        pi = incoming_ref[slab_i, rows, :].astype(jnp.float32)
                        row_r = ((f * 2 + 0) * shot_dev + h) * receiver_dev + r
                        row_i = ((f * 2 + 1) * shot_dev + h) * receiver_dev + r
                        qr = qt_ref[row_r : row_r + 1, :]
                        qi = qt_ref[row_i : row_i + 1, :]
                        w = weights[h]
                        real_term = w * (pr * qr - pi * qi)
                        imag_term = w * (pr * qi + pi * qr)
                        real_sum = real_term if real_sum is None else real_sum + real_term
                        imag_sum = imag_term if imag_sum is None else imag_sum + imag_term
                    col_r = ((f * 2 + 0) * shot_dev + i) * receiver_dev + r
                    col_i = ((f * 2 + 1) * shot_dev + i) * receiver_dev + r
                    acc_ref[rows, col_r : col_r + 1] = jnp.sum(real_sum, axis=1, keepdims=True)
                    acc_ref[rows, col_i : col_i + 1] = jnp.sum(imag_sum, axis=1, keepdims=True)
        acc_ref[rows, :] = (acc_ref[rows, :] * KMAX ** (-0.5)).astype(jnp.bfloat16).astype(jnp.float32)
        for t in range(block):
            target = top + t

            @pl.when(target != me)
            def _():
                pltpu.make_async_remote_copy(
                    src_ref=acc_ref.at[pl.ds(target, 1)],
                    dst_ref=recv_ref.at[pl.ds(me, 1)],
                    send_sem=sems.at[0],
                    recv_sem=sems.at[1],
                    device_id=(target, half),
                    device_id_type=pl.DeviceIdType.MESH,
                ).start()

            @pl.when(target == me)
            def _():
                recv_ref[pl.ds(me, 1), :] = acc_ref[pl.ds(me, 1), :]

        return carry

    lax.fori_loop(0, steps, chunk, 0)
    every = pltpu.make_async_remote_copy(
        src_ref=acc_ref.at[pl.ds(0, groups - 1)],
        dst_ref=recv_ref.at[pl.ds(0, groups - 1)],
        send_sem=sems.at[0],
        recv_sem=sems.at[1],
        device_id=(me, half),
        device_id_type=pl.DeviceIdType.MESH,
    )
    every.wait_send()
    every.wait_recv()
    out_ref[...] = recv_ref[...].astype(out_ref.dtype)


def shards(traces, frequency_bins, aperture, lengths, filters):
    shot_dev, receivers, time_dev = traces.shape
    groups = lax.axis_size("shot")
    shots = shot_dev * groups
    receiver_dev = receivers // groups
    stride = receivers // shots
    freq_dev = lax.axis_size("freq")
    local_bins = NF // freq_dev
    start_time = lax.axis_index("freq") * time_dev
    half_taps = (TAPS - 1) // 2
    flat_traces = traces.reshape(shot_dev * receivers, time_dev)
    cosines, sines = fourier_rows(frequency_bins, start_time, time_dev, NT)
    basis_rows = (jnp.stack([cosines, -sines], axis=1) * NT ** (-0.5)).astype(jnp.bfloat16)
    basis_rows = basis_rows.reshape(NF * 2, time_dev)
    term = lax.dot_general(
        basis_rows, flat_traces, (((1,), (1,)), ((), ())), preferred_element_type=jnp.float32
    )
    term = term.reshape(NF, 2, shot_dev, receivers)
    core = lax.axis_index("freq")
    mine = lax.dynamic_slice_in_dim(term, core * local_bins, local_bins, axis=0)
    theirs = lax.dynamic_slice_in_dim(term, (1 - core) * local_bins, local_bins, axis=0)
    theirs = lax.ppermute(theirs, "freq", [(0, 1), (1, 0)])
    spectra = (mine + theirs).astype(jnp.bfloat16)
    rows = local_bins * 2 * shot_dev
    near = spectra.reshape(rows, groups, receiver_dev).transpose(1, 0, 2).reshape(groups, rows * receiver_dev)
    stations = jnp.concatenate(
        [spectra[:, :, :, 0 :: 2 * stride], spectra[:, :, :, stride :: 2 * stride]], axis=-1
    ).reshape(1, rows * shots)
    lanes = 128
    outgoing = jnp.concatenate(
        [
            near.reshape(groups, rows * receiver_dev // lanes, lanes).transpose(1, 0, 2),
            jnp.broadcast_to(stations.reshape(rows * shots // lanes, 1, lanes), (rows * shots // lanes, groups, lanes)),
        ],
        axis=0,
    )
    incoming = lax.all_to_all(outgoing, "shot", 1, 1, tiled=True)
    used = jnp.arange(KMAX, dtype=jnp.int32)[None, None, :] < lengths[:, :, None]
    codes = jnp.where(used, (aperture % shot_dev) * groups + aperture // shot_dev, -1)
    codes = codes.reshape(groups, shot_dev, receiver_dev, KMAX).transpose(1, 2, 0, 3)
    counts = jnp.sum(
        (codes[..., None] == jnp.arange(shots, dtype=jnp.int32)).astype(jnp.float32), axis=3
    )
    kernel = functools.partial(
        multiply_kernel, local_bins=local_bins, shot_dev=shot_dev, receiver_dev=receiver_dev, groups=groups
    )
    back = pl.pallas_call(
        kernel,
        out_shape=jax.ShapeDtypeStruct((groups, rows * receiver_dev), jnp.bfloat16),
        in_specs=[pl.BlockSpec(memory_space=pltpu.VMEM)] * 2,
        out_specs=pl.BlockSpec(memory_space=pltpu.VMEM),
        scratch_shapes=[
            pltpu.VMEM((rows * receiver_dev, groups), jnp.float32),
            pltpu.VMEM((groups, rows * receiver_dev), jnp.float32),
            pltpu.VMEM((groups, rows * receiver_dev), jnp.float32),
            pltpu.SemaphoreType.DMA((2,)),
        ],
        compiler_params=pltpu.CompilerParams(has_side_effects=True),
        cost_estimate=pl.CostEstimate(
            flops=16 * groups * shots * rows * receiver_dev // 2, transcendentals=0, bytes_accessed=4 * 1024 * 1024
        ),
    )(incoming, counts)
    piece = lax.all_gather(back, "freq", axis=0, tiled=False)
    piece = piece.reshape(freq_dev, groups, local_bins, 2, shot_dev, receiver_dev)
    piece = piece.transpose(4, 1, 5, 0, 2, 3).reshape(shot_dev, receivers, NF * 2)
    wide = time_dev + 2 * half_taps
    wide_times = start_time - half_taps + jnp.arange(wide, dtype=jnp.int32)
    inside = (wide_times >= 0) & (wide_times < NT)
    phases = frequency_bins[:, None] * jnp.clip(wide_times, 0, NT - 1)[None, :] % NT
    angles = phases.astype(jnp.float32) * (2.0 * math.pi / NT)
    wide_rows = jnp.stack([jnp.cos(angles), -jnp.sin(angles)], axis=1).astype(jnp.bfloat16)
    wide_rows = jnp.where(inside[None, None, :], wide_rows.astype(jnp.float32), 0.0).reshape(NF * 2, wide)
    taps = filters.astype(jnp.float32)
    shaped = sum(
        taps[:, tap, None, None] * wide_rows[None, :, 2 * half_taps - tap : 2 * half_taps - tap + time_dev]
        for tap in range(TAPS)
    )
    leading = shaped.astype(jnp.bfloat16)
    trailing = (shaped - leading.astype(jnp.float32)).astype(jnp.bfloat16)
    filtered = lax.dot_general(
        jnp.concatenate([piece, piece], axis=2),
        jnp.concatenate([leading, trailing], axis=1),
        (((2,), (1,)), ((0,), (0,))),
        preferred_element_type=jnp.float32,
    )
    return filtered.astype(jnp.bfloat16)


def solution(mesh):
    in_specs = (
        P("shot", None, "freq"),
        P(),
        P(None, "shot", None),
        P(None, "shot"),
        P("shot", None),
    )
    out_specs = P("shot", None, "freq")
    return jax.shard_map(shards, mesh=mesh, in_specs=in_specs, out_specs=out_specs, check_vma=False)
```

```python
import functools
import math

import jax
import jax.numpy as jnp
from jax import lax
from jax.experimental import pallas as pl
from jax.experimental.pallas import tpu as pltpu
from jax.sharding import PartitionSpec as P

NT = 1024
NF = 8
KMAX = 32
TAPS = 31


def extended(shard, sides, width):
    for axis, dim in sides:
        devices, length = (lax.axis_size(axis), shard.shape[dim])
        up = [(i, (i + 1) % devices) for i in range(devices - 1)]
        down = [(j, i) for i, j in up]
        last = lax.slice_in_dim(shard, length - width, length, axis=dim)
        leading = lax.slice_in_dim(shard, 0, width, axis=dim)
        before = lax.ppermute(last, axis, up)
        after = lax.ppermute(leading, axis, down)
        shard = jnp.concatenate([before, shard, after], axis=dim)
    return shard


def fourier_rows(bin_rows, first_time, sample_count, period):
    sample_times = first_time + jnp.arange(sample_count, dtype=jnp.int32)
    phases = bin_rows[:, None] * sample_times[None, :] % period
    angles = phases.astype(jnp.float32) * (2.0 * math.pi / period)
    return (jnp.cos(angles), jnp.sin(angles))


def multiply_kernel(
    incoming_ref, counts_ref, out_ref, qt_ref, acc_ref, recv_ref, sems, *, local_bins, shot_dev, receiver_dev, groups
):
    qt_ref[...] = incoming_ref[0].astype(jnp.float32).T
    me = lax.axis_index("shot")
    half = lax.axis_index("freq")
    block = 16

    steps = groups // block

    def remote_send(target):
        pltpu.make_async_remote_copy(
            src_ref=acc_ref.at[pl.ds(target, 1)],
            dst_ref=recv_ref.at[pl.ds(me, 1)],
            send_sem=sems.at[0],
            recv_sem=sems.at[1],
            device_id=(target, half),
            device_id_type=pl.DeviceIdType.MESH,
        ).start()

    def compute(top):
        rows = pl.ds(top, block)
        for i in range(shot_dev):
            for r in range(receiver_dev):
                weights = [counts_ref[i, r, rows, h * groups : (h + 1) * groups] for h in range(shot_dev)]
                for f in range(local_bins):
                    real_sum = None
                    imag_sum = None
                    for h in range(shot_dev):
                        slab_r = 1 + ((f * 2 + 0) * shot_dev + i) * shot_dev + h
                        slab_i = 1 + ((f * 2 + 1) * shot_dev + i) * shot_dev + h
                        pr = incoming_ref[slab_r, rows, :].astype(jnp.float32)
                        pi = incoming_ref[slab_i, rows, :].astype(jnp.float32)
                        row_r = ((f * 2 + 0) * shot_dev + h) * receiver_dev + r
                        row_i = ((f * 2 + 1) * shot_dev + h) * receiver_dev + r
                        qr = qt_ref[row_r : row_r + 1, :]
                        qi = qt_ref[row_i : row_i + 1, :]
                        w = weights[h]
                        real_term = w * (pr * qr - pi * qi)
                        imag_term = w * (pr * qi + pi * qr)
                        real_sum = real_term if real_sum is None else real_sum + real_term
                        imag_sum = imag_term if imag_sum is None else imag_sum + imag_term
                    col_r = ((f * 2 + 0) * shot_dev + i) * receiver_dev + r
                    col_i = ((f * 2 + 1) * shot_dev + i) * receiver_dev + r
                    acc_ref[rows, col_r : col_r + 1] = jnp.sum(real_sum, axis=1, keepdims=True)
                    acc_ref[rows, col_i : col_i + 1] = jnp.sum(imag_sum, axis=1, keepdims=True)
        acc_ref[rows, :] = (acc_ref[rows, :] * KMAX ** (-0.5)).astype(jnp.bfloat16).astype(jnp.float32)

    own_block = me // block
    own_top = pl.multiple_of(own_block * block, block)
    compute(own_top)
    for t in range(block):
        target = own_top + lax.rem(me + t, block)

        @pl.when(target != me)
        def _():
            remote_send(target)

    recv_ref[pl.ds(me, 1), :] = acc_ref[pl.ds(me, 1), :]

    def chunk(step, carry):
        top = pl.multiple_of(lax.rem(own_block + step, steps) * block, block)
        compute(top)
        for t in range(block):
            remote_send(top + lax.rem(me + t, block))
        return carry

    lax.fori_loop(1, steps, chunk, 0)
    every = pltpu.make_async_remote_copy(
        src_ref=acc_ref.at[pl.ds(0, groups - 1)],
        dst_ref=recv_ref.at[pl.ds(0, groups - 1)],
        send_sem=sems.at[0],
        recv_sem=sems.at[1],
        device_id=(me, half),
        device_id_type=pl.DeviceIdType.MESH,
    )
    every.wait_send()
    every.wait_recv()
    out_ref[...] = recv_ref[...].astype(out_ref.dtype)


def shards(traces, frequency_bins, aperture, lengths, filters):
    shot_dev, receivers, time_dev = traces.shape
    groups = lax.axis_size("shot")
    shots = shot_dev * groups
    receiver_dev = receivers // groups
    stride = receivers // shots
    freq_dev = lax.axis_size("freq")
    local_bins = NF // freq_dev
    start_time = lax.axis_index("freq") * time_dev
    half_taps = (TAPS - 1) // 2
    flat_traces = traces.reshape(shot_dev * receivers, time_dev)
    cosines, sines = fourier_rows(frequency_bins, start_time, time_dev, NT)
    basis_rows = (jnp.stack([cosines, -sines], axis=1) * NT ** (-0.5)).astype(jnp.bfloat16)
    basis_rows = basis_rows.reshape(NF * 2, time_dev)
    term = lax.dot_general(
        basis_rows, flat_traces, (((1,), (1,)), ((), ())), preferred_element_type=jnp.float32
    )
    term = term.reshape(NF, 2, shot_dev, receivers)
    core = lax.axis_index("freq")
    mine = lax.dynamic_slice_in_dim(term, core * local_bins, local_bins, axis=0)
    theirs = lax.dynamic_slice_in_dim(term, (1 - core) * local_bins, local_bins, axis=0)
    theirs = lax.ppermute(theirs, "freq", [(0, 1), (1, 0)])
    spectra = (mine + theirs).astype(jnp.bfloat16)
    rows = local_bins * 2 * shot_dev
    near = spectra.reshape(rows, groups, receiver_dev).transpose(1, 0, 2).reshape(groups, rows * receiver_dev)
    stations = jnp.concatenate(
        [spectra[:, :, :, 0 :: 2 * stride], spectra[:, :, :, stride :: 2 * stride]], axis=-1
    ).reshape(1, rows * shots)
    lanes = 128
    outgoing = jnp.concatenate(
        [
            near.reshape(groups, rows * receiver_dev // lanes, lanes).transpose(1, 0, 2),
            jnp.broadcast_to(stations.reshape(rows * shots // lanes, 1, lanes), (rows * shots // lanes, groups, lanes)),
        ],
        axis=0,
    )
    incoming = lax.all_to_all(outgoing, "shot", 1, 1, tiled=True)
    used = jnp.arange(KMAX, dtype=jnp.int32)[None, None, :] < lengths[:, :, None]
    codes = jnp.where(used, (aperture % shot_dev) * groups + aperture // shot_dev, -1)
    codes = codes.reshape(groups, shot_dev, receiver_dev, KMAX).transpose(1, 2, 0, 3)
    counts = jnp.sum(
        (codes[..., None] == jnp.arange(shots, dtype=jnp.int32)).astype(jnp.float32), axis=3
    )
    kernel = functools.partial(
        multiply_kernel, local_bins=local_bins, shot_dev=shot_dev, receiver_dev=receiver_dev, groups=groups
    )
    back = pl.pallas_call(
        kernel,
        out_shape=jax.ShapeDtypeStruct((groups, rows * receiver_dev), jnp.bfloat16),
        in_specs=[pl.BlockSpec(memory_space=pltpu.VMEM)] * 2,
        out_specs=pl.BlockSpec(memory_space=pltpu.VMEM),
        scratch_shapes=[
            pltpu.VMEM((rows * receiver_dev, groups), jnp.float32),
            pltpu.VMEM((groups, rows * receiver_dev), jnp.float32),
            pltpu.VMEM((groups, rows * receiver_dev), jnp.float32),
            pltpu.SemaphoreType.DMA((2,)),
        ],
        compiler_params=pltpu.CompilerParams(has_side_effects=True),
        cost_estimate=pl.CostEstimate(
            flops=16 * groups * shots * rows * receiver_dev // 2, transcendentals=0, bytes_accessed=4 * 1024 * 1024
        ),
    )(incoming, counts)
    piece = lax.all_gather(back, "freq", axis=0, tiled=False)
    piece = piece.reshape(freq_dev, groups, local_bins, 2, shot_dev, receiver_dev)
    piece = piece.transpose(4, 1, 5, 0, 2, 3).reshape(shot_dev, receivers, NF * 2)
    wide = time_dev + 2 * half_taps
    wide_times = start_time - half_taps + jnp.arange(wide, dtype=jnp.int32)
    inside = (wide_times >= 0) & (wide_times < NT)
    phases = frequency_bins[:, None] * jnp.clip(wide_times, 0, NT - 1)[None, :] % NT
    angles = phases.astype(jnp.float32) * (2.0 * math.pi / NT)
    wide_rows = jnp.stack([jnp.cos(angles), -jnp.sin(angles)], axis=1).astype(jnp.bfloat16)
    wide_rows = jnp.where(inside[None, None, :], wide_rows.astype(jnp.float32), 0.0).reshape(NF * 2, wide)
    taps = filters.astype(jnp.float32)
    shaped = sum(
        taps[:, tap, None, None] * wide_rows[None, :, 2 * half_taps - tap : 2 * half_taps - tap + time_dev]
        for tap in range(TAPS)
    )
    leading = shaped.astype(jnp.bfloat16)
    trailing = (shaped - leading.astype(jnp.float32)).astype(jnp.bfloat16)
    filtered = lax.dot_general(
        jnp.concatenate([piece, piece], axis=2),
        jnp.concatenate([leading, trailing], axis=1),
        (((2,), (1,)), ((0,), (0,))),
        preferred_element_type=jnp.float32,
    )
    return filtered.astype(jnp.bfloat16)


def solution(mesh):
    in_specs = (
        P("shot", None, "freq"),
        P(),
        P(None, "shot", None),
        P(None, "shot"),
        P("shot", None),
    )
    out_specs = P("shot", None, "freq")
    return jax.shard_map(shards, mesh=mesh, in_specs=in_specs, out_specs=out_specs, check_vma=False)
```

```python
import functools
import math

import jax
import jax.numpy as jnp
from jax import lax
from jax.experimental import pallas as pl
from jax.experimental.pallas import tpu as pltpu
from jax.sharding import PartitionSpec as P

NT = 1024
NF = 8
KMAX = 32
TAPS = 31


def extended(shard, sides, width):
    for axis, dim in sides:
        devices, length = (lax.axis_size(axis), shard.shape[dim])
        up = [(i, (i + 1) % devices) for i in range(devices - 1)]
        down = [(j, i) for i, j in up]
        last = lax.slice_in_dim(shard, length - width, length, axis=dim)
        leading = lax.slice_in_dim(shard, 0, width, axis=dim)
        before = lax.ppermute(last, axis, up)
        after = lax.ppermute(leading, axis, down)
        shard = jnp.concatenate([before, shard, after], axis=dim)
    return shard


def fourier_rows(bin_rows, first_time, sample_count, period):
    sample_times = first_time + jnp.arange(sample_count, dtype=jnp.int32)
    phases = bin_rows[:, None] * sample_times[None, :] % period
    angles = phases.astype(jnp.float32) * (2.0 * math.pi / period)
    return (jnp.cos(angles), jnp.sin(angles))


def multiply_kernel(
    incoming_ref, counts_ref, out_ref, qt_ref, acc_ref, recv_ref, sems, *, local_bins, shot_dev, receiver_dev, groups
):
    qt_ref[...] = incoming_ref[0].astype(jnp.float32).T
    me = lax.axis_index("shot")
    half = lax.axis_index("freq")
    block = 16

    steps = groups // block

    def remote_send(target):
        pltpu.make_async_remote_copy(
            src_ref=acc_ref.at[pl.ds(target, 1)],
            dst_ref=recv_ref.at[pl.ds(me, 1)],
            send_sem=sems.at[0],
            recv_sem=sems.at[1],
            device_id=(target, half),
            device_id_type=pl.DeviceIdType.MESH,
        ).start()

    def compute(top):
        rows = pl.ds(top, block)
        for i in range(shot_dev):
            for r in range(receiver_dev):
                weights = [counts_ref[i, r, rows, h * groups : (h + 1) * groups] for h in range(shot_dev)]
                for f in range(local_bins):
                    real_sum = None
                    imag_sum = None
                    for h in range(shot_dev):
                        slab_r = 1 + ((f * 2 + 0) * shot_dev + i) * shot_dev + h
                        slab_i = 1 + ((f * 2 + 1) * shot_dev + i) * shot_dev + h
                        pr = incoming_ref[slab_r, rows, :].astype(jnp.float32)
                        pi = incoming_ref[slab_i, rows, :].astype(jnp.float32)
                        row_r = ((f * 2 + 0) * shot_dev + h) * receiver_dev + r
                        row_i = ((f * 2 + 1) * shot_dev + h) * receiver_dev + r
                        qr = qt_ref[row_r : row_r + 1, :]
                        qi = qt_ref[row_i : row_i + 1, :]
                        w = weights[h]
                        real_term = w * (pr * qr - pi * qi)
                        imag_term = w * (pr * qi + pi * qr)
                        real_sum = real_term if real_sum is None else real_sum + real_term
                        imag_sum = imag_term if imag_sum is None else imag_sum + imag_term
                    col_r = ((f * 2 + 0) * shot_dev + i) * receiver_dev + r
                    col_i = ((f * 2 + 1) * shot_dev + i) * receiver_dev + r
                    acc_ref[rows, col_r : col_r + 1] = jnp.sum(real_sum, axis=1, keepdims=True)
                    acc_ref[rows, col_i : col_i + 1] = jnp.sum(imag_sum, axis=1, keepdims=True)
        acc_ref[rows, :] = (acc_ref[rows, :] * KMAX ** (-0.5)).astype(jnp.bfloat16).astype(jnp.float32)

    own_block = me // block
    own_top = pl.multiple_of(own_block * block, block)
    compute(own_top)
    for t in range(block):
        target = own_top + lax.rem(me + t, block)

        @pl.when(target != me)
        def _():
            remote_send(target)

    recv_ref[pl.ds(me, 1), :] = acc_ref[pl.ds(me, 1), :]

    def chunk(step, carry):
        top = pl.multiple_of(lax.rem(own_block + step, steps) * block, block)
        compute(top)
        for t in range(block):
            remote_send(top + lax.rem(me + t, block))
        return carry

    lax.fori_loop(1, steps, chunk, 0)
    every = pltpu.make_async_remote_copy(
        src_ref=acc_ref.at[pl.ds(0, groups - 1)],
        dst_ref=recv_ref.at[pl.ds(0, groups - 1)],
        send_sem=sems.at[0],
        recv_sem=sems.at[1],
        device_id=(me, half),
        device_id_type=pl.DeviceIdType.MESH,
    )
    every.wait_send()
    every.wait_recv()
    out_ref[...] = recv_ref[...].astype(out_ref.dtype)


def shards(traces, frequency_bins, aperture, lengths, filters):
    shot_dev, receivers, time_dev = traces.shape
    groups = lax.axis_size("shot")
    shots = shot_dev * groups
    receiver_dev = receivers // groups
    stride = receivers // shots
    freq_dev = lax.axis_size("freq")
    local_bins = NF // freq_dev
    start_time = lax.axis_index("freq") * time_dev
    half_taps = (TAPS - 1) // 2
    flat_traces = traces.reshape(shot_dev * receivers, time_dev)
    cosines, sines = fourier_rows(frequency_bins, start_time, time_dev, NT)
    basis_rows = (jnp.stack([cosines, -sines], axis=1) * NT ** (-0.5)).astype(jnp.bfloat16)
    basis_rows = basis_rows.reshape(NF * 2, time_dev)
    term = lax.dot_general(
        basis_rows, flat_traces, (((1,), (1,)), ((), ())), preferred_element_type=jnp.float32
    )
    term = term.reshape(NF, 2, shot_dev, receivers)
    core = lax.axis_index("freq")
    mine = lax.dynamic_slice_in_dim(term, core * local_bins, local_bins, axis=0)
    theirs = lax.dynamic_slice_in_dim(term, (1 - core) * local_bins, local_bins, axis=0)
    theirs = lax.ppermute(theirs, "freq", [(0, 1), (1, 0)])
    spectra = (mine + theirs).astype(jnp.bfloat16)
    rows = local_bins * 2 * shot_dev
    near = spectra.reshape(rows, groups, receiver_dev).transpose(1, 0, 2).reshape(groups, rows * receiver_dev)
    stations = jnp.concatenate(
        [spectra[:, :, :, 0 :: 2 * stride], spectra[:, :, :, stride :: 2 * stride]], axis=-1
    ).reshape(1, rows * shots)
    lanes = 128
    outgoing = jnp.concatenate(
        [
            near.reshape(groups, rows * receiver_dev // lanes, lanes).transpose(1, 0, 2),
            jnp.broadcast_to(stations.reshape(rows * shots // lanes, 1, lanes), (rows * shots // lanes, groups, lanes)),
        ],
        axis=0,
    )
    outgoing, aperture, lengths = lax.optimization_barrier((outgoing, aperture, lengths))
    incoming = lax.all_to_all(outgoing, "shot", 1, 1, tiled=True)
    used = jnp.arange(KMAX, dtype=jnp.int32)[None, None, :] < lengths[:, :, None]
    codes = jnp.where(used, (aperture % shot_dev) * groups + aperture // shot_dev, -1)
    codes = codes.reshape(groups, shot_dev, receiver_dev, KMAX).transpose(1, 2, 0, 3)
    counts = jnp.sum(
        (codes[..., None] == jnp.arange(shots, dtype=jnp.int32)).astype(jnp.float32), axis=3
    )
    kernel = functools.partial(
        multiply_kernel, local_bins=local_bins, shot_dev=shot_dev, receiver_dev=receiver_dev, groups=groups
    )
    back = pl.pallas_call(
        kernel,
        out_shape=jax.ShapeDtypeStruct((groups, rows * receiver_dev), jnp.bfloat16),
        in_specs=[pl.BlockSpec(memory_space=pltpu.VMEM)] * 2,
        out_specs=pl.BlockSpec(memory_space=pltpu.VMEM),
        scratch_shapes=[
            pltpu.VMEM((rows * receiver_dev, groups), jnp.float32),
            pltpu.VMEM((groups, rows * receiver_dev), jnp.float32),
            pltpu.VMEM((groups, rows * receiver_dev), jnp.float32),
            pltpu.SemaphoreType.DMA((2,)),
        ],
        compiler_params=pltpu.CompilerParams(has_side_effects=True),
        cost_estimate=pl.CostEstimate(
            flops=16 * groups * shots * rows * receiver_dev // 2, transcendentals=0, bytes_accessed=4 * 1024 * 1024
        ),
    )(incoming, counts)
    piece = lax.all_gather(back, "freq", axis=0, tiled=False)
    piece = piece.reshape(freq_dev, groups, local_bins, 2, shot_dev, receiver_dev)
    piece = piece.transpose(4, 1, 5, 0, 2, 3).reshape(shot_dev, receivers, NF * 2)
    wide = time_dev + 2 * half_taps
    wide_times = start_time - half_taps + jnp.arange(wide, dtype=jnp.int32)
    inside = (wide_times >= 0) & (wide_times < NT)
    phases = frequency_bins[:, None] * jnp.clip(wide_times, 0, NT - 1)[None, :] % NT
    angles = phases.astype(jnp.float32) * (2.0 * math.pi / NT)
    wide_rows = jnp.stack([jnp.cos(angles), -jnp.sin(angles)], axis=1).astype(jnp.bfloat16)
    wide_rows = jnp.where(inside[None, None, :], wide_rows.astype(jnp.float32), 0.0).reshape(NF * 2, wide)
    taps = filters.astype(jnp.float32)
    shaped = sum(
        taps[:, tap, None, None] * wide_rows[None, :, 2 * half_taps - tap : 2 * half_taps - tap + time_dev]
        for tap in range(TAPS)
    )
    leading = shaped.astype(jnp.bfloat16)
    trailing = (shaped - leading.astype(jnp.float32)).astype(jnp.bfloat16)
    filtered = lax.dot_general(
        jnp.concatenate([piece, piece], axis=2),
        jnp.concatenate([leading, trailing], axis=1),
        (((2,), (1,)), ((0,), (0,))),
        preferred_element_type=jnp.float32,
    )
    return filtered.astype(jnp.bfloat16)


def solution(mesh):
    in_specs = (
        P("shot", None, "freq"),
        P(),
        P(None, "shot", None),
        P(None, "shot"),
        P("shot", None),
    )
    out_specs = P("shot", None, "freq")
    return jax.shard_map(shards, mesh=mesh, in_specs=in_specs, out_specs=out_specs, check_vma=False)
```

```python
import functools
import math

import jax
import jax.numpy as jnp
from jax import lax
from jax.experimental import pallas as pl
from jax.experimental.pallas import tpu as pltpu
from jax.sharding import PartitionSpec as P

NT = 1024
NF = 8
KMAX = 32
TAPS = 31


def extended(shard, sides, width):
    for axis, dim in sides:
        devices, length = (lax.axis_size(axis), shard.shape[dim])
        up = [(i, (i + 1) % devices) for i in range(devices - 1)]
        down = [(j, i) for i, j in up]
        last = lax.slice_in_dim(shard, length - width, length, axis=dim)
        leading = lax.slice_in_dim(shard, 0, width, axis=dim)
        before = lax.ppermute(last, axis, up)
        after = lax.ppermute(leading, axis, down)
        shard = jnp.concatenate([before, shard, after], axis=dim)
    return shard


def fourier_rows(bin_rows, first_time, sample_count, period):
    sample_times = first_time + jnp.arange(sample_count, dtype=jnp.int32)
    phases = bin_rows[:, None] * sample_times[None, :] % period
    angles = phases.astype(jnp.float32) * (2.0 * math.pi / period)
    return (jnp.cos(angles), jnp.sin(angles))


def multiply_kernel(
    incoming_ref, counts_ref, out_ref, qt_ref, acc_ref, recv_ref, sems, *, local_bins, shot_dev, receiver_dev, groups
):
    qt_ref[...] = incoming_ref[0].astype(jnp.float32).T
    me = lax.axis_index("shot")
    half = lax.axis_index("freq")
    block = 32

    steps = groups // block

    def remote_send(target):
        pltpu.make_async_remote_copy(
            src_ref=acc_ref.at[pl.ds(target, 1)],
            dst_ref=recv_ref.at[pl.ds(me, 1)],
            send_sem=sems.at[0],
            recv_sem=sems.at[1],
            device_id=(target, half),
            device_id_type=pl.DeviceIdType.MESH,
        ).start()

    def compute(top):
        rows = pl.ds(top, block)
        for i in range(shot_dev):
            for r in range(receiver_dev):
                weights = [counts_ref[i, r, rows, h * groups : (h + 1) * groups] for h in range(shot_dev)]
                for f in range(local_bins):
                    real_sum = None
                    imag_sum = None
                    for h in range(shot_dev):
                        slab_r = 1 + ((f * 2 + 0) * shot_dev + i) * shot_dev + h
                        slab_i = 1 + ((f * 2 + 1) * shot_dev + i) * shot_dev + h
                        pr = incoming_ref[slab_r, rows, :].astype(jnp.float32)
                        pi = incoming_ref[slab_i, rows, :].astype(jnp.float32)
                        row_r = ((f * 2 + 0) * shot_dev + h) * receiver_dev + r
                        row_i = ((f * 2 + 1) * shot_dev + h) * receiver_dev + r
                        qr = qt_ref[row_r : row_r + 1, :]
                        qi = qt_ref[row_i : row_i + 1, :]
                        w = weights[h]
                        real_term = w * (pr * qr - pi * qi)
                        imag_term = w * (pr * qi + pi * qr)
                        real_sum = real_term if real_sum is None else real_sum + real_term
                        imag_sum = imag_term if imag_sum is None else imag_sum + imag_term
                    col_r = ((f * 2 + 0) * shot_dev + i) * receiver_dev + r
                    col_i = ((f * 2 + 1) * shot_dev + i) * receiver_dev + r
                    acc_ref[rows, col_r : col_r + 1] = jnp.sum(real_sum, axis=1, keepdims=True)
                    acc_ref[rows, col_i : col_i + 1] = jnp.sum(imag_sum, axis=1, keepdims=True)
        acc_ref[rows, :] = (acc_ref[rows, :] * KMAX ** (-0.5)).astype(jnp.bfloat16).astype(jnp.float32)

    own_block = me // block
    own_top = pl.multiple_of(own_block * block, block)
    compute(own_top)
    for t in range(block):
        target = own_top + lax.rem(me + t, block)

        @pl.when(target != me)
        def _():
            remote_send(target)

    recv_ref[pl.ds(me, 1), :] = acc_ref[pl.ds(me, 1), :]

    def chunk(step, carry):
        top = pl.multiple_of(lax.rem(own_block + step, steps) * block, block)
        compute(top)
        for t in range(block):
            remote_send(top + lax.rem(me + t, block))
        return carry

    lax.fori_loop(1, steps, chunk, 0)
    every = pltpu.make_async_remote_copy(
        src_ref=acc_ref.at[pl.ds(0, groups - 1)],
        dst_ref=recv_ref.at[pl.ds(0, groups - 1)],
        send_sem=sems.at[0],
        recv_sem=sems.at[1],
        device_id=(me, half),
        device_id_type=pl.DeviceIdType.MESH,
    )
    every.wait_send()
    every.wait_recv()
    out_ref[...] = recv_ref[...].astype(out_ref.dtype)


def shards(traces, frequency_bins, aperture, lengths, filters):
    shot_dev, receivers, time_dev = traces.shape
    groups = lax.axis_size("shot")
    shots = shot_dev * groups
    receiver_dev = receivers // groups
    stride = receivers // shots
    freq_dev = lax.axis_size("freq")
    local_bins = NF // freq_dev
    start_time = lax.axis_index("freq") * time_dev
    half_taps = (TAPS - 1) // 2
    flat_traces = traces.reshape(shot_dev * receivers, time_dev)
    cosines, sines = fourier_rows(frequency_bins, start_time, time_dev, NT)
    basis_rows = (jnp.stack([cosines, -sines], axis=1) * NT ** (-0.5)).astype(jnp.bfloat16)
    basis_rows = basis_rows.reshape(NF * 2, time_dev)
    term = lax.dot_general(
        basis_rows, flat_traces, (((1,), (1,)), ((), ())), preferred_element_type=jnp.float32
    )
    term = term.reshape(NF, 2, shot_dev, receivers)
    core = lax.axis_index("freq")
    mine = lax.dynamic_slice_in_dim(term, core * local_bins, local_bins, axis=0)
    theirs = lax.dynamic_slice_in_dim(term, (1 - core) * local_bins, local_bins, axis=0)
    theirs = lax.ppermute(theirs, "freq", [(0, 1), (1, 0)])
    spectra = (mine + theirs).astype(jnp.bfloat16)
    rows = local_bins * 2 * shot_dev
    near = spectra.reshape(rows, groups, receiver_dev).transpose(1, 0, 2).reshape(groups, rows * receiver_dev)
    stations = jnp.concatenate(
        [spectra[:, :, :, 0 :: 2 * stride], spectra[:, :, :, stride :: 2 * stride]], axis=-1
    ).reshape(1, rows * shots)
    lanes = 128
    outgoing = jnp.concatenate(
        [
            near.reshape(groups, rows * receiver_dev // lanes, lanes).transpose(1, 0, 2),
            jnp.broadcast_to(stations.reshape(rows * shots // lanes, 1, lanes), (rows * shots // lanes, groups, lanes)),
        ],
        axis=0,
    )
    outgoing, aperture, lengths = lax.optimization_barrier((outgoing, aperture, lengths))
    incoming = lax.all_to_all(outgoing, "shot", 1, 1, tiled=True)
    used = jnp.arange(KMAX, dtype=jnp.int32)[None, None, :] < lengths[:, :, None]
    codes = jnp.where(used, (aperture % shot_dev) * groups + aperture // shot_dev, -1)
    codes = codes.reshape(groups, shot_dev, receiver_dev, KMAX).transpose(1, 2, 0, 3)
    counts = jnp.sum(
        (codes[..., None] == jnp.arange(shots, dtype=jnp.int32)).astype(jnp.float32), axis=3
    )
    kernel = functools.partial(
        multiply_kernel, local_bins=local_bins, shot_dev=shot_dev, receiver_dev=receiver_dev, groups=groups
    )
    back = pl.pallas_call(
        kernel,
        out_shape=jax.ShapeDtypeStruct((groups, rows * receiver_dev), jnp.bfloat16),
        in_specs=[pl.BlockSpec(memory_space=pltpu.VMEM)] * 2,
        out_specs=pl.BlockSpec(memory_space=pltpu.VMEM),
        scratch_shapes=[
            pltpu.VMEM((rows * receiver_dev, groups), jnp.float32),
            pltpu.VMEM((groups, rows * receiver_dev), jnp.float32),
            pltpu.VMEM((groups, rows * receiver_dev), jnp.float32),
            pltpu.SemaphoreType.DMA((2,)),
        ],
        compiler_params=pltpu.CompilerParams(has_side_effects=True),
        cost_estimate=pl.CostEstimate(
            flops=16 * groups * shots * rows * receiver_dev // 2, transcendentals=0, bytes_accessed=4 * 1024 * 1024
        ),
    )(incoming, counts)
    piece = lax.all_gather(back, "freq", axis=0, tiled=False)
    piece = piece.reshape(freq_dev, groups, local_bins, 2, shot_dev, receiver_dev)
    piece = piece.transpose(4, 1, 5, 0, 2, 3).reshape(shot_dev, receivers, NF * 2)
    wide = time_dev + 2 * half_taps
    wide_times = start_time - half_taps + jnp.arange(wide, dtype=jnp.int32)
    inside = (wide_times >= 0) & (wide_times < NT)
    phases = frequency_bins[:, None] * jnp.clip(wide_times, 0, NT - 1)[None, :] % NT
    angles = phases.astype(jnp.float32) * (2.0 * math.pi / NT)
    wide_rows = jnp.stack([jnp.cos(angles), -jnp.sin(angles)], axis=1).astype(jnp.bfloat16)
    wide_rows = jnp.where(inside[None, None, :], wide_rows.astype(jnp.float32), 0.0).reshape(NF * 2, wide)
    taps = filters.astype(jnp.float32)
    shaped = sum(
        taps[:, tap, None, None] * wide_rows[None, :, 2 * half_taps - tap : 2 * half_taps - tap + time_dev]
        for tap in range(TAPS)
    )
    leading = shaped.astype(jnp.bfloat16)
    trailing = (shaped - leading.astype(jnp.float32)).astype(jnp.bfloat16)
    filtered = lax.dot_general(
        jnp.concatenate([piece, piece], axis=2),
        jnp.concatenate([leading, trailing], axis=1),
        (((2,), (1,)), ((0,), (0,))),
        preferred_element_type=jnp.float32,
    )
    return filtered.astype(jnp.bfloat16)


def solution(mesh):
    in_specs = (
        P("shot", None, "freq"),
        P(),
        P(None, "shot", None),
        P(None, "shot"),
        P("shot", None),
    )
    out_specs = P("shot", None, "freq")
    return jax.shard_map(shards, mesh=mesh, in_specs=in_specs, out_specs=out_specs, check_vma=False)
```

```python
import functools
import math

import jax
import jax.numpy as jnp
from jax import lax
from jax.experimental import pallas as pl
from jax.experimental.pallas import tpu as pltpu
from jax.sharding import PartitionSpec as P

NT = 1024
NF = 8
KMAX = 32
TAPS = 31


def extended(shard, sides, width):
    for axis, dim in sides:
        devices, length = (lax.axis_size(axis), shard.shape[dim])
        up = [(i, (i + 1) % devices) for i in range(devices - 1)]
        down = [(j, i) for i, j in up]
        last = lax.slice_in_dim(shard, length - width, length, axis=dim)
        leading = lax.slice_in_dim(shard, 0, width, axis=dim)
        before = lax.ppermute(last, axis, up)
        after = lax.ppermute(leading, axis, down)
        shard = jnp.concatenate([before, shard, after], axis=dim)
    return shard


def fourier_rows(bin_rows, first_time, sample_count, period):
    sample_times = first_time + jnp.arange(sample_count, dtype=jnp.int32)
    phases = bin_rows[:, None] * sample_times[None, :] % period
    angles = phases.astype(jnp.float32) * (2.0 * math.pi / period)
    return (jnp.cos(angles), jnp.sin(angles))


def multiply_kernel(
    incoming_ref, counts_ref, out_ref, qt_ref, acc_ref, recv_ref, sems, *, local_bins, shot_dev, receiver_dev, groups
):
    qt_ref[...] = incoming_ref[0].astype(jnp.float32).T
    me = lax.axis_index("shot")
    half = lax.axis_index("freq")
    block = 8

    steps = groups // block

    def remote_send(target):
        pltpu.make_async_remote_copy(
            src_ref=acc_ref.at[pl.ds(target, 1)],
            dst_ref=recv_ref.at[pl.ds(me, 1)],
            send_sem=sems.at[0],
            recv_sem=sems.at[1],
            device_id=(target, half),
            device_id_type=pl.DeviceIdType.MESH,
        ).start()

    def compute(top):
        rows = pl.ds(top, block)
        for i in range(shot_dev):
            for r in range(receiver_dev):
                weights = [counts_ref[i, r, rows, h * groups : (h + 1) * groups] for h in range(shot_dev)]
                for f in range(local_bins):
                    real_sum = None
                    imag_sum = None
                    for h in range(shot_dev):
                        slab_r = 1 + ((f * 2 + 0) * shot_dev + i) * shot_dev + h
                        slab_i = 1 + ((f * 2 + 1) * shot_dev + i) * shot_dev + h
                        pr = incoming_ref[slab_r, rows, :].astype(jnp.float32)
                        pi = incoming_ref[slab_i, rows, :].astype(jnp.float32)
                        row_r = ((f * 2 + 0) * shot_dev + h) * receiver_dev + r
                        row_i = ((f * 2 + 1) * shot_dev + h) * receiver_dev + r
                        qr = qt_ref[row_r : row_r + 1, :]
                        qi = qt_ref[row_i : row_i + 1, :]
                        w = weights[h]
                        real_term = w * (pr * qr - pi * qi)
                        imag_term = w * (pr * qi + pi * qr)
                        real_sum = real_term if real_sum is None else real_sum + real_term
                        imag_sum = imag_term if imag_sum is None else imag_sum + imag_term
                    col_r = ((f * 2 + 0) * shot_dev + i) * receiver_dev + r
                    col_i = ((f * 2 + 1) * shot_dev + i) * receiver_dev + r
                    acc_ref[rows, col_r : col_r + 1] = jnp.sum(real_sum, axis=1, keepdims=True)
                    acc_ref[rows, col_i : col_i + 1] = jnp.sum(imag_sum, axis=1, keepdims=True)
        acc_ref[rows, :] = (acc_ref[rows, :] * KMAX ** (-0.5)).astype(jnp.bfloat16).astype(jnp.float32)

    own_block = me // block
    own_top = pl.multiple_of(own_block * block, block)
    compute(own_top)
    for t in range(block):
        target = own_top + lax.rem(me + t, block)

        @pl.when(target != me)
        def _():
            remote_send(target)

    recv_ref[pl.ds(me, 1), :] = acc_ref[pl.ds(me, 1), :]

    def chunk(step, carry):
        top = pl.multiple_of(lax.rem(own_block + step, steps) * block, block)
        compute(top)
        for t in range(block):
            remote_send(top + lax.rem(me + t, block))
        return carry

    lax.fori_loop(1, steps, chunk, 0)
    every = pltpu.make_async_remote_copy(
        src_ref=acc_ref.at[pl.ds(0, groups - 1)],
        dst_ref=recv_ref.at[pl.ds(0, groups - 1)],
        send_sem=sems.at[0],
        recv_sem=sems.at[1],
        device_id=(me, half),
        device_id_type=pl.DeviceIdType.MESH,
    )
    every.wait_send()
    every.wait_recv()
    out_ref[...] = recv_ref[...].astype(out_ref.dtype)


def shards(traces, frequency_bins, aperture, lengths, filters):
    shot_dev, receivers, time_dev = traces.shape
    groups = lax.axis_size("shot")
    shots = shot_dev * groups
    receiver_dev = receivers // groups
    stride = receivers // shots
    freq_dev = lax.axis_size("freq")
    local_bins = NF // freq_dev
    start_time = lax.axis_index("freq") * time_dev
    half_taps = (TAPS - 1) // 2
    flat_traces = traces.reshape(shot_dev * receivers, time_dev)
    cosines, sines = fourier_rows(frequency_bins, start_time, time_dev, NT)
    basis_rows = (jnp.stack([cosines, -sines], axis=1) * NT ** (-0.5)).astype(jnp.bfloat16)
    basis_rows = basis_rows.reshape(NF * 2, time_dev)
    term = lax.dot_general(
        basis_rows, flat_traces, (((1,), (1,)), ((), ())), preferred_element_type=jnp.float32
    )
    term = term.reshape(NF, 2, shot_dev, receivers)
    core = lax.axis_index("freq")
    mine = lax.dynamic_slice_in_dim(term, core * local_bins, local_bins, axis=0)
    theirs = lax.dynamic_slice_in_dim(term, (1 - core) * local_bins, local_bins, axis=0)
    theirs = lax.ppermute(theirs, "freq", [(0, 1), (1, 0)])
    spectra = (mine + theirs).astype(jnp.bfloat16)
    rows = local_bins * 2 * shot_dev
    near = spectra.reshape(rows, groups, receiver_dev).transpose(1, 0, 2).reshape(groups, rows * receiver_dev)
    stations = jnp.concatenate(
        [spectra[:, :, :, 0 :: 2 * stride], spectra[:, :, :, stride :: 2 * stride]], axis=-1
    ).reshape(1, rows * shots)
    lanes = 128
    outgoing = jnp.concatenate(
        [
            near.reshape(groups, rows * receiver_dev // lanes, lanes).transpose(1, 0, 2),
            jnp.broadcast_to(stations.reshape(rows * shots // lanes, 1, lanes), (rows * shots // lanes, groups, lanes)),
        ],
        axis=0,
    )
    outgoing, aperture, lengths = lax.optimization_barrier((outgoing, aperture, lengths))
    incoming = lax.all_to_all(outgoing, "shot", 1, 1, tiled=True)
    used = jnp.arange(KMAX, dtype=jnp.int32)[None, None, :] < lengths[:, :, None]
    codes = jnp.where(used, (aperture % shot_dev) * groups + aperture // shot_dev, -1)
    codes = codes.reshape(groups, shot_dev, receiver_dev, KMAX).transpose(1, 2, 0, 3)
    counts = jnp.sum(
        (codes[..., None] == jnp.arange(shots, dtype=jnp.int32)).astype(jnp.float32), axis=3
    )
    kernel = functools.partial(
        multiply_kernel, local_bins=local_bins, shot_dev=shot_dev, receiver_dev=receiver_dev, groups=groups
    )
    back = pl.pallas_call(
        kernel,
        out_shape=jax.ShapeDtypeStruct((groups, rows * receiver_dev), jnp.bfloat16),
        in_specs=[pl.BlockSpec(memory_space=pltpu.VMEM)] * 2,
        out_specs=pl.BlockSpec(memory_space=pltpu.VMEM),
        scratch_shapes=[
            pltpu.VMEM((rows * receiver_dev, groups), jnp.float32),
            pltpu.VMEM((groups, rows * receiver_dev), jnp.float32),
            pltpu.VMEM((groups, rows * receiver_dev), jnp.float32),
            pltpu.SemaphoreType.DMA((2,)),
        ],
        compiler_params=pltpu.CompilerParams(has_side_effects=True),
        cost_estimate=pl.CostEstimate(
            flops=16 * groups * shots * rows * receiver_dev // 2, transcendentals=0, bytes_accessed=4 * 1024 * 1024
        ),
    )(incoming, counts)
    piece = lax.all_gather(back, "freq", axis=0, tiled=False)
    piece = piece.reshape(freq_dev, groups, local_bins, 2, shot_dev, receiver_dev)
    piece = piece.transpose(4, 1, 5, 0, 2, 3).reshape(shot_dev, receivers, NF * 2)
    wide = time_dev + 2 * half_taps
    wide_times = start_time - half_taps + jnp.arange(wide, dtype=jnp.int32)
    inside = (wide_times >= 0) & (wide_times < NT)
    phases = frequency_bins[:, None] * jnp.clip(wide_times, 0, NT - 1)[None, :] % NT
    angles = phases.astype(jnp.float32) * (2.0 * math.pi / NT)
    wide_rows = jnp.stack([jnp.cos(angles), -jnp.sin(angles)], axis=1).astype(jnp.bfloat16)
    wide_rows = jnp.where(inside[None, None, :], wide_rows.astype(jnp.float32), 0.0).reshape(NF * 2, wide)
    taps = filters.astype(jnp.float32)
    shaped = sum(
        taps[:, tap, None, None] * wide_rows[None, :, 2 * half_taps - tap : 2 * half_taps - tap + time_dev]
        for tap in range(TAPS)
    )
    leading = shaped.astype(jnp.bfloat16)
    trailing = (shaped - leading.astype(jnp.float32)).astype(jnp.bfloat16)
    filtered = lax.dot_general(
        jnp.concatenate([piece, piece], axis=2),
        jnp.concatenate([leading, trailing], axis=1),
        (((2,), (1,)), ((0,), (0,))),
        preferred_element_type=jnp.float32,
    )
    return filtered.astype(jnp.bfloat16)


def solution(mesh):
    in_specs = (
        P("shot", None, "freq"),
        P(),
        P(None, "shot", None),
        P(None, "shot"),
        P("shot", None),
    )
    out_specs = P("shot", None, "freq")
    return jax.shard_map(shards, mesh=mesh, in_specs=in_specs, out_specs=out_specs, check_vma=False)
```

```python
import functools
import math

import jax
import jax.numpy as jnp
from jax import lax
from jax.experimental import pallas as pl
from jax.experimental.pallas import tpu as pltpu
from jax.sharding import PartitionSpec as P

NT = 1024
NF = 8
KMAX = 32
TAPS = 31


def extended(shard, sides, width):
    for axis, dim in sides:
        devices, length = (lax.axis_size(axis), shard.shape[dim])
        up = [(i, (i + 1) % devices) for i in range(devices - 1)]
        down = [(j, i) for i, j in up]
        last = lax.slice_in_dim(shard, length - width, length, axis=dim)
        leading = lax.slice_in_dim(shard, 0, width, axis=dim)
        before = lax.ppermute(last, axis, up)
        after = lax.ppermute(leading, axis, down)
        shard = jnp.concatenate([before, shard, after], axis=dim)
    return shard


def fourier_rows(bin_rows, first_time, sample_count, period):
    sample_times = first_time + jnp.arange(sample_count, dtype=jnp.int32)
    phases = bin_rows[:, None] * sample_times[None, :] % period
    angles = phases.astype(jnp.float32) * (2.0 * math.pi / period)
    return (jnp.cos(angles), jnp.sin(angles))


def multiply_kernel(
    incoming_ref, counts_ref, out_ref, qt_ref, acc_ref, recv_ref, sems, *, local_bins, shot_dev, receiver_dev, groups
):
    qt_ref[...] = incoming_ref[0].astype(jnp.float32).T
    me = lax.axis_index("shot")
    half = lax.axis_index("freq")
    block = 8

    steps = groups // block

    def remote_send(target):
        pltpu.make_async_remote_copy(
            src_ref=acc_ref.at[pl.ds(target, 1)],
            dst_ref=recv_ref.at[pl.ds(me, 1)],
            send_sem=sems.at[0],
            recv_sem=sems.at[1],
            device_id=(target, half),
            device_id_type=pl.DeviceIdType.MESH,
        ).start()

    def compute(top):
        rows = pl.ds(top, block)
        for i in range(shot_dev):
            for r in range(receiver_dev):
                weights = [counts_ref[i, r, rows, h * groups : (h + 1) * groups] for h in range(shot_dev)]
                for f in range(local_bins):
                    real_sum = None
                    imag_sum = None
                    for h in range(shot_dev):
                        slab_r = 1 + ((f * 2 + 0) * shot_dev + i) * shot_dev + h
                        slab_i = 1 + ((f * 2 + 1) * shot_dev + i) * shot_dev + h
                        pr = incoming_ref[slab_r, rows, :].astype(jnp.float32)
                        pi = incoming_ref[slab_i, rows, :].astype(jnp.float32)
                        row_r = ((f * 2 + 0) * shot_dev + h) * receiver_dev + r
                        row_i = ((f * 2 + 1) * shot_dev + h) * receiver_dev + r
                        qr = qt_ref[row_r : row_r + 1, :]
                        qi = qt_ref[row_i : row_i + 1, :]
                        w = weights[h]
                        real_term = w * (pr * qr - pi * qi)
                        imag_term = w * (pr * qi + pi * qr)
                        real_sum = real_term if real_sum is None else real_sum + real_term
                        imag_sum = imag_term if imag_sum is None else imag_sum + imag_term
                    col_r = ((f * 2 + 0) * shot_dev + i) * receiver_dev + r
                    col_i = ((f * 2 + 1) * shot_dev + i) * receiver_dev + r
                    acc_ref[rows, col_r : col_r + 1] = jnp.sum(real_sum, axis=1, keepdims=True)
                    acc_ref[rows, col_i : col_i + 1] = jnp.sum(imag_sum, axis=1, keepdims=True)
        acc_ref[rows, :] = (acc_ref[rows, :] * KMAX ** (-0.5)).astype(jnp.bfloat16).astype(jnp.float32)

    own_block = me // block
    own_top = pl.multiple_of(own_block * block, block)
    compute(own_top)
    for t in range(block):
        target = own_top + lax.rem(me + t, block)

        @pl.when(target != me)
        def _():
            remote_send(target)

    recv_ref[pl.ds(me, 1), :] = acc_ref[pl.ds(me, 1), :]

    def chunk(step, carry):
        top = pl.multiple_of(lax.rem(own_block + step, steps) * block, block)
        compute(top)
        for t in range(block):
            remote_send(top + lax.rem(me + t, block))
        return carry

    lax.fori_loop(1, steps, chunk, 0)
    every = pltpu.make_async_remote_copy(
        src_ref=acc_ref.at[pl.ds(0, groups - 1)],
        dst_ref=recv_ref.at[pl.ds(0, groups - 1)],
        send_sem=sems.at[0],
        recv_sem=sems.at[1],
        device_id=(me, half),
        device_id_type=pl.DeviceIdType.MESH,
    )
    every.wait_send()
    every.wait_recv()
    out_ref[...] = recv_ref[...].astype(out_ref.dtype)


def shards(traces, frequency_bins, aperture, lengths, filters):
    shot_dev, receivers, time_dev = traces.shape
    groups = lax.axis_size("shot")
    shots = shot_dev * groups
    receiver_dev = receivers // groups
    stride = receivers // shots
    freq_dev = lax.axis_size("freq")
    local_bins = NF // freq_dev
    start_time = lax.axis_index("freq") * time_dev
    half_taps = (TAPS - 1) // 2
    flat_traces = traces.reshape(shot_dev * receivers, time_dev)
    cosines, sines = fourier_rows(frequency_bins, start_time, time_dev, NT)
    basis_rows = (jnp.stack([cosines, -sines], axis=1) * NT ** (-0.5)).astype(jnp.bfloat16)
    basis_rows = basis_rows.reshape(NF * 2, time_dev)
    term = lax.dot_general(
        basis_rows, flat_traces, (((1,), (1,)), ((), ())), preferred_element_type=jnp.float32
    )
    term = term.reshape(NF, 2, shot_dev, receivers)
    core = lax.axis_index("freq")
    mine = lax.dynamic_slice_in_dim(term, core * local_bins, local_bins, axis=0)
    theirs = lax.dynamic_slice_in_dim(term, (1 - core) * local_bins, local_bins, axis=0)
    theirs = lax.ppermute(theirs, "freq", [(0, 1), (1, 0)])
    spectra = (mine + theirs).astype(jnp.bfloat16)
    rows = local_bins * 2 * shot_dev
    near = spectra.reshape(rows, groups, receiver_dev).transpose(1, 0, 2).reshape(groups, rows * receiver_dev)
    stations = jnp.concatenate(
        [spectra[:, :, :, 0 :: 2 * stride], spectra[:, :, :, stride :: 2 * stride]], axis=-1
    ).reshape(1, rows * shots)
    lanes = 128
    outgoing = jnp.concatenate(
        [
            near.reshape(groups, rows * receiver_dev // lanes, lanes).transpose(1, 0, 2),
            jnp.broadcast_to(stations.reshape(rows * shots // lanes, 1, lanes), (rows * shots // lanes, groups, lanes)),
        ],
        axis=0,
    )
    outgoing, aperture, lengths = lax.optimization_barrier((outgoing, aperture, lengths))
    incoming = lax.all_to_all(outgoing, "shot", 1, 1, tiled=True)
    used = jnp.arange(KMAX, dtype=jnp.int32)[None, None, :] < lengths[:, :, None]
    codes = jnp.where(used, (aperture % shot_dev) * groups + aperture // shot_dev, -1)
    codes = codes.reshape(groups, shot_dev, receiver_dev, KMAX).transpose(1, 2, 0, 3)
    counts = jnp.sum(
        (codes[..., None] == jnp.arange(shots, dtype=jnp.int32)).astype(jnp.float32), axis=3
    )
    kernel = functools.partial(
        multiply_kernel, local_bins=local_bins, shot_dev=shot_dev, receiver_dev=receiver_dev, groups=groups
    )
    back = pl.pallas_call(
        kernel,
        out_shape=jax.ShapeDtypeStruct((groups, rows * receiver_dev), jnp.bfloat16),
        in_specs=[pl.BlockSpec(memory_space=pltpu.VMEM)] * 2,
        out_specs=pl.BlockSpec(memory_space=pltpu.VMEM),
        scratch_shapes=[
            pltpu.VMEM((rows * receiver_dev, groups), jnp.float32),
            pltpu.VMEM((groups, rows * receiver_dev), jnp.float32),
            pltpu.VMEM((groups, rows * receiver_dev), jnp.float32),
            pltpu.SemaphoreType.DMA((2,)),
        ],
        compiler_params=pltpu.CompilerParams(has_side_effects=True),
        cost_estimate=pl.CostEstimate(
            flops=16 * groups * shots * rows * receiver_dev // 2, transcendentals=0, bytes_accessed=4 * 1024 * 1024
        ),
    )(incoming, counts)
    other = lax.ppermute(back, "freq", [(0, 1), (1, 0)])
    piece = jnp.where(core == 0, jnp.stack([back, other]), jnp.stack([other, back]))
    piece = piece.reshape(freq_dev, groups, local_bins, 2, shot_dev, receiver_dev)
    piece = piece.transpose(4, 1, 5, 0, 2, 3).reshape(shot_dev, receivers, NF * 2)
    wide = time_dev + 2 * half_taps
    wide_times = start_time - half_taps + jnp.arange(wide, dtype=jnp.int32)
    inside = (wide_times >= 0) & (wide_times < NT)
    phases = frequency_bins[:, None] * jnp.clip(wide_times, 0, NT - 1)[None, :] % NT
    angles = phases.astype(jnp.float32) * (2.0 * math.pi / NT)
    wide_rows = jnp.stack([jnp.cos(angles), -jnp.sin(angles)], axis=1).astype(jnp.bfloat16)
    wide_rows = jnp.where(inside[None, None, :], wide_rows.astype(jnp.float32), 0.0).reshape(NF * 2, wide)
    taps = filters.astype(jnp.float32)
    shaped = sum(
        taps[:, tap, None, None] * wide_rows[None, :, 2 * half_taps - tap : 2 * half_taps - tap + time_dev]
        for tap in range(TAPS)
    )
    leading = shaped.astype(jnp.bfloat16)
    trailing = (shaped - leading.astype(jnp.float32)).astype(jnp.bfloat16)
    filtered = lax.dot_general(
        jnp.concatenate([piece, piece], axis=2),
        jnp.concatenate([leading, trailing], axis=1),
        (((2,), (1,)), ((0,), (0,))),
        preferred_element_type=jnp.float32,
    )
    return filtered.astype(jnp.bfloat16)


def solution(mesh):
    in_specs = (
        P("shot", None, "freq"),
        P(),
        P(None, "shot", None),
        P(None, "shot"),
        P("shot", None),
    )
    out_specs = P("shot", None, "freq")
    return jax.shard_map(shards, mesh=mesh, in_specs=in_specs, out_specs=out_specs, check_vma=False)
```

```python
import functools
import math

import jax
import jax.numpy as jnp
from jax import lax
from jax.experimental import pallas as pl
from jax.experimental.pallas import tpu as pltpu
from jax.sharding import PartitionSpec as P

NT = 1024
NF = 8
KMAX = 32
TAPS = 31


def extended(shard, sides, width):
    for axis, dim in sides:
        devices, length = (lax.axis_size(axis), shard.shape[dim])
        up = [(i, (i + 1) % devices) for i in range(devices - 1)]
        down = [(j, i) for i, j in up]
        last = lax.slice_in_dim(shard, length - width, length, axis=dim)
        leading = lax.slice_in_dim(shard, 0, width, axis=dim)
        before = lax.ppermute(last, axis, up)
        after = lax.ppermute(leading, axis, down)
        shard = jnp.concatenate([before, shard, after], axis=dim)
    return shard


def fourier_rows(bin_rows, first_time, sample_count, period):
    sample_times = first_time + jnp.arange(sample_count, dtype=jnp.int32)
    phases = bin_rows[:, None] * sample_times[None, :] % period
    angles = phases.astype(jnp.float32) * (2.0 * math.pi / period)
    return (jnp.cos(angles), jnp.sin(angles))


def multiply_kernel(
    incoming_ref, counts_ref, out_ref, qt_ref, acc_ref, recv_ref, sems, *, local_bins, shot_dev, receiver_dev, groups
):
    qt_ref[...] = incoming_ref[0].astype(jnp.float32).T
    me = lax.axis_index("shot")
    half = lax.axis_index("freq")
    block = 8

    steps = groups // block

    def remote_send(target):
        pltpu.make_async_remote_copy(
            src_ref=acc_ref.at[pl.ds(target, 1)],
            dst_ref=recv_ref.at[pl.ds(me, 1)],
            send_sem=sems.at[0],
            recv_sem=sems.at[1],
            device_id=(target, half),
            device_id_type=pl.DeviceIdType.MESH,
        ).start()

    def compute(top):
        rows = pl.ds(top, block)
        for i in range(shot_dev):
            for r in range(receiver_dev):
                weights = [
                    counts_ref[i, r, rows, h * groups : (h + 1) * groups].astype(jnp.float32) for h in range(shot_dev)
                ]
                for f in range(local_bins):
                    real_sum = None
                    imag_sum = None
                    for h in range(shot_dev):
                        slab_r = 1 + ((f * 2 + 0) * shot_dev + i) * shot_dev + h
                        slab_i = 1 + ((f * 2 + 1) * shot_dev + i) * shot_dev + h
                        pr = incoming_ref[slab_r, rows, :].astype(jnp.float32)
                        pi = incoming_ref[slab_i, rows, :].astype(jnp.float32)
                        row_r = ((f * 2 + 0) * shot_dev + h) * receiver_dev + r
                        row_i = ((f * 2 + 1) * shot_dev + h) * receiver_dev + r
                        qr = qt_ref[row_r : row_r + 1, :]
                        qi = qt_ref[row_i : row_i + 1, :]
                        w = weights[h]
                        real_term = w * (pr * qr - pi * qi)
                        imag_term = w * (pr * qi + pi * qr)
                        real_sum = real_term if real_sum is None else real_sum + real_term
                        imag_sum = imag_term if imag_sum is None else imag_sum + imag_term
                    col_r = ((f * 2 + 0) * shot_dev + i) * receiver_dev + r
                    col_i = ((f * 2 + 1) * shot_dev + i) * receiver_dev + r
                    acc_ref[rows, col_r : col_r + 1] = jnp.sum(real_sum, axis=1, keepdims=True)
                    acc_ref[rows, col_i : col_i + 1] = jnp.sum(imag_sum, axis=1, keepdims=True)
        acc_ref[rows, :] = (acc_ref[rows, :] * KMAX ** (-0.5)).astype(jnp.bfloat16).astype(jnp.float32)

    own_block = me // block
    own_top = pl.multiple_of(own_block * block, block)
    compute(own_top)
    for t in range(block):
        target = own_top + lax.rem(me + t, block)

        @pl.when(target != me)
        def _():
            remote_send(target)

    recv_ref[pl.ds(me, 1), :] = acc_ref[pl.ds(me, 1), :]

    def chunk(step, carry):
        top = pl.multiple_of(lax.rem(own_block + step, steps) * block, block)
        compute(top)
        for t in range(block):
            remote_send(top + lax.rem(me + t, block))
        return carry

    lax.fori_loop(1, steps, chunk, 0)
    every = pltpu.make_async_remote_copy(
        src_ref=acc_ref.at[pl.ds(0, groups - 1)],
        dst_ref=recv_ref.at[pl.ds(0, groups - 1)],
        send_sem=sems.at[0],
        recv_sem=sems.at[1],
        device_id=(me, half),
        device_id_type=pl.DeviceIdType.MESH,
    )
    every.wait_send()
    every.wait_recv()
    out_ref[...] = recv_ref[...].astype(out_ref.dtype)


def shards(traces, frequency_bins, aperture, lengths, filters):
    shot_dev, receivers, time_dev = traces.shape
    groups = lax.axis_size("shot")
    shots = shot_dev * groups
    receiver_dev = receivers // groups
    stride = receivers // shots
    freq_dev = lax.axis_size("freq")
    local_bins = NF // freq_dev
    start_time = lax.axis_index("freq") * time_dev
    half_taps = (TAPS - 1) // 2
    flat_traces = traces.reshape(shot_dev * receivers, time_dev)
    cosines, sines = fourier_rows(frequency_bins, start_time, time_dev, NT)
    basis_rows = (jnp.stack([cosines, -sines], axis=1) * NT ** (-0.5)).astype(jnp.bfloat16)
    basis_rows = basis_rows.reshape(NF * 2, time_dev)
    term = lax.dot_general(
        basis_rows, flat_traces, (((1,), (1,)), ((), ())), preferred_element_type=jnp.float32
    )
    term = term.reshape(NF, 2, shot_dev, receivers)
    core = lax.axis_index("freq")
    mine = lax.dynamic_slice_in_dim(term, core * local_bins, local_bins, axis=0)
    theirs = lax.dynamic_slice_in_dim(term, (1 - core) * local_bins, local_bins, axis=0)
    theirs = lax.ppermute(theirs, "freq", [(0, 1), (1, 0)])
    spectra = (mine + theirs).astype(jnp.bfloat16)
    rows = local_bins * 2 * shot_dev
    near = spectra.reshape(rows, groups, receiver_dev).transpose(1, 0, 2).reshape(groups, rows * receiver_dev)
    stations = jnp.concatenate(
        [spectra[:, :, :, 0 :: 2 * stride], spectra[:, :, :, stride :: 2 * stride]], axis=-1
    ).reshape(1, rows * shots)
    lanes = 128
    outgoing = jnp.concatenate(
        [
            near.reshape(groups, rows * receiver_dev // lanes, lanes).transpose(1, 0, 2),
            jnp.broadcast_to(stations.reshape(rows * shots // lanes, 1, lanes), (rows * shots // lanes, groups, lanes)),
        ],
        axis=0,
    )
    outgoing, aperture, lengths = lax.optimization_barrier((outgoing, aperture, lengths))
    incoming = lax.all_to_all(outgoing, "shot", 1, 1, tiled=True)
    used = jnp.arange(KMAX, dtype=jnp.int32)[None, None, :] < lengths[:, :, None]
    codes = jnp.where(used, (aperture % shot_dev) * groups + aperture // shot_dev, -1)
    codes = codes.reshape(groups, shot_dev, receiver_dev, KMAX).transpose(1, 2, 0, 3)
    counts = jnp.sum(
        (codes[..., None] == jnp.arange(shots, dtype=jnp.int32)).astype(jnp.float32), axis=3
    ).astype(jnp.bfloat16)
    kernel = functools.partial(
        multiply_kernel, local_bins=local_bins, shot_dev=shot_dev, receiver_dev=receiver_dev, groups=groups
    )
    back = pl.pallas_call(
        kernel,
        out_shape=jax.ShapeDtypeStruct((groups, rows * receiver_dev), jnp.bfloat16),
        in_specs=[pl.BlockSpec(memory_space=pltpu.VMEM)] * 2,
        out_specs=pl.BlockSpec(memory_space=pltpu.VMEM),
        scratch_shapes=[
            pltpu.VMEM((rows * receiver_dev, groups), jnp.float32),
            pltpu.VMEM((groups, rows * receiver_dev), jnp.float32),
            pltpu.VMEM((groups, rows * receiver_dev), jnp.float32),
            pltpu.SemaphoreType.DMA((2,)),
        ],
        compiler_params=pltpu.CompilerParams(has_side_effects=True),
        cost_estimate=pl.CostEstimate(
            flops=16 * groups * shots * rows * receiver_dev // 2, transcendentals=0, bytes_accessed=4 * 1024 * 1024
        ),
    )(incoming, counts)
    piece = lax.all_gather(back, "freq", axis=0, tiled=False)
    piece = piece.reshape(freq_dev, groups, local_bins, 2, shot_dev, receiver_dev)
    piece = piece.transpose(4, 1, 5, 0, 2, 3).reshape(shot_dev, receivers, NF * 2)
    wide = time_dev + 2 * half_taps
    wide_times = start_time - half_taps + jnp.arange(wide, dtype=jnp.int32)
    inside = (wide_times >= 0) & (wide_times < NT)
    phases = frequency_bins[:, None] * jnp.clip(wide_times, 0, NT - 1)[None, :] % NT
    angles = phases.astype(jnp.float32) * (2.0 * math.pi / NT)
    wide_rows = jnp.stack([jnp.cos(angles), -jnp.sin(angles)], axis=1).astype(jnp.bfloat16)
    wide_rows = jnp.where(inside[None, None, :], wide_rows.astype(jnp.float32), 0.0).reshape(NF * 2, wide)
    taps = filters.astype(jnp.float32)
    shaped = sum(
        taps[:, tap, None, None] * wide_rows[None, :, 2 * half_taps - tap : 2 * half_taps - tap + time_dev]
        for tap in range(TAPS)
    )
    leading = shaped.astype(jnp.bfloat16)
    trailing = (shaped - leading.astype(jnp.float32)).astype(jnp.bfloat16)
    filtered = lax.dot_general(
        jnp.concatenate([piece, piece], axis=2),
        jnp.concatenate([leading, trailing], axis=1),
        (((2,), (1,)), ((0,), (0,))),
        preferred_element_type=jnp.float32,
    )
    return filtered.astype(jnp.bfloat16)


def solution(mesh):
    in_specs = (
        P("shot", None, "freq"),
        P(),
        P(None, "shot", None),
        P(None, "shot"),
        P("shot", None),
    )
    out_specs = P("shot", None, "freq")
    return jax.shard_map(shards, mesh=mesh, in_specs=in_specs, out_specs=out_specs, check_vma=False)
```

```python
import functools
import math

import jax
import jax.numpy as jnp
from jax import lax
from jax.experimental import pallas as pl
from jax.experimental.pallas import tpu as pltpu
from jax.sharding import PartitionSpec as P

NT = 1024
NF = 8
KMAX = 32
TAPS = 31


def extended(shard, sides, width):
    for axis, dim in sides:
        devices, length = (lax.axis_size(axis), shard.shape[dim])
        up = [(i, (i + 1) % devices) for i in range(devices - 1)]
        down = [(j, i) for i, j in up]
        last = lax.slice_in_dim(shard, length - width, length, axis=dim)
        leading = lax.slice_in_dim(shard, 0, width, axis=dim)
        before = lax.ppermute(last, axis, up)
        after = lax.ppermute(leading, axis, down)
        shard = jnp.concatenate([before, shard, after], axis=dim)
    return shard


def fourier_rows(bin_rows, first_time, sample_count, period):
    sample_times = first_time + jnp.arange(sample_count, dtype=jnp.int32)
    phases = bin_rows[:, None] * sample_times[None, :] % period
    angles = phases.astype(jnp.float32) * (2.0 * math.pi / period)
    return (jnp.cos(angles), jnp.sin(angles))


def multiply_kernel(
    incoming_ref, counts_ref, out_ref, qt_ref, acc_ref, recv_ref, sems, *, local_bins, shot_dev, receiver_dev, groups
):
    qt_ref[...] = incoming_ref[0].astype(jnp.float32).T
    me = lax.axis_index("shot")
    half = lax.axis_index("freq")
    block = 8

    steps = groups // block

    def remote_send(target):
        pltpu.make_async_remote_copy(
            src_ref=acc_ref.at[pl.ds(target, 1)],
            dst_ref=recv_ref.at[pl.ds(me, 1)],
            send_sem=sems.at[0],
            recv_sem=sems.at[1],
            device_id=(target, half),
            device_id_type=pl.DeviceIdType.MESH,
        ).start()

    def compute(top):
        rows = pl.ds(top, block)
        for i in range(shot_dev):
            for r in range(receiver_dev):
                weights = [counts_ref[i, r, rows, h * groups : (h + 1) * groups] for h in range(shot_dev)]
                for f in range(local_bins):
                    real_sum = None
                    imag_sum = None
                    for h in range(shot_dev):
                        slab_r = 1 + ((f * 2 + 0) * shot_dev + i) * shot_dev + h
                        slab_i = 1 + ((f * 2 + 1) * shot_dev + i) * shot_dev + h
                        pr = incoming_ref[slab_r, rows, :].astype(jnp.float32)
                        pi = incoming_ref[slab_i, rows, :].astype(jnp.float32)
                        row_r = ((f * 2 + 0) * shot_dev + h) * receiver_dev + r
                        row_i = ((f * 2 + 1) * shot_dev + h) * receiver_dev + r
                        qr = qt_ref[row_r : row_r + 1, :]
                        qi = qt_ref[row_i : row_i + 1, :]
                        w = weights[h]
                        real_term = w * (pr * qr - pi * qi)
                        imag_term = w * (pr * qi + pi * qr)
                        real_sum = real_term if real_sum is None else real_sum + real_term
                        imag_sum = imag_term if imag_sum is None else imag_sum + imag_term
                    col_r = ((f * 2 + 0) * shot_dev + i) * receiver_dev + r
                    col_i = ((f * 2 + 1) * shot_dev + i) * receiver_dev + r
                    acc_ref[rows, col_r : col_r + 1] = jnp.sum(real_sum, axis=1, keepdims=True)
                    acc_ref[rows, col_i : col_i + 1] = jnp.sum(imag_sum, axis=1, keepdims=True)
        acc_ref[rows, :] = (acc_ref[rows, :] * KMAX ** (-0.5)).astype(jnp.bfloat16).astype(jnp.float32)

    own_block = me // block
    own_top = pl.multiple_of(own_block * block, block)
    compute(own_top)
    for t in range(block):
        target = own_top + lax.rem(me + t, block)

        @pl.when(target != me)
        def _():
            remote_send(target)

    recv_ref[pl.ds(me, 1), :] = acc_ref[pl.ds(me, 1), :]

    def chunk(step, carry):
        top = pl.multiple_of(lax.rem(own_block + step, steps) * block, block)
        compute(top)
        for t in range(block):
            remote_send(top + lax.rem(me + t, block))
        return carry

    lax.fori_loop(1, steps, chunk, 0)
    every = pltpu.make_async_remote_copy(
        src_ref=acc_ref.at[pl.ds(0, groups - 1)],
        dst_ref=recv_ref.at[pl.ds(0, groups - 1)],
        send_sem=sems.at[0],
        recv_sem=sems.at[1],
        device_id=(me, half),
        device_id_type=pl.DeviceIdType.MESH,
    )
    every.wait_send()
    every.wait_recv()
    qt_ref[...] = recv_ref[...].T
    width = groups * receiver_dev
    owners = lax.broadcasted_iota(jnp.int32, (groups, width), 0)
    places = lax.broadcasted_iota(jnp.int32, (groups, width), 1)
    rows_out = local_bins * 2
    for i in range(shot_dev):
        total = None
        for r in range(receiver_dev):
            spread = (places == owners * receiver_dev + r).astype(jnp.bfloat16)
            picked = qt_ref[pl.ds(i * receiver_dev + r, rows_out, stride=shot_dev * receiver_dev), :]
            term = jnp.dot(picked.astype(jnp.bfloat16), spread, preferred_element_type=jnp.float32)
            total = term if total is None else total + term
        out_ref[i * rows_out : (i + 1) * rows_out, :] = total.astype(out_ref.dtype)


def shards(traces, frequency_bins, aperture, lengths, filters):
    shot_dev, receivers, time_dev = traces.shape
    groups = lax.axis_size("shot")
    shots = shot_dev * groups
    receiver_dev = receivers // groups
    stride = receivers // shots
    freq_dev = lax.axis_size("freq")
    local_bins = NF // freq_dev
    start_time = lax.axis_index("freq") * time_dev
    half_taps = (TAPS - 1) // 2
    flat_traces = traces.reshape(shot_dev * receivers, time_dev)
    cosines, sines = fourier_rows(frequency_bins, start_time, time_dev, NT)
    basis_rows = (jnp.stack([cosines, -sines], axis=1) * NT ** (-0.5)).astype(jnp.bfloat16)
    basis_rows = basis_rows.reshape(NF * 2, time_dev)
    term = lax.dot_general(
        basis_rows, flat_traces, (((1,), (1,)), ((), ())), preferred_element_type=jnp.float32
    )
    term = term.reshape(NF, 2, shot_dev, receivers)
    core = lax.axis_index("freq")
    mine = lax.dynamic_slice_in_dim(term, core * local_bins, local_bins, axis=0)
    theirs = lax.dynamic_slice_in_dim(term, (1 - core) * local_bins, local_bins, axis=0)
    theirs = lax.ppermute(theirs, "freq", [(0, 1), (1, 0)])
    spectra = (mine + theirs).astype(jnp.bfloat16)
    rows = local_bins * 2 * shot_dev
    near = spectra.reshape(rows, groups, receiver_dev).transpose(1, 0, 2).reshape(groups, rows * receiver_dev)
    stations = jnp.concatenate(
        [spectra[:, :, :, 0 :: 2 * stride], spectra[:, :, :, stride :: 2 * stride]], axis=-1
    ).reshape(1, rows * shots)
    lanes = 128
    outgoing = jnp.concatenate(
        [
            near.reshape(groups, rows * receiver_dev // lanes, lanes).transpose(1, 0, 2),
            jnp.broadcast_to(stations.reshape(rows * shots // lanes, 1, lanes), (rows * shots // lanes, groups, lanes)),
        ],
        axis=0,
    )
    outgoing, aperture, lengths = lax.optimization_barrier((outgoing, aperture, lengths))
    incoming = lax.all_to_all(outgoing, "shot", 1, 1, tiled=True)
    used = jnp.arange(KMAX, dtype=jnp.int32)[None, None, :] < lengths[:, :, None]
    codes = jnp.where(used, (aperture % shot_dev) * groups + aperture // shot_dev, -1)
    codes = codes.reshape(groups, shot_dev, receiver_dev, KMAX).transpose(1, 2, 0, 3)
    counts = jnp.sum(
        (codes[..., None] == jnp.arange(shots, dtype=jnp.int32)).astype(jnp.float32), axis=3
    )
    kernel = functools.partial(
        multiply_kernel, local_bins=local_bins, shot_dev=shot_dev, receiver_dev=receiver_dev, groups=groups
    )
    back = pl.pallas_call(
        kernel,
        out_shape=jax.ShapeDtypeStruct((shot_dev * local_bins * 2, receivers), jnp.bfloat16),
        in_specs=[pl.BlockSpec(memory_space=pltpu.VMEM)] * 2,
        out_specs=pl.BlockSpec(memory_space=pltpu.VMEM),
        scratch_shapes=[
            pltpu.VMEM((rows * receiver_dev, groups), jnp.float32),
            pltpu.VMEM((groups, rows * receiver_dev), jnp.float32),
            pltpu.VMEM((groups, rows * receiver_dev), jnp.float32),
            pltpu.SemaphoreType.DMA((2,)),
        ],
        compiler_params=pltpu.CompilerParams(has_side_effects=True),
        cost_estimate=pl.CostEstimate(
            flops=16 * groups * shots * rows * receiver_dev // 2, transcendentals=0, bytes_accessed=4 * 1024 * 1024
        ),
    )(incoming, counts)
    piece = lax.all_gather(back, "freq", axis=0, tiled=False)
    piece = piece.reshape(freq_dev, shot_dev, local_bins * 2, receivers).transpose(1, 0, 2, 3)
    piece = piece.reshape(shot_dev, NF * 2, receivers)
    wide = time_dev + 2 * half_taps
    wide_times = start_time - half_taps + jnp.arange(wide, dtype=jnp.int32)
    inside = (wide_times >= 0) & (wide_times < NT)
    phases = frequency_bins[:, None] * jnp.clip(wide_times, 0, NT - 1)[None, :] % NT
    angles = phases.astype(jnp.float32) * (2.0 * math.pi / NT)
    wide_rows = jnp.stack([jnp.cos(angles), -jnp.sin(angles)], axis=1).astype(jnp.bfloat16)
    wide_rows = jnp.where(inside[None, None, :], wide_rows.astype(jnp.float32), 0.0).reshape(NF * 2, wide)
    taps = filters.astype(jnp.float32)
    shaped = sum(
        taps[:, tap, None, None] * wide_rows[None, :, 2 * half_taps - tap : 2 * half_taps - tap + time_dev]
        for tap in range(TAPS)
    )
    leading = shaped.astype(jnp.bfloat16)
    trailing = (shaped - leading.astype(jnp.float32)).astype(jnp.bfloat16)
    filtered = lax.dot_general(
        jnp.concatenate([piece, piece], axis=1),
        jnp.concatenate([leading, trailing], axis=1),
        (((1,), (1,)), ((0,), (0,))),
        preferred_element_type=jnp.float32,
    )
    return filtered.astype(jnp.bfloat16)


def solution(mesh):
    in_specs = (
        P("shot", None, "freq"),
        P(),
        P(None, "shot", None),
        P(None, "shot"),
        P("shot", None),
    )
    out_specs = P("shot", None, "freq")
    return jax.shard_map(shards, mesh=mesh, in_specs=in_specs, out_specs=out_specs, check_vma=False)
```

```python
import functools
import math

import jax
import jax.numpy as jnp
from jax import lax
from jax.experimental import pallas as pl
from jax.experimental.pallas import tpu as pltpu
from jax.sharding import PartitionSpec as P

NT = 1024
NF = 8
KMAX = 32
TAPS = 31


def extended(shard, sides, width):
    for axis, dim in sides:
        devices, length = (lax.axis_size(axis), shard.shape[dim])
        up = [(i, (i + 1) % devices) for i in range(devices - 1)]
        down = [(j, i) for i, j in up]
        last = lax.slice_in_dim(shard, length - width, length, axis=dim)
        leading = lax.slice_in_dim(shard, 0, width, axis=dim)
        before = lax.ppermute(last, axis, up)
        after = lax.ppermute(leading, axis, down)
        shard = jnp.concatenate([before, shard, after], axis=dim)
    return shard


def fourier_rows(bin_rows, first_time, sample_count, period):
    sample_times = first_time + jnp.arange(sample_count, dtype=jnp.int32)
    phases = bin_rows[:, None] * sample_times[None, :] % period
    angles = phases.astype(jnp.float32) * (2.0 * math.pi / period)
    return (jnp.cos(angles), jnp.sin(angles))


def multiply_kernel(
    incoming_ref, counts_ref, out_ref, qt_ref, acc_ref, recv_ref, sems, *, local_bins, shot_dev, receiver_dev, groups
):
    qt_ref[...] = incoming_ref[0].astype(jnp.float32).T
    me = lax.axis_index("shot")
    half = lax.axis_index("freq")
    block = 8

    steps = groups // block

    def remote_send(target):
        pltpu.make_async_remote_copy(
            src_ref=acc_ref.at[pl.ds(target, 1)],
            dst_ref=recv_ref.at[pl.ds(me, 1)],
            send_sem=sems.at[0],
            recv_sem=sems.at[1],
            device_id=(target, half),
            device_id_type=pl.DeviceIdType.MESH,
        ).start()

    def compute(top):
        rows = pl.ds(top, block)
        for i in range(shot_dev):
            for r in range(receiver_dev):
                weights = [counts_ref[i, r, rows, h * groups : (h + 1) * groups] for h in range(shot_dev)]
                for f in range(local_bins):
                    real_sum = None
                    imag_sum = None
                    for h in range(shot_dev):
                        slab_r = 1 + ((f * 2 + 0) * shot_dev + i) * shot_dev + h
                        slab_i = 1 + ((f * 2 + 1) * shot_dev + i) * shot_dev + h
                        pr = incoming_ref[slab_r, rows, :].astype(jnp.float32)
                        pi = incoming_ref[slab_i, rows, :].astype(jnp.float32)
                        row_r = ((f * 2 + 0) * shot_dev + h) * receiver_dev + r
                        row_i = ((f * 2 + 1) * shot_dev + h) * receiver_dev + r
                        qr = qt_ref[row_r : row_r + 1, :]
                        qi = qt_ref[row_i : row_i + 1, :]
                        w = weights[h]
                        real_term = w * (pr * qr - pi * qi)
                        imag_term = w * (pr * qi + pi * qr)
                        real_sum = real_term if real_sum is None else real_sum + real_term
                        imag_sum = imag_term if imag_sum is None else imag_sum + imag_term
                    col_r = ((f * 2 + 0) * shot_dev + i) * receiver_dev + r
                    col_i = ((f * 2 + 1) * shot_dev + i) * receiver_dev + r
                    acc_ref[rows, col_r : col_r + 1] = jnp.sum(real_sum, axis=1, keepdims=True)
                    acc_ref[rows, col_i : col_i + 1] = jnp.sum(imag_sum, axis=1, keepdims=True)
        acc_ref[rows, :] = (acc_ref[rows, :] * KMAX ** (-0.5)).astype(jnp.bfloat16).astype(jnp.float32)

    own_block = me // block
    own_top = pl.multiple_of(own_block * block, block)
    compute(own_top)
    for t in range(block):
        target = own_top + lax.rem(me + t, block)

        @pl.when(target != me)
        def _():
            remote_send(target)

    recv_ref[pl.ds(me, 1), :] = acc_ref[pl.ds(me, 1), :]

    def chunk(step, carry):
        top = pl.multiple_of(lax.rem(own_block + step, steps) * block, block)
        compute(top)
        for t in range(block):
            remote_send(top + lax.rem(me + t, block))
        return carry

    lax.fori_loop(1, steps, chunk, 0)
    every = pltpu.make_async_remote_copy(
        src_ref=acc_ref.at[pl.ds(0, groups - 1)],
        dst_ref=recv_ref.at[pl.ds(0, groups - 1)],
        send_sem=sems.at[0],
        recv_sem=sems.at[1],
        device_id=(me, half),
        device_id_type=pl.DeviceIdType.MESH,
    )
    every.wait_send()
    every.wait_recv()
    qt_ref[...] = recv_ref[...].T
    width = groups * receiver_dev
    owners = lax.broadcasted_iota(jnp.int32, (groups, width), 0)
    places = lax.broadcasted_iota(jnp.int32, (groups, width), 1)
    rows_out = local_bins * 2
    for i in range(shot_dev):
        total = None
        for r in range(receiver_dev):
            spread = (places == owners * receiver_dev + r).astype(jnp.bfloat16)
            picked = qt_ref[pl.ds(i * receiver_dev + r, rows_out, stride=shot_dev * receiver_dev), :]
            term = jnp.dot(picked.astype(jnp.bfloat16), spread, preferred_element_type=jnp.float32)
            total = term if total is None else total + term
        out_ref[i * rows_out : (i + 1) * rows_out, :] = total.astype(out_ref.dtype)


def shards(traces, frequency_bins, aperture, lengths, filters):
    shot_dev, receivers, time_dev = traces.shape
    groups = lax.axis_size("shot")
    shots = shot_dev * groups
    receiver_dev = receivers // groups
    stride = receivers // shots
    freq_dev = lax.axis_size("freq")
    local_bins = NF // freq_dev
    start_time = lax.axis_index("freq") * time_dev
    half_taps = (TAPS - 1) // 2
    flat_traces = traces.reshape(shot_dev * receivers, time_dev)
    cosines, sines = fourier_rows(frequency_bins, start_time, time_dev, NT)
    basis_rows = (jnp.stack([cosines, -sines], axis=1) * NT ** (-0.5)).astype(jnp.bfloat16)
    basis_rows = basis_rows.reshape(NF * 2, time_dev)
    term = lax.dot_general(
        basis_rows, flat_traces, (((1,), (1,)), ((), ())), preferred_element_type=jnp.float32
    )
    term = term.reshape(NF, 2, shot_dev, receivers)
    core = lax.axis_index("freq")
    mine = lax.dynamic_slice_in_dim(term, core * local_bins, local_bins, axis=0)
    theirs = lax.dynamic_slice_in_dim(term, (1 - core) * local_bins, local_bins, axis=0)
    theirs = lax.ppermute(theirs, "freq", [(0, 1), (1, 0)])
    spectra = (mine + theirs).astype(jnp.bfloat16)
    rows = local_bins * 2 * shot_dev
    near = spectra.reshape(rows, groups, receiver_dev).transpose(1, 0, 2).reshape(groups, rows * receiver_dev)
    stations = jnp.concatenate(
        [spectra[:, :, :, 0 :: 2 * stride], spectra[:, :, :, stride :: 2 * stride]], axis=-1
    ).reshape(1, rows * shots)
    lanes = 128
    outgoing = jnp.concatenate(
        [
            near.reshape(groups, rows * receiver_dev // lanes, lanes).transpose(1, 0, 2),
            jnp.broadcast_to(stations.reshape(rows * shots // lanes, 1, lanes), (rows * shots // lanes, groups, lanes)),
        ],
        axis=0,
    )
    outgoing, aperture, lengths = lax.optimization_barrier((outgoing, aperture, lengths))
    incoming = lax.all_to_all(outgoing, "shot", 1, 1, tiled=True)
    used = jnp.arange(KMAX, dtype=jnp.int32)[None, None, :] < lengths[:, :, None]
    codes = jnp.where(used, (aperture % shot_dev) * groups + aperture // shot_dev, -1)
    codes = codes.reshape(groups, shot_dev, receiver_dev, KMAX).transpose(1, 2, 0, 3)
    counts = jnp.sum(
        (codes[..., None] == jnp.arange(shots, dtype=jnp.int32)).astype(jnp.float32), axis=3
    )
    kernel = functools.partial(
        multiply_kernel, local_bins=local_bins, shot_dev=shot_dev, receiver_dev=receiver_dev, groups=groups
    )
    back = pl.pallas_call(
        kernel,
        out_shape=jax.ShapeDtypeStruct((shot_dev * local_bins * 2, receivers), jnp.bfloat16),
        in_specs=[pl.BlockSpec(memory_space=pltpu.VMEM)] * 2,
        out_specs=pl.BlockSpec(memory_space=pltpu.VMEM),
        scratch_shapes=[
            pltpu.VMEM((rows * receiver_dev, groups), jnp.float32),
            pltpu.VMEM((groups, rows * receiver_dev), jnp.float32),
            pltpu.VMEM((groups, rows * receiver_dev), jnp.float32),
            pltpu.SemaphoreType.DMA((2,)),
        ],
        compiler_params=pltpu.CompilerParams(has_side_effects=True),
        cost_estimate=pl.CostEstimate(
            flops=16 * groups * shots * rows * receiver_dev // 2, transcendentals=0, bytes_accessed=4 * 1024 * 1024
        ),
    )(incoming, counts)
    piece = lax.all_gather(back.reshape(shot_dev, local_bins * 2, receivers), "freq", axis=1, tiled=True)
    wide = time_dev + 2 * half_taps
    wide_times = start_time - half_taps + jnp.arange(wide, dtype=jnp.int32)
    inside = (wide_times >= 0) & (wide_times < NT)
    phases = frequency_bins[:, None] * jnp.clip(wide_times, 0, NT - 1)[None, :] % NT
    angles = phases.astype(jnp.float32) * (2.0 * math.pi / NT)
    wide_rows = jnp.stack([jnp.cos(angles), -jnp.sin(angles)], axis=1).astype(jnp.bfloat16)
    wide_rows = jnp.where(inside[None, None, :], wide_rows.astype(jnp.float32), 0.0).reshape(NF * 2, wide)
    taps = filters.astype(jnp.float32)
    shaped = sum(
        taps[:, tap, None, None] * wide_rows[None, :, 2 * half_taps - tap : 2 * half_taps - tap + time_dev]
        for tap in range(TAPS)
    )
    leading = shaped.astype(jnp.bfloat16)
    trailing = (shaped - leading.astype(jnp.float32)).astype(jnp.bfloat16)
    filtered = lax.dot_general(
        jnp.concatenate([piece, piece], axis=1),
        jnp.concatenate([leading, trailing], axis=1),
        (((1,), (1,)), ((0,), (0,))),
        preferred_element_type=jnp.float32,
    )
    return filtered.astype(jnp.bfloat16)


def solution(mesh):
    in_specs = (
        P("shot", None, "freq"),
        P(),
        P(None, "shot", None),
        P(None, "shot"),
        P("shot", None),
    )
    out_specs = P("shot", None, "freq")
    return jax.shard_map(shards, mesh=mesh, in_specs=in_specs, out_specs=out_specs, check_vma=False)
```

```python
import functools
import math

import jax
import jax.numpy as jnp
from jax import lax
from jax.experimental import pallas as pl
from jax.experimental.pallas import tpu as pltpu
from jax.sharding import PartitionSpec as P

NT = 1024
NF = 8
KMAX = 32
TAPS = 31


def extended(shard, sides, width):
    for axis, dim in sides:
        devices, length = (lax.axis_size(axis), shard.shape[dim])
        up = [(i, (i + 1) % devices) for i in range(devices - 1)]
        down = [(j, i) for i, j in up]
        last = lax.slice_in_dim(shard, length - width, length, axis=dim)
        leading = lax.slice_in_dim(shard, 0, width, axis=dim)
        before = lax.ppermute(last, axis, up)
        after = lax.ppermute(leading, axis, down)
        shard = jnp.concatenate([before, shard, after], axis=dim)
    return shard


def fourier_rows(bin_rows, first_time, sample_count, period):
    sample_times = first_time + jnp.arange(sample_count, dtype=jnp.int32)
    phases = bin_rows[:, None] * sample_times[None, :] % period
    angles = phases.astype(jnp.float32) * (2.0 * math.pi / period)
    return (jnp.cos(angles), jnp.sin(angles))


def multiply_kernel(
    incoming_ref, counts_ref, out_ref, qt_ref, acc_ref, recv_ref, sems, *, local_bins, shot_dev, receiver_dev, groups
):
    qt_ref[...] = incoming_ref[0].astype(jnp.float32).T
    me = lax.axis_index("shot")
    half = lax.axis_index("freq")
    block = 8

    steps = groups // block

    def remote_send(target):
        pltpu.make_async_remote_copy(
            src_ref=acc_ref.at[pl.ds(target, 1)],
            dst_ref=recv_ref.at[pl.ds(me, 1)],
            send_sem=sems.at[0],
            recv_sem=sems.at[1],
            device_id=(target, half),
            device_id_type=pl.DeviceIdType.MESH,
        ).start()

    def compute(top):
        rows = pl.ds(top, block)
        for i in range(shot_dev):
            for r in range(receiver_dev):
                weights = [counts_ref[i, r, rows, h * groups : (h + 1) * groups] for h in range(shot_dev)]
                for f in range(local_bins):
                    real_sum = None
                    imag_sum = None
                    for h in range(shot_dev):
                        slab_r = 1 + ((f * 2 + 0) * shot_dev + i) * shot_dev + h
                        slab_i = 1 + ((f * 2 + 1) * shot_dev + i) * shot_dev + h
                        pr = incoming_ref[slab_r, rows, :].astype(jnp.float32)
                        pi = incoming_ref[slab_i, rows, :].astype(jnp.float32)
                        row_r = ((f * 2 + 0) * shot_dev + h) * receiver_dev + r
                        row_i = ((f * 2 + 1) * shot_dev + h) * receiver_dev + r
                        qr = qt_ref[row_r : row_r + 1, :]
                        qi = qt_ref[row_i : row_i + 1, :]
                        w = weights[h]
                        real_term = w * (pr * qr - pi * qi)
                        imag_term = w * (pr * qi + pi * qr)
                        real_sum = real_term if real_sum is None else real_sum + real_term
                        imag_sum = imag_term if imag_sum is None else imag_sum + imag_term
                    col_r = ((f * 2 + 0) * shot_dev + i) * receiver_dev + r
                    col_i = ((f * 2 + 1) * shot_dev + i) * receiver_dev + r
                    acc_ref[rows, col_r : col_r + 1] = jnp.sum(real_sum, axis=1, keepdims=True)
                    acc_ref[rows, col_i : col_i + 1] = jnp.sum(imag_sum, axis=1, keepdims=True)
        acc_ref[rows, :] = (acc_ref[rows, :] * KMAX ** (-0.5)).astype(jnp.bfloat16).astype(jnp.float32)

    own_block = me // block
    own_top = pl.multiple_of(own_block * block, block)
    compute(own_top)
    for t in range(block):
        target = own_top + lax.rem(me + t, block)

        @pl.when(target != me)
        def _():
            remote_send(target)

    recv_ref[pl.ds(me, 1), :] = acc_ref[pl.ds(me, 1), :]

    def chunk(step, carry):
        top = pl.multiple_of(lax.rem(own_block + step, steps) * block, block)
        compute(top)
        for t in range(block):
            remote_send(top + lax.rem(me + t, block))
        return carry

    lax.fori_loop(1, steps, chunk, 0)
    every = pltpu.make_async_remote_copy(
        src_ref=acc_ref.at[pl.ds(0, groups - 1)],
        dst_ref=recv_ref.at[pl.ds(0, groups - 1)],
        send_sem=sems.at[0],
        recv_sem=sems.at[1],
        device_id=(me, half),
        device_id_type=pl.DeviceIdType.MESH,
    )
    every.wait_send()
    every.wait_recv()
    qt_ref[...] = recv_ref[...].T
    width = groups * receiver_dev
    owners = lax.broadcasted_iota(jnp.int32, (groups, width), 0)
    places = lax.broadcasted_iota(jnp.int32, (groups, width), 1)
    rows_out = local_bins * 2
    for i in range(shot_dev):
        total = None
        for r in range(receiver_dev):
            spread = (places == owners * receiver_dev + r).astype(jnp.bfloat16)
            picked = qt_ref[pl.ds(i * receiver_dev + r, rows_out, stride=shot_dev * receiver_dev), :]
            term = jnp.dot(picked.astype(jnp.bfloat16), spread, preferred_element_type=jnp.float32)
            total = term if total is None else total + term
        out_ref[i * rows_out : (i + 1) * rows_out, :] = total.astype(out_ref.dtype)


def shards(traces, frequency_bins, aperture, lengths, filters):
    shot_dev, receivers, time_dev = traces.shape
    groups = lax.axis_size("shot")
    shots = shot_dev * groups
    receiver_dev = receivers // groups
    stride = receivers // shots
    freq_dev = lax.axis_size("freq")
    local_bins = NF // freq_dev
    start_time = lax.axis_index("freq") * time_dev
    half_taps = (TAPS - 1) // 2
    flat_traces = traces.reshape(shot_dev * receivers, time_dev)
    cosines, sines = fourier_rows(frequency_bins, start_time, time_dev, NT)
    basis_rows = (jnp.stack([cosines, -sines], axis=1) * NT ** (-0.5)).astype(jnp.bfloat16)
    basis_rows = basis_rows.reshape(NF * 2, time_dev)
    term = lax.dot_general(
        basis_rows, flat_traces, (((1,), (1,)), ((), ())), preferred_element_type=jnp.float32
    )
    term = term.reshape(NF, 2, shot_dev, receivers)
    core = lax.axis_index("freq")
    mine = lax.dynamic_slice_in_dim(term, core * local_bins, local_bins, axis=0)
    theirs = lax.dynamic_slice_in_dim(term, (1 - core) * local_bins, local_bins, axis=0)
    theirs = lax.ppermute(theirs, "freq", [(0, 1), (1, 0)])
    spectra = (mine + theirs).astype(jnp.bfloat16)
    rows = local_bins * 2 * shot_dev
    near = spectra.reshape(rows, groups, receiver_dev).transpose(1, 0, 2).reshape(groups, rows * receiver_dev)
    station_of = jnp.arange(shots, dtype=jnp.int32)
    station_of = (station_of % groups) * 2 * stride + (station_of // groups) * stride
    selection = (jnp.arange(receivers, dtype=jnp.int32)[:, None] == station_of[None, :]).astype(jnp.bfloat16)
    stations = jnp.dot(
        spectra.reshape(rows, receivers), selection, preferred_element_type=jnp.float32
    ).astype(jnp.bfloat16).reshape(1, rows * shots)
    lanes = 128
    outgoing = jnp.concatenate(
        [
            near.reshape(groups, rows * receiver_dev // lanes, lanes).transpose(1, 0, 2),
            jnp.broadcast_to(stations.reshape(rows * shots // lanes, 1, lanes), (rows * shots // lanes, groups, lanes)),
        ],
        axis=0,
    )
    outgoing, aperture, lengths = lax.optimization_barrier((outgoing, aperture, lengths))
    incoming = lax.all_to_all(outgoing, "shot", 1, 1, tiled=True)
    used = jnp.arange(KMAX, dtype=jnp.int32)[None, None, :] < lengths[:, :, None]
    codes = jnp.where(used, (aperture % shot_dev) * groups + aperture // shot_dev, -1)
    codes = codes.reshape(groups, shot_dev, receiver_dev, KMAX).transpose(1, 2, 0, 3)
    counts = jnp.sum(
        (codes[..., None] == jnp.arange(shots, dtype=jnp.int32)).astype(jnp.float32), axis=3
    )
    kernel = functools.partial(
        multiply_kernel, local_bins=local_bins, shot_dev=shot_dev, receiver_dev=receiver_dev, groups=groups
    )
    back = pl.pallas_call(
        kernel,
        out_shape=jax.ShapeDtypeStruct((shot_dev * local_bins * 2, receivers), jnp.bfloat16),
        in_specs=[pl.BlockSpec(memory_space=pltpu.VMEM)] * 2,
        out_specs=pl.BlockSpec(memory_space=pltpu.VMEM),
        scratch_shapes=[
            pltpu.VMEM((rows * receiver_dev, groups), jnp.float32),
            pltpu.VMEM((groups, rows * receiver_dev), jnp.float32),
            pltpu.VMEM((groups, rows * receiver_dev), jnp.float32),
            pltpu.SemaphoreType.DMA((2,)),
        ],
        compiler_params=pltpu.CompilerParams(has_side_effects=True),
        cost_estimate=pl.CostEstimate(
            flops=16 * groups * shots * rows * receiver_dev // 2, transcendentals=0, bytes_accessed=4 * 1024 * 1024
        ),
    )(incoming, counts)
    piece = lax.all_gather(back, "freq", axis=0, tiled=False)
    piece = piece.reshape(freq_dev, shot_dev, local_bins * 2, receivers).transpose(1, 0, 2, 3)
    piece = piece.reshape(shot_dev, NF * 2, receivers)
    wide = time_dev + 2 * half_taps
    wide_times = start_time - half_taps + jnp.arange(wide, dtype=jnp.int32)
    inside = (wide_times >= 0) & (wide_times < NT)
    phases = frequency_bins[:, None] * jnp.clip(wide_times, 0, NT - 1)[None, :] % NT
    angles = phases.astype(jnp.float32) * (2.0 * math.pi / NT)
    wide_rows = jnp.stack([jnp.cos(angles), -jnp.sin(angles)], axis=1).astype(jnp.bfloat16)
    wide_rows = jnp.where(inside[None, None, :], wide_rows.astype(jnp.float32), 0.0).reshape(NF * 2, wide)
    taps = filters.astype(jnp.float32)
    shaped = sum(
        taps[:, tap, None, None] * wide_rows[None, :, 2 * half_taps - tap : 2 * half_taps - tap + time_dev]
        for tap in range(TAPS)
    )
    leading = shaped.astype(jnp.bfloat16)
    trailing = (shaped - leading.astype(jnp.float32)).astype(jnp.bfloat16)
    filtered = lax.dot_general(
        jnp.concatenate([piece, piece], axis=1),
        jnp.concatenate([leading, trailing], axis=1),
        (((1,), (1,)), ((0,), (0,))),
        preferred_element_type=jnp.float32,
    )
    return filtered.astype(jnp.bfloat16)


def solution(mesh):
    in_specs = (
        P("shot", None, "freq"),
        P(),
        P(None, "shot", None),
        P(None, "shot"),
        P("shot", None),
    )
    out_specs = P("shot", None, "freq")
    return jax.shard_map(shards, mesh=mesh, in_specs=in_specs, out_specs=out_specs, check_vma=False)
```

```python
import functools
import math

import jax
import jax.numpy as jnp
from jax import lax
from jax.experimental import pallas as pl
from jax.experimental.pallas import tpu as pltpu
from jax.sharding import PartitionSpec as P

NT = 1024
NF = 8
KMAX = 32
TAPS = 31


def extended(shard, sides, width):
    for axis, dim in sides:
        devices, length = (lax.axis_size(axis), shard.shape[dim])
        up = [(i, (i + 1) % devices) for i in range(devices - 1)]
        down = [(j, i) for i, j in up]
        last = lax.slice_in_dim(shard, length - width, length, axis=dim)
        leading = lax.slice_in_dim(shard, 0, width, axis=dim)
        before = lax.ppermute(last, axis, up)
        after = lax.ppermute(leading, axis, down)
        shard = jnp.concatenate([before, shard, after], axis=dim)
    return shard


def fourier_rows(bin_rows, first_time, sample_count, period):
    sample_times = first_time + jnp.arange(sample_count, dtype=jnp.int32)
    phases = bin_rows[:, None] * sample_times[None, :] % period
    angles = phases.astype(jnp.float32) * (2.0 * math.pi / period)
    return (jnp.cos(angles), jnp.sin(angles))


def multiply_kernel(
    incoming_ref, counts_ref, out_ref, qt_ref, acc_ref, recv_ref, sems, *, local_bins, shot_dev, receiver_dev, groups
):
    qt_ref[...] = incoming_ref[0].astype(jnp.float32).T
    me = lax.axis_index("shot")
    half = lax.axis_index("freq")
    block = 8

    steps = groups // block

    def remote_send(target):
        pltpu.make_async_remote_copy(
            src_ref=acc_ref.at[pl.ds(target, 1)],
            dst_ref=recv_ref.at[pl.ds(me, 1)],
            send_sem=sems.at[0],
            recv_sem=sems.at[1],
            device_id=(target, half),
            device_id_type=pl.DeviceIdType.MESH,
        ).start()

    def compute(top):
        rows = pl.ds(top, block)
        for i in range(shot_dev):
            for r in range(receiver_dev):
                weights = [counts_ref[i, r, rows, h * groups : (h + 1) * groups] for h in range(shot_dev)]
                for f in range(local_bins):
                    real_sum = None
                    imag_sum = None
                    for h in range(shot_dev):
                        slab_r = 1 + ((f * 2 + 0) * shot_dev + i) * shot_dev + h
                        slab_i = 1 + ((f * 2 + 1) * shot_dev + i) * shot_dev + h
                        pr = incoming_ref[slab_r, rows, :].astype(jnp.float32)
                        pi = incoming_ref[slab_i, rows, :].astype(jnp.float32)
                        row_r = ((f * 2 + 0) * shot_dev + h) * receiver_dev + r
                        row_i = ((f * 2 + 1) * shot_dev + h) * receiver_dev + r
                        qr = qt_ref[row_r : row_r + 1, :]
                        qi = qt_ref[row_i : row_i + 1, :]
                        w = weights[h]
                        real_term = w * (pr * qr - pi * qi)
                        imag_term = w * (pr * qi + pi * qr)
                        real_sum = real_term if real_sum is None else real_sum + real_term
                        imag_sum = imag_term if imag_sum is None else imag_sum + imag_term
                    col_r = ((f * 2 + 0) * shot_dev + i) * receiver_dev + r
                    col_i = ((f * 2 + 1) * shot_dev + i) * receiver_dev + r
                    acc_ref[rows, col_r : col_r + 1] = jnp.sum(real_sum, axis=1, keepdims=True)
                    acc_ref[rows, col_i : col_i + 1] = jnp.sum(imag_sum, axis=1, keepdims=True)
        acc_ref[rows, :] = (acc_ref[rows, :] * KMAX ** (-0.5)).astype(jnp.bfloat16).astype(jnp.float32)

    own_block = me // block
    own_top = pl.multiple_of(own_block * block, block)
    compute(own_top)
    for t in range(block):
        target = own_top + lax.rem(me + t, block)

        @pl.when(target != me)
        def _():
            remote_send(target)

    recv_ref[pl.ds(me, 1), :] = acc_ref[pl.ds(me, 1), :]

    def chunk(step, carry):
        top = pl.multiple_of(lax.rem(own_block + step, steps) * block, block)
        compute(top)
        for t in range(block):
            remote_send(top + lax.rem(me + t, block))
        return carry

    lax.fori_loop(1, steps, chunk, 0)
    every = pltpu.make_async_remote_copy(
        src_ref=acc_ref.at[pl.ds(0, groups - 1)],
        dst_ref=recv_ref.at[pl.ds(0, groups - 1)],
        send_sem=sems.at[0],
        recv_sem=sems.at[1],
        device_id=(me, half),
        device_id_type=pl.DeviceIdType.MESH,
    )
    every.wait_send()
    every.wait_recv()
    qt_ref[...] = recv_ref[...].T
    width = groups * receiver_dev
    owners = lax.broadcasted_iota(jnp.int32, (groups, width), 0)
    places = lax.broadcasted_iota(jnp.int32, (groups, width), 1)
    rows_out = local_bins * 2
    for i in range(shot_dev):
        total = None
        for r in range(receiver_dev):
            spread = (places == owners * receiver_dev + r).astype(jnp.bfloat16)
            picked = qt_ref[pl.ds(i * receiver_dev + r, rows_out, stride=shot_dev * receiver_dev), :]
            term = jnp.dot(picked.astype(jnp.bfloat16), spread, preferred_element_type=jnp.float32)
            total = term if total is None else total + term
        out_ref[i * rows_out : (i + 1) * rows_out, :] = total.astype(out_ref.dtype)


def shards(traces, frequency_bins, aperture, lengths, filters):
    shot_dev, receivers, time_dev = traces.shape
    groups = lax.axis_size("shot")
    shots = shot_dev * groups
    receiver_dev = receivers // groups
    stride = receivers // shots
    freq_dev = lax.axis_size("freq")
    local_bins = NF // freq_dev
    start_time = lax.axis_index("freq") * time_dev
    half_taps = (TAPS - 1) // 2
    flat_traces = traces.reshape(shot_dev * receivers, time_dev)
    cosines, sines = fourier_rows(frequency_bins, start_time, time_dev, NT)
    basis_rows = (jnp.stack([cosines, -sines], axis=1) * NT ** (-0.5)).astype(jnp.bfloat16)
    basis_rows = basis_rows.reshape(NF * 2, time_dev)
    term = lax.dot_general(
        basis_rows, flat_traces, (((1,), (1,)), ((), ())), preferred_element_type=jnp.float32
    )
    term = term.reshape(NF, 2, shot_dev, receivers)
    core = lax.axis_index("freq")
    mine = lax.dynamic_slice_in_dim(term, core * local_bins, local_bins, axis=0)
    theirs = lax.dynamic_slice_in_dim(term, (1 - core) * local_bins, local_bins, axis=0)
    theirs = lax.ppermute(theirs, "freq", [(0, 1), (1, 0)])
    spectra = (mine + theirs).astype(jnp.bfloat16)
    rows = local_bins * 2 * shot_dev
    every = jnp.arange(receivers, dtype=jnp.int32)
    flat = spectra.reshape(rows, 1, receivers)
    spread = jnp.where(
        (every % receiver_dev)[None, None, :] == jnp.arange(receiver_dev, dtype=jnp.int32)[None, :, None], flat, 0
    ).reshape(rows * receiver_dev, receivers)
    owner = (every[None, :] // receiver_dev == jnp.arange(groups, dtype=jnp.int32)[:, None]).astype(jnp.bfloat16)
    near = lax.dot_general(
        owner, spread, (((1,), (1,)), ((), ())), preferred_element_type=jnp.float32
    ).astype(jnp.bfloat16)
    station_of = jnp.arange(shots, dtype=jnp.int32)
    station_of = (station_of % groups) * 2 * stride + (station_of // groups) * stride
    selection = (jnp.arange(receivers, dtype=jnp.int32)[:, None] == station_of[None, :]).astype(jnp.bfloat16)
    stations = jnp.dot(
        spectra.reshape(rows, receivers), selection, preferred_element_type=jnp.float32
    ).astype(jnp.bfloat16).reshape(1, rows * shots)
    lanes = 128
    outgoing = jnp.concatenate(
        [
            near.reshape(groups, rows * receiver_dev // lanes, lanes).transpose(1, 0, 2),
            jnp.broadcast_to(stations.reshape(rows * shots // lanes, 1, lanes), (rows * shots // lanes, groups, lanes)),
        ],
        axis=0,
    )
    outgoing, aperture, lengths = lax.optimization_barrier((outgoing, aperture, lengths))
    incoming = lax.all_to_all(outgoing, "shot", 1, 1, tiled=True)
    used = jnp.arange(KMAX, dtype=jnp.int32)[None, None, :] < lengths[:, :, None]
    codes = jnp.where(used, (aperture % shot_dev) * groups + aperture // shot_dev, -1)
    codes = codes.reshape(groups, shot_dev, receiver_dev, KMAX).transpose(1, 2, 0, 3)
    counts = jnp.sum(
        (codes[..., None] == jnp.arange(shots, dtype=jnp.int32)).astype(jnp.float32), axis=3
    )
    kernel = functools.partial(
        multiply_kernel, local_bins=local_bins, shot_dev=shot_dev, receiver_dev=receiver_dev, groups=groups
    )
    back = pl.pallas_call(
        kernel,
        out_shape=jax.ShapeDtypeStruct((shot_dev * local_bins * 2, receivers), jnp.bfloat16),
        in_specs=[pl.BlockSpec(memory_space=pltpu.VMEM)] * 2,
        out_specs=pl.BlockSpec(memory_space=pltpu.VMEM),
        scratch_shapes=[
            pltpu.VMEM((rows * receiver_dev, groups), jnp.float32),
            pltpu.VMEM((groups, rows * receiver_dev), jnp.float32),
            pltpu.VMEM((groups, rows * receiver_dev), jnp.float32),
            pltpu.SemaphoreType.DMA((2,)),
        ],
        compiler_params=pltpu.CompilerParams(has_side_effects=True),
        cost_estimate=pl.CostEstimate(
            flops=16 * groups * shots * rows * receiver_dev // 2, transcendentals=0, bytes_accessed=4 * 1024 * 1024
        ),
    )(incoming, counts)
    piece = lax.all_gather(back, "freq", axis=0, tiled=False)
    piece = piece.reshape(freq_dev, shot_dev, local_bins * 2, receivers).transpose(1, 0, 2, 3)
    piece = piece.reshape(shot_dev, NF * 2, receivers)
    wide = time_dev + 2 * half_taps
    wide_times = start_time - half_taps + jnp.arange(wide, dtype=jnp.int32)
    inside = (wide_times >= 0) & (wide_times < NT)
    phases = frequency_bins[:, None] * jnp.clip(wide_times, 0, NT - 1)[None, :] % NT
    angles = phases.astype(jnp.float32) * (2.0 * math.pi / NT)
    wide_rows = jnp.stack([jnp.cos(angles), -jnp.sin(angles)], axis=1).astype(jnp.bfloat16)
    wide_rows = jnp.where(inside[None, None, :], wide_rows.astype(jnp.float32), 0.0).reshape(NF * 2, wide)
    taps = filters.astype(jnp.float32)
    shaped = sum(
        taps[:, tap, None, None] * wide_rows[None, :, 2 * half_taps - tap : 2 * half_taps - tap + time_dev]
        for tap in range(TAPS)
    )
    leading = shaped.astype(jnp.bfloat16)
    trailing = (shaped - leading.astype(jnp.float32)).astype(jnp.bfloat16)
    filtered = lax.dot_general(
        jnp.concatenate([piece, piece], axis=1),
        jnp.concatenate([leading, trailing], axis=1),
        (((1,), (1,)), ((0,), (0,))),
        preferred_element_type=jnp.float32,
    )
    return filtered.astype(jnp.bfloat16)


def solution(mesh):
    in_specs = (
        P("shot", None, "freq"),
        P(),
        P(None, "shot", None),
        P(None, "shot"),
        P("shot", None),
    )
    out_specs = P("shot", None, "freq")
    return jax.shard_map(shards, mesh=mesh, in_specs=in_specs, out_specs=out_specs, check_vma=False)
```

```python
import functools
import math

import jax
import jax.numpy as jnp
from jax import lax
from jax.experimental import pallas as pl
from jax.experimental.pallas import tpu as pltpu
from jax.sharding import PartitionSpec as P

NT = 1024
NF = 8
KMAX = 32
TAPS = 31


def extended(shard, sides, width):
    for axis, dim in sides:
        devices, length = (lax.axis_size(axis), shard.shape[dim])
        up = [(i, (i + 1) % devices) for i in range(devices - 1)]
        down = [(j, i) for i, j in up]
        last = lax.slice_in_dim(shard, length - width, length, axis=dim)
        leading = lax.slice_in_dim(shard, 0, width, axis=dim)
        before = lax.ppermute(last, axis, up)
        after = lax.ppermute(leading, axis, down)
        shard = jnp.concatenate([before, shard, after], axis=dim)
    return shard


def fourier_rows(bin_rows, first_time, sample_count, period):
    sample_times = first_time + jnp.arange(sample_count, dtype=jnp.int32)
    phases = bin_rows[:, None] * sample_times[None, :] % period
    angles = phases.astype(jnp.float32) * (2.0 * math.pi / period)
    return (jnp.cos(angles), jnp.sin(angles))


def multiply_kernel(
    incoming_ref, counts_ref, out_ref, qt_ref, acc_ref, recv_ref, both_ref, sems, pair_sems, *, local_bins, shot_dev, receiver_dev, groups
):
    qt_ref[...] = incoming_ref[0].astype(jnp.float32).T
    me = lax.axis_index("shot")
    half = lax.axis_index("freq")
    block = 8

    steps = groups // block

    def remote_send(target):
        pltpu.make_async_remote_copy(
            src_ref=acc_ref.at[pl.ds(target, 1)],
            dst_ref=recv_ref.at[pl.ds(me, 1)],
            send_sem=sems.at[0],
            recv_sem=sems.at[1],
            device_id=(target, half),
            device_id_type=pl.DeviceIdType.MESH,
        ).start()

    def compute(top):
        rows = pl.ds(top, block)
        for i in range(shot_dev):
            for r in range(receiver_dev):
                weights = [counts_ref[i, r, rows, h * groups : (h + 1) * groups] for h in range(shot_dev)]
                for f in range(local_bins):
                    real_sum = None
                    imag_sum = None
                    for h in range(shot_dev):
                        slab_r = 1 + ((f * 2 + 0) * shot_dev + i) * shot_dev + h
                        slab_i = 1 + ((f * 2 + 1) * shot_dev + i) * shot_dev + h
                        pr = incoming_ref[slab_r, rows, :].astype(jnp.float32)
                        pi = incoming_ref[slab_i, rows, :].astype(jnp.float32)
                        row_r = ((f * 2 + 0) * shot_dev + h) * receiver_dev + r
                        row_i = ((f * 2 + 1) * shot_dev + h) * receiver_dev + r
                        qr = qt_ref[row_r : row_r + 1, :]
                        qi = qt_ref[row_i : row_i + 1, :]
                        w = weights[h]
                        real_term = w * (pr * qr - pi * qi)
                        imag_term = w * (pr * qi + pi * qr)
                        real_sum = real_term if real_sum is None else real_sum + real_term
                        imag_sum = imag_term if imag_sum is None else imag_sum + imag_term
                    col_r = ((f * 2 + 0) * shot_dev + i) * receiver_dev + r
                    col_i = ((f * 2 + 1) * shot_dev + i) * receiver_dev + r
                    acc_ref[rows, col_r : col_r + 1] = jnp.sum(real_sum, axis=1, keepdims=True)
                    acc_ref[rows, col_i : col_i + 1] = jnp.sum(imag_sum, axis=1, keepdims=True)
        acc_ref[rows, :] = (acc_ref[rows, :] * KMAX ** (-0.5)).astype(jnp.bfloat16).astype(jnp.float32)

    own_block = me // block
    own_top = pl.multiple_of(own_block * block, block)
    compute(own_top)
    for t in range(block):
        target = own_top + lax.rem(me + t, block)

        @pl.when(target != me)
        def _():
            remote_send(target)

    recv_ref[pl.ds(me, 1), :] = acc_ref[pl.ds(me, 1), :]

    def chunk(step, carry):
        top = pl.multiple_of(lax.rem(own_block + step, steps) * block, block)
        compute(top)
        for t in range(block):
            remote_send(top + lax.rem(me + t, block))
        return carry

    lax.fori_loop(1, steps, chunk, 0)
    every = pltpu.make_async_remote_copy(
        src_ref=acc_ref.at[pl.ds(0, groups - 1)],
        dst_ref=recv_ref.at[pl.ds(0, groups - 1)],
        send_sem=sems.at[0],
        recv_sem=sems.at[1],
        device_id=(me, half),
        device_id_type=pl.DeviceIdType.MESH,
    )
    every.wait_send()
    every.wait_recv()
    qt_ref[...] = recv_ref[...].T
    width = groups * receiver_dev
    owners = lax.broadcasted_iota(jnp.int32, (groups, width), 0)
    places = lax.broadcasted_iota(jnp.int32, (groups, width), 1)
    rows_out = local_bins * 2
    for i in range(shot_dev):
        total = None
        for r in range(receiver_dev):
            spread = (places == owners * receiver_dev + r).astype(jnp.bfloat16)
            picked = qt_ref[pl.ds(i * receiver_dev + r, rows_out, stride=shot_dev * receiver_dev), :]
            term = jnp.dot(picked.astype(jnp.bfloat16), spread, preferred_element_type=jnp.float32)
            total = term if total is None else total + term
        both_ref[i, pl.ds(half * rows_out, rows_out), :] = total
    swap = pltpu.make_async_remote_copy(
        src_ref=both_ref.at[:, pl.ds(half * rows_out, rows_out), :],
        dst_ref=both_ref.at[:, pl.ds(half * rows_out, rows_out), :],
        send_sem=pair_sems.at[0],
        recv_sem=pair_sems.at[1],
        device_id=(me, 1 - half),
        device_id_type=pl.DeviceIdType.MESH,
    )
    swap.start()
    swap.wait_send()
    swap.wait_recv()
    out_ref[...] = both_ref[...].astype(out_ref.dtype)


def shards(traces, frequency_bins, aperture, lengths, filters):
    shot_dev, receivers, time_dev = traces.shape
    groups = lax.axis_size("shot")
    shots = shot_dev * groups
    receiver_dev = receivers // groups
    stride = receivers // shots
    freq_dev = lax.axis_size("freq")
    local_bins = NF // freq_dev
    start_time = lax.axis_index("freq") * time_dev
    half_taps = (TAPS - 1) // 2
    flat_traces = traces.reshape(shot_dev * receivers, time_dev)
    cosines, sines = fourier_rows(frequency_bins, start_time, time_dev, NT)
    basis_rows = (jnp.stack([cosines, -sines], axis=1) * NT ** (-0.5)).astype(jnp.bfloat16)
    basis_rows = basis_rows.reshape(NF * 2, time_dev)
    term = lax.dot_general(
        basis_rows, flat_traces, (((1,), (1,)), ((), ())), preferred_element_type=jnp.float32
    )
    term = term.reshape(NF, 2, shot_dev, receivers)
    core = lax.axis_index("freq")
    mine = lax.dynamic_slice_in_dim(term, core * local_bins, local_bins, axis=0)
    theirs = lax.dynamic_slice_in_dim(term, (1 - core) * local_bins, local_bins, axis=0)
    theirs = lax.ppermute(theirs, "freq", [(0, 1), (1, 0)])
    spectra = (mine + theirs).astype(jnp.bfloat16)
    rows = local_bins * 2 * shot_dev
    every = jnp.arange(receivers, dtype=jnp.int32)
    flat = spectra.reshape(rows, 1, receivers)
    spread = jnp.where(
        (every % receiver_dev)[None, None, :] == jnp.arange(receiver_dev, dtype=jnp.int32)[None, :, None], flat, 0
    ).reshape(rows * receiver_dev, receivers)
    owner = (every[None, :] // receiver_dev == jnp.arange(groups, dtype=jnp.int32)[:, None]).astype(jnp.bfloat16)
    near = lax.dot_general(
        owner, spread, (((1,), (1,)), ((), ())), preferred_element_type=jnp.float32
    ).astype(jnp.bfloat16)
    station_of = jnp.arange(shots, dtype=jnp.int32)
    station_of = (station_of % groups) * 2 * stride + (station_of // groups) * stride
    selection = (jnp.arange(receivers, dtype=jnp.int32)[:, None] == station_of[None, :]).astype(jnp.bfloat16)
    stations = jnp.dot(
        spectra.reshape(rows, receivers), selection, preferred_element_type=jnp.float32
    ).astype(jnp.bfloat16).reshape(1, rows * shots)
    lanes = 128
    outgoing = jnp.concatenate(
        [
            near.reshape(groups, rows * receiver_dev // lanes, lanes).transpose(1, 0, 2),
            jnp.broadcast_to(stations.reshape(rows * shots // lanes, 1, lanes), (rows * shots // lanes, groups, lanes)),
        ],
        axis=0,
    )
    outgoing, aperture, lengths = lax.optimization_barrier((outgoing, aperture, lengths))
    incoming = lax.all_to_all(outgoing, "shot", 1, 1, tiled=True)
    used = jnp.arange(KMAX, dtype=jnp.int32)[None, None, :] < lengths[:, :, None]
    codes = jnp.where(used, (aperture % shot_dev) * groups + aperture // shot_dev, -1)
    codes = codes.reshape(groups, shot_dev, receiver_dev, KMAX).transpose(1, 2, 0, 3)
    counts = jnp.sum(
        (codes[..., None] == jnp.arange(shots, dtype=jnp.int32)).astype(jnp.float32), axis=3
    )
    kernel = functools.partial(
        multiply_kernel, local_bins=local_bins, shot_dev=shot_dev, receiver_dev=receiver_dev, groups=groups
    )
    back = pl.pallas_call(
        kernel,
        out_shape=jax.ShapeDtypeStruct((shot_dev, NF * 2, receivers), jnp.bfloat16),
        in_specs=[pl.BlockSpec(memory_space=pltpu.VMEM)] * 2,
        out_specs=pl.BlockSpec(memory_space=pltpu.VMEM),
        scratch_shapes=[
            pltpu.VMEM((rows * receiver_dev, groups), jnp.float32),
            pltpu.VMEM((groups, rows * receiver_dev), jnp.float32),
            pltpu.VMEM((groups, rows * receiver_dev), jnp.float32),
            pltpu.VMEM((shot_dev, NF * 2, receivers), jnp.float32),
            pltpu.SemaphoreType.DMA((2,)),
            pltpu.SemaphoreType.DMA((2,)),
        ],
        compiler_params=pltpu.CompilerParams(has_side_effects=True),
        cost_estimate=pl.CostEstimate(
            flops=16 * groups * shots * rows * receiver_dev // 2, transcendentals=0, bytes_accessed=4 * 1024 * 1024
        ),
    )(incoming, counts)
    piece = back
    wide = time_dev + 2 * half_taps
    wide_times = start_time - half_taps + jnp.arange(wide, dtype=jnp.int32)
    inside = (wide_times >= 0) & (wide_times < NT)
    phases = frequency_bins[:, None] * jnp.clip(wide_times, 0, NT - 1)[None, :] % NT
    angles = phases.astype(jnp.float32) * (2.0 * math.pi / NT)
    wide_rows = jnp.stack([jnp.cos(angles), -jnp.sin(angles)], axis=1).astype(jnp.bfloat16)
    wide_rows = jnp.where(inside[None, None, :], wide_rows.astype(jnp.float32), 0.0).reshape(NF * 2, wide)
    taps = filters.astype(jnp.float32)
    shaped = sum(
        taps[:, tap, None, None] * wide_rows[None, :, 2 * half_taps - tap : 2 * half_taps - tap + time_dev]
        for tap in range(TAPS)
    )
    leading = shaped.astype(jnp.bfloat16)
    trailing = (shaped - leading.astype(jnp.float32)).astype(jnp.bfloat16)
    filtered = lax.dot_general(
        jnp.concatenate([piece, piece], axis=1),
        jnp.concatenate([leading, trailing], axis=1),
        (((1,), (1,)), ((0,), (0,))),
        preferred_element_type=jnp.float32,
    )
    return filtered.astype(jnp.bfloat16)


def solution(mesh):
    in_specs = (
        P("shot", None, "freq"),
        P(),
        P(None, "shot", None),
        P(None, "shot"),
        P("shot", None),
    )
    out_specs = P("shot", None, "freq")
    return jax.shard_map(shards, mesh=mesh, in_specs=in_specs, out_specs=out_specs, check_vma=False)
```

```python
import functools
import math

import jax
import jax.numpy as jnp
from jax import lax
from jax.experimental import pallas as pl
from jax.experimental.pallas import tpu as pltpu
from jax.sharding import PartitionSpec as P

NT = 1024
NF = 8
KMAX = 32
TAPS = 31


def extended(shard, sides, width):
    for axis, dim in sides:
        devices, length = (lax.axis_size(axis), shard.shape[dim])
        up = [(i, (i + 1) % devices) for i in range(devices - 1)]
        down = [(j, i) for i, j in up]
        last = lax.slice_in_dim(shard, length - width, length, axis=dim)
        leading = lax.slice_in_dim(shard, 0, width, axis=dim)
        before = lax.ppermute(last, axis, up)
        after = lax.ppermute(leading, axis, down)
        shard = jnp.concatenate([before, shard, after], axis=dim)
    return shard


def fourier_rows(bin_rows, first_time, sample_count, period):
    sample_times = first_time + jnp.arange(sample_count, dtype=jnp.int32)
    phases = bin_rows[:, None] * sample_times[None, :] % period
    angles = phases.astype(jnp.float32) * (2.0 * math.pi / period)
    return (jnp.cos(angles), jnp.sin(angles))


def multiply_kernel(
    incoming_ref, counts_ref, out_ref, qt_ref, acc_ref, recv_ref, both_ref, sems, pair_sems, *, local_bins, shot_dev, receiver_dev, groups
):
    qt_ref[...] = incoming_ref[0].astype(jnp.float32).T
    me = lax.axis_index("shot")
    half = lax.axis_index("freq")
    block = 8

    steps = groups // block

    def remote_send(target):
        pltpu.make_async_remote_copy(
            src_ref=acc_ref.at[pl.ds(target, 1)],
            dst_ref=recv_ref.at[pl.ds(me, 1)],
            send_sem=sems.at[0],
            recv_sem=sems.at[1],
            device_id=(target, half),
            device_id_type=pl.DeviceIdType.MESH,
        ).start()

    def compute(top):
        rows = pl.ds(top, block)
        for i in range(shot_dev):
            for r in range(receiver_dev):
                weights = [
                    counts_ref[i, r, rows, h * groups : (h + 1) * groups].astype(jnp.float32) for h in range(shot_dev)
                ]
                for f in range(local_bins):
                    real_sum = None
                    imag_sum = None
                    for h in range(shot_dev):
                        slab_r = 1 + ((f * 2 + 0) * shot_dev + i) * shot_dev + h
                        slab_i = 1 + ((f * 2 + 1) * shot_dev + i) * shot_dev + h
                        pr = incoming_ref[slab_r, rows, :].astype(jnp.float32)
                        pi = incoming_ref[slab_i, rows, :].astype(jnp.float32)
                        row_r = ((f * 2 + 0) * shot_dev + h) * receiver_dev + r
                        row_i = ((f * 2 + 1) * shot_dev + h) * receiver_dev + r
                        qr = qt_ref[row_r : row_r + 1, :]
                        qi = qt_ref[row_i : row_i + 1, :]
                        w = weights[h]
                        real_term = w * (pr * qr - pi * qi)
                        imag_term = w * (pr * qi + pi * qr)
                        real_sum = real_term if real_sum is None else real_sum + real_term
                        imag_sum = imag_term if imag_sum is None else imag_sum + imag_term
                    col_r = ((f * 2 + 0) * shot_dev + i) * receiver_dev + r
                    col_i = ((f * 2 + 1) * shot_dev + i) * receiver_dev + r
                    acc_ref[rows, col_r : col_r + 1] = jnp.sum(real_sum, axis=1, keepdims=True)
                    acc_ref[rows, col_i : col_i + 1] = jnp.sum(imag_sum, axis=1, keepdims=True)
        acc_ref[rows, :] = (acc_ref[rows, :] * KMAX ** (-0.5)).astype(jnp.bfloat16).astype(jnp.float32)

    own_block = me // block
    own_top = pl.multiple_of(own_block * block, block)
    compute(own_top)
    for t in range(block):
        target = own_top + lax.rem(me + t, block)

        @pl.when(target != me)
        def _():
            remote_send(target)

    recv_ref[pl.ds(me, 1), :] = acc_ref[pl.ds(me, 1), :]

    def chunk(step, carry):
        top = pl.multiple_of(lax.rem(own_block + step, steps) * block, block)
        compute(top)
        for t in range(block):
            remote_send(top + lax.rem(me + t, block))
        return carry

    lax.fori_loop(1, steps, chunk, 0)
    every = pltpu.make_async_remote_copy(
        src_ref=acc_ref.at[pl.ds(0, groups - 1)],
        dst_ref=recv_ref.at[pl.ds(0, groups - 1)],
        send_sem=sems.at[0],
        recv_sem=sems.at[1],
        device_id=(me, half),
        device_id_type=pl.DeviceIdType.MESH,
    )
    every.wait_send()
    every.wait_recv()
    qt_ref[...] = recv_ref[...].T
    width = groups * receiver_dev
    owners = lax.broadcasted_iota(jnp.int32, (groups, width), 0)
    places = lax.broadcasted_iota(jnp.int32, (groups, width), 1)
    rows_out = local_bins * 2
    for i in range(shot_dev):
        total = None
        for r in range(receiver_dev):
            spread = (places == owners * receiver_dev + r).astype(jnp.bfloat16)
            picked = qt_ref[pl.ds(i * receiver_dev + r, rows_out, stride=shot_dev * receiver_dev), :]
            term = jnp.dot(picked.astype(jnp.bfloat16), spread, preferred_element_type=jnp.float32)
            total = term if total is None else total + term
        both_ref[i, pl.ds(half * rows_out, rows_out), :] = total
    swap = pltpu.make_async_remote_copy(
        src_ref=both_ref.at[:, pl.ds(half * rows_out, rows_out), :],
        dst_ref=both_ref.at[:, pl.ds(half * rows_out, rows_out), :],
        send_sem=pair_sems.at[0],
        recv_sem=pair_sems.at[1],
        device_id=(me, 1 - half),
        device_id_type=pl.DeviceIdType.MESH,
    )
    swap.start()
    swap.wait_send()
    swap.wait_recv()
    out_ref[...] = both_ref[...].astype(out_ref.dtype)


def shards(traces, frequency_bins, aperture, lengths, filters):
    shot_dev, receivers, time_dev = traces.shape
    groups = lax.axis_size("shot")
    shots = shot_dev * groups
    receiver_dev = receivers // groups
    stride = receivers // shots
    freq_dev = lax.axis_size("freq")
    local_bins = NF // freq_dev
    start_time = lax.axis_index("freq") * time_dev
    half_taps = (TAPS - 1) // 2
    flat_traces = traces.reshape(shot_dev * receivers, time_dev)
    cosines, sines = fourier_rows(frequency_bins, start_time, time_dev, NT)
    basis_rows = (jnp.stack([cosines, -sines], axis=1) * NT ** (-0.5)).astype(jnp.bfloat16)
    basis_rows = basis_rows.reshape(NF * 2, time_dev)
    term = lax.dot_general(
        basis_rows, flat_traces, (((1,), (1,)), ((), ())), preferred_element_type=jnp.float32
    )
    term = term.reshape(NF, 2, shot_dev, receivers)
    core = lax.axis_index("freq")
    mine = lax.dynamic_slice_in_dim(term, core * local_bins, local_bins, axis=0)
    theirs = lax.dynamic_slice_in_dim(term, (1 - core) * local_bins, local_bins, axis=0)
    theirs = lax.ppermute(theirs, "freq", [(0, 1), (1, 0)])
    spectra = (mine + theirs).astype(jnp.bfloat16)
    rows = local_bins * 2 * shot_dev
    every = jnp.arange(receivers, dtype=jnp.int32)
    flat = spectra.reshape(rows, 1, receivers)
    spread = jnp.where(
        (every % receiver_dev)[None, None, :] == jnp.arange(receiver_dev, dtype=jnp.int32)[None, :, None], flat, 0
    ).reshape(rows * receiver_dev, receivers)
    owner = (every[None, :] // receiver_dev == jnp.arange(groups, dtype=jnp.int32)[:, None]).astype(jnp.bfloat16)
    near = lax.dot_general(
        owner, spread, (((1,), (1,)), ((), ())), preferred_element_type=jnp.float32
    ).astype(jnp.bfloat16)
    station_of = jnp.arange(shots, dtype=jnp.int32)
    station_of = (station_of % groups) * 2 * stride + (station_of // groups) * stride
    selection = (jnp.arange(receivers, dtype=jnp.int32)[:, None] == station_of[None, :]).astype(jnp.bfloat16)
    stations = jnp.dot(
        spectra.reshape(rows, receivers), selection, preferred_element_type=jnp.float32
    ).astype(jnp.bfloat16).reshape(1, rows * shots)
    lanes = 128
    outgoing = jnp.concatenate(
        [
            near.reshape(groups, rows * receiver_dev // lanes, lanes).transpose(1, 0, 2),
            jnp.broadcast_to(stations.reshape(rows * shots // lanes, 1, lanes), (rows * shots // lanes, groups, lanes)),
        ],
        axis=0,
    )
    outgoing, aperture, lengths = lax.optimization_barrier((outgoing, aperture, lengths))
    incoming = lax.all_to_all(outgoing, "shot", 1, 1, tiled=True)
    used = jnp.arange(KMAX, dtype=jnp.int32)[None, None, :] < lengths[:, :, None]
    codes = jnp.where(used, (aperture % shot_dev) * groups + aperture // shot_dev, -1)
    codes = codes.reshape(groups, shot_dev, receiver_dev, KMAX).transpose(1, 2, 0, 3)
    counts = jnp.sum(
        (codes[..., None] == jnp.arange(shots, dtype=jnp.int32)).astype(jnp.float32), axis=3
    ).astype(jnp.bfloat16)
    kernel = functools.partial(
        multiply_kernel, local_bins=local_bins, shot_dev=shot_dev, receiver_dev=receiver_dev, groups=groups
    )
    back = pl.pallas_call(
        kernel,
        out_shape=jax.ShapeDtypeStruct((shot_dev, NF * 2, receivers), jnp.bfloat16),
        in_specs=[pl.BlockSpec(memory_space=pltpu.VMEM)] * 2,
        out_specs=pl.BlockSpec(memory_space=pltpu.VMEM),
        scratch_shapes=[
            pltpu.VMEM((rows * receiver_dev, groups), jnp.float32),
            pltpu.VMEM((groups, rows * receiver_dev), jnp.float32),
            pltpu.VMEM((groups, rows * receiver_dev), jnp.float32),
            pltpu.VMEM((shot_dev, NF * 2, receivers), jnp.float32),
            pltpu.SemaphoreType.DMA((2,)),
            pltpu.SemaphoreType.DMA((2,)),
        ],
        compiler_params=pltpu.CompilerParams(has_side_effects=True),
        cost_estimate=pl.CostEstimate(
            flops=16 * groups * shots * rows * receiver_dev // 2, transcendentals=0, bytes_accessed=4 * 1024 * 1024
        ),
    )(incoming, counts)
    piece = back
    wide = time_dev + 2 * half_taps
    wide_times = start_time - half_taps + jnp.arange(wide, dtype=jnp.int32)
    inside = (wide_times >= 0) & (wide_times < NT)
    phases = frequency_bins[:, None] * jnp.clip(wide_times, 0, NT - 1)[None, :] % NT
    angles = phases.astype(jnp.float32) * (2.0 * math.pi / NT)
    wide_rows = jnp.stack([jnp.cos(angles), -jnp.sin(angles)], axis=1).astype(jnp.bfloat16)
    wide_rows = jnp.where(inside[None, None, :], wide_rows.astype(jnp.float32), 0.0).reshape(NF * 2, wide)
    taps = filters.astype(jnp.float32)
    shaped = sum(
        taps[:, tap, None, None] * wide_rows[None, :, 2 * half_taps - tap : 2 * half_taps - tap + time_dev]
        for tap in range(TAPS)
    )
    leading = shaped.astype(jnp.bfloat16)
    trailing = (shaped - leading.astype(jnp.float32)).astype(jnp.bfloat16)
    filtered = lax.dot_general(
        jnp.concatenate([piece, piece], axis=1),
        jnp.concatenate([leading, trailing], axis=1),
        (((1,), (1,)), ((0,), (0,))),
        preferred_element_type=jnp.float32,
    )
    return filtered.astype(jnp.bfloat16)


def solution(mesh):
    in_specs = (
        P("shot", None, "freq"),
        P(),
        P(None, "shot", None),
        P(None, "shot"),
        P("shot", None),
    )
    out_specs = P("shot", None, "freq")
    return jax.shard_map(shards, mesh=mesh, in_specs=in_specs, out_specs=out_specs, check_vma=False)
```
